128 devices in a mesh: expert: 8 (over y, z_lo), fsdp: 16 (over x, z_hi, core).
Axes of the slice: x: 4, y: 4, z: 4 (z_hi: 2, z_lo: 2; z = z_hi * 2 + z_lo), core: 2. Of those that a mesh axis runs over, the one named last changes fastest.
Arguments:
- tokens: bfloat16 [18432, 2048], P(('expert', 'fsdp')), may hold values from -6 to 6
- expert_ids: int32 [18432, 6], P(('expert', 'fsdp')), may hold values from 0 to 15, as said below
- combine: float32 [18432, 6], P(('expert', 'fsdp')), may hold values from 0.05 to 1
- gate_weight: bfloat16 [16, 1408, 2048], P('expert', 'fsdp'), may hold values from -0.125 to 0.125
- up_weight: bfloat16 [16, 1408, 2048], P('expert', 'fsdp'), may hold values from -0.125 to 0.125
- down_weight: bfloat16 [16, 1408, 2048], P('expert', 'fsdp'), may hold values from -0.15625 to 0.15625
Outputs:
- mixed: bfloat16 [18432, 2048], P(('expert', 'fsdp'))
The draws below stay inside these ranges and needn't reach their ends.
Inputs may be any that keep to these rules, and one draw needn't show every extreme that they name: `expert_ids`: each row names 6 different experts. Within the 144 rows of each device no expert is named more than 72 times, and one and the same expert is named exactly 72 times by the rows of every device.
All inputs are finite; a program needn't handle non-finite values.
Results may differ from the reference program's by a relative error of at most 0.0058.
Values may be sent and summed in bfloat16 or wider, within the bound.
A program may use at most 128 MiB of HBM per device.

```python
import math
import jax
import jax.numpy as jnp
from jax import lax

D = 2048
FF = 1408
EXPERTS = 16
TOP = 6
TOK_DEV = 144
CAP = 72
TOKENS = 18432


def draw_expert_ids(key, part):
    block_count = TOKENS // TOK_DEV
    hot_key, rest_key = jax.random.split(jax.random.fold_in(key, 17))
    hot_expert = jax.random.randint(hot_key, (), 0, EXPERTS)
    column = jnp.arange(TOP, dtype=jnp.int32)

    def one_block(block_key):
        first_key, second_key, third_key, fourth_key = jax.random.split(block_key, 4)
        token_rank = jax.random.permutation(first_key, TOK_DEV)
        is_hot = token_rank < CAP
        spread = jax.random.permutation(second_key, TOK_DEV)
        offset = spread * (EXPERTS - 1) // TOK_DEV
        shuffle = jax.random.permutation(third_key, EXPERTS - 1)
        rotation = jax.random.randint(fourth_key, (TOK_DEV,), 0, TOP)
        window_pos = jnp.where(is_hot[:, None], column[None, :] - 1, column[None, :])
        other_index = shuffle[(offset[:, None] + jnp.maximum(window_pos, 0)) % (EXPERTS - 1)]
        other_expert = (hot_expert + 1 + other_index) % EXPERTS
        row_ids = jnp.where(window_pos < 0, hot_expert, other_expert)
        rotated = (column[None, :] + rotation[:, None]) % TOP
        return jnp.take_along_axis(row_ids, rotated, axis=1)
    block_keys = jax.random.split(rest_key, block_count)
    return jax.vmap(one_block)(block_keys).reshape(TOKENS, TOP).astype(jnp.int32)


def levels(key, dims, pieces, least, largest):
    loudness, own = 1.0, jax.random.fold_in(key, 6)
    for dim, blocks in pieces:
        draws = jnp.exp(jax.random.uniform(jax.random.fold_in(own, dim), (blocks,), jnp.float32, least / len(pieces), largest / len(pieces)))
        loudness = loudness * jnp.repeat(draws, dims[dim] // blocks).reshape([-1 if axis == dim else 1 for axis in range(len(dims))])
    return loudness


def normal_values(rng, extent, deviation, bound, cuts=(), kind=jnp.bfloat16):
    gain = levels(rng, extent, cuts, -0.22, 0.18) if cuts else 1.0
    entries = jax.random.normal(rng, extent, jnp.float32) * deviation * gain
    return jnp.minimum(jnp.maximum(entries, -bound), bound).astype(kind)


def setup_inputs(seed: int = 0) -> dict:
    streams_of = jax.random.split(jax.random.key(seed), 7)
    tokens = normal_values(streams_of[0], (TOKENS, D), 1.0, 6.0, ((0, 128),))
    expert_ids = draw_expert_ids(jax.random.fold_in(streams_of[6], 71), 0)
    combine = jnp.clip(jnp.exp(math.log(1.0) - 2.9957323 * jax.random.uniform(streams_of[2], (TOKENS, TOP), jnp.float32) ** levels(streams_of[2], (TOKENS, TOP), ((0, 128),), -0.2, 0.2)), 0.05, 1.0)
    gate_weight = normal_values(streams_of[3], (EXPERTS, FF, D), D ** -0.5, 0.125, ((0, 8), (1, 16)))
    up_weight = normal_values(streams_of[4], (EXPERTS, FF, D), D ** -0.5, 0.125, ((0, 8), (1, 16)))
    down_weight = normal_values(streams_of[5], (EXPERTS, FF, D), FF ** -0.5, 0.15625, ((0, 8), (1, 16)))
    return {"tokens": tokens, "expert_ids": expert_ids, "combine": combine, "gate_weight": gate_weight, "up_weight": up_weight, "down_weight": down_weight}


def reference(tokens, expert_ids, combine, gate_weight, up_weight, down_weight):
    limit_rows = (TOKENS // TOK_DEV) * CAP

    def one_expert(running, expert_index):
        chosen = expert_ids == expert_index
        weight = jnp.sum(jnp.where(chosen, combine, jnp.zeros_like(combine)), axis=1)
        named = jnp.any(chosen, axis=1)
        picked = jnp.argsort(jnp.where(named, 0, 1).astype(jnp.int32), stable=True)[:limit_rows].astype(jnp.int32)
        chosen_rows = tokens[picked]
        gate_pre = jnp.dot(chosen_rows, gate_weight[expert_index].T, preferred_element_type=jnp.float32)
        up_pre = jnp.dot(chosen_rows, up_weight[expert_index].T, preferred_element_type=jnp.float32)
        hidden = (jax.nn.silu(gate_pre) * up_pre).astype(jnp.bfloat16)
        produced = jnp.dot(hidden, down_weight[expert_index], preferred_element_type=jnp.float32).astype(jnp.bfloat16)
        term = weight[picked][:, None] * produced.astype(jnp.float32)
        return running.at[picked].add(term), None

    running, unused = lax.scan(one_expert, jnp.zeros((TOKENS, D), jnp.float32), jnp.arange(EXPERTS, dtype=jnp.int32))
    return running.astype(jnp.bfloat16)
```

```python
import jax
import jax.numpy as jnp
from jax import lax
from jax.sharding import Mesh
from jax.sharding import PartitionSpec as P

CAP = 72


def gather_expert(piece, core):
    mine = lax.dynamic_index_in_dim(piece, core, 0, keepdims=False)
    other = lax.dynamic_index_in_dim(piece, 1 - core, 0, keepdims=False)
    got = lax.ppermute(other, "core", [(0, 1), (1, 0)])
    pair = jnp.stack([mine, got])
    return lax.all_gather(pair, "chip", axis=0, tiled=True).reshape(-1, piece.shape[-1])


def per_device(tokens, expert_ids, combine, gate_weight, up_weight, down_weight):
    core = lax.axis_index("core")
    per_group = gate_weight.shape[0]
    groups = lax.axis_size("expert")
    n_expert = per_group * groups
    tok_rows, top_k = expert_ids.shape
    model_width = tokens.shape[1]

    gate_full = gather_expert(gate_weight, core)
    up_full = gather_expert(up_weight, core)
    down_full = gather_expert(down_weight, core)

    flat_ids = expert_ids.reshape(-1)
    onehot = (flat_ids[:, None] == jnp.arange(n_expert, dtype=jnp.int32)[None, :]).astype(jnp.int32)
    earlier = jnp.cumsum(onehot, axis=0) - onehot
    rank_within = jnp.sum(earlier * onehot, axis=1)
    slot_index = flat_ids * CAP + rank_within
    source = jnp.arange(tok_rows * top_k, dtype=jnp.int32) // top_k
    outgoing = (
        jnp.zeros((n_expert * CAP, model_width), jnp.bfloat16).at[slot_index].set(tokens[source])
    )
    outgoing = outgoing.reshape(n_expert, CAP, model_width)
    arrived = lax.all_to_all(outgoing, ("expert", "core"), 0, 0, tiled=True)
    rows = arrived.reshape(n_expert * CAP, model_width)

    gate_pre = jnp.dot(rows, gate_full.T, preferred_element_type=jnp.float32)
    up_pre = jnp.dot(rows, up_full.T, preferred_element_type=jnp.float32)
    hidden = (jax.nn.silu(gate_pre) * up_pre).astype(jnp.bfloat16)
    produced = jnp.dot(hidden, down_full, preferred_element_type=jnp.float32).astype(jnp.bfloat16)
    produced = produced.reshape(n_expert, CAP, model_width)
    returned = lax.all_to_all(produced, ("expert", "core"), 0, 0, tiled=True)
    back_rows = returned.reshape(n_expert * CAP, model_width)[slot_index]
    weighted = back_rows.astype(jnp.float32).reshape(tok_rows, top_k, model_width) * combine[:, :, None]
    return jnp.sum(weighted, axis=1).astype(jnp.bfloat16)


def solution(mesh):
    groups = mesh.shape["expert"]
    chips = mesh.shape["fsdp"] // 2
    inner = Mesh(mesh.devices.reshape(groups, chips, 2), ("expert", "chip", "core"))
    rows = P(("expert", "chip", "core"), None)
    weights = P("expert", ("chip", "core"), None)
    return jax.shard_map(
        per_device,
        mesh=inner,
        in_specs=(rows, rows, rows, weights, weights, weights),
        out_specs=rows,
        check_vma=False,
    )
```

```python
import functools

import jax
import jax.numpy as jnp
from jax import lax
from jax.experimental import pallas as pl
from jax.experimental.pallas import tpu as pltpu
from jax.sharding import Mesh
from jax.sharding import PartitionSpec as P

CAP = 72
MESH_ID = pl.DeviceIdType.MESH


def weight_kernel(n_x, g_in, u_in, d_in, g_out, u_out, d_out, send_sem, recv_sem, local_sem):
    ins = (g_in, u_in, d_in)
    outs = (g_out, u_out, d_out)
    x = lax.axis_index("x")
    h = lax.axis_index("zhi")
    c = lax.axis_index("core")

    def block(xx, hh, cc):
        return (xx * 2 + hh) * 2 + cc

    me = block(x, h, c)
    x_peers = [lax.rem(x + s, n_x) for s in range(1, n_x)]
    partner = {"core": 1 - c}
    z_peer = {"zhi": 1 - h}
    x_devs = [{"x": xp} for xp in x_peers]

    barrier = pltpu.get_barrier_semaphore()
    for dev in [partner, z_peer] + x_devs:
        pl.semaphore_signal(barrier, inc=1, device_id=dev, device_id_type=MESH_ID)
    pl.semaphore_wait(barrier, 2 + len(x_devs))

    count = [0]

    def send(src_of, blk, dev):
        k = count[0]
        count[0] += 1
        copies = []
        for m in range(3):
            cp = pltpu.make_async_remote_copy(
                src_ref=src_of(m),
                dst_ref=outs[m].at[blk],
                send_sem=send_sem.at[m, k],
                recv_sem=recv_sem.at[m, blk],
                device_id=dev,
                device_id_type=MESH_ID,
            )
            cp.start()
            copies.append(cp)
        return copies

    def wait_in(blk):
        for m in range(3):
            pltpu.make_async_remote_copy(
                src_ref=ins[m].at[0],
                dst_ref=outs[m].at[blk],
                send_sem=send_sem.at[m, 0],
                recv_sem=recv_sem.at[m, blk],
                device_id=partner,
                device_id_type=MESH_ID,
            ).wait_recv()

    sent = []
    local = []
    for m in range(3):
        cp = pltpu.make_async_copy(ins[m].at[h], outs[m].at[me], local_sem.at[m])
        cp.start()
        local.append(cp)
    sent += send(lambda m: ins[m].at[1 - h], me, z_peer)
    for dev in [partner] + x_devs:
        sent += send(lambda m: ins[m].at[h], me, dev)

    z_blk = block(x, 1 - h, c)
    wait_in(z_blk)
    for dev in [partner] + x_devs:
        sent += send(lambda m: outs[m].at[z_blk], z_blk, dev)

    for xp in x_peers:
        for hh in (h, 1 - h):
            blk = block(xp, hh, c)
            wait_in(blk)
            sent += send(lambda m: outs[m].at[blk], blk, partner)

    for xx in range(n_x):
        for hh in (0, 1):
            wait_in(block(xx, hh, 1 - c))

    for cp in sent:
        cp.wait_send()
    for cp in local:
        cp.wait()


def gather_weights(gate_weight, up_weight, down_weight, n_x):
    blk_rows, width = gate_weight.shape[1], gate_weight.shape[2]
    n_blocks = n_x * 4
    n_send = 1 + 2 * n_x + 2 * (n_x - 1)
    shape = jax.ShapeDtypeStruct((n_blocks, blk_rows, width), gate_weight.dtype)
    any_spec = pl.BlockSpec(memory_space=pl.ANY)
    nbytes = 3 * n_blocks * blk_rows * width * 2
    return pl.pallas_call(
        functools.partial(weight_kernel, n_x),
        out_shape=(shape, shape, shape),
        in_specs=[any_spec] * 3,
        out_specs=(any_spec, any_spec, any_spec),
        scratch_shapes=[
            pltpu.SemaphoreType.DMA((3, n_send)),
            pltpu.SemaphoreType.DMA((3, n_blocks)),
            pltpu.SemaphoreType.DMA((3,)),
        ],
        compiler_params=pltpu.CompilerParams(collective_id=0, has_side_effects=True),
        cost_estimate=pl.CostEstimate(flops=0, transcendentals=0, bytes_accessed=nbytes),
    )(gate_weight, up_weight, down_weight)


def per_device(tokens, expert_ids, combine, gate_weight, up_weight, down_weight):
    n_x = lax.axis_size("x")
    per_group = gate_weight.shape[0]
    groups = lax.axis_size("expert")
    n_expert = per_group * groups
    tok_rows, top_k = expert_ids.shape
    model_width = tokens.shape[1]

    g_all, u_all, d_all = gather_weights(gate_weight, up_weight, down_weight, n_x)
    gate_full = g_all.reshape(-1, model_width)
    up_full = u_all.reshape(-1, model_width)
    down_full = d_all.reshape(-1, model_width)

    flat_ids = expert_ids.reshape(-1)
    onehot = (flat_ids[:, None] == jnp.arange(n_expert, dtype=jnp.int32)[None, :]).astype(jnp.int32)
    earlier = jnp.cumsum(onehot, axis=0) - onehot
    rank_within = jnp.sum(earlier * onehot, axis=1)
    slot_index = flat_ids * CAP + rank_within
    source = jnp.arange(tok_rows * top_k, dtype=jnp.int32) // top_k
    outgoing = (
        jnp.zeros((n_expert * CAP, model_width), jnp.bfloat16).at[slot_index].set(tokens[source])
    )
    outgoing = outgoing.reshape(n_expert, CAP, model_width)
    arrived = lax.all_to_all(outgoing, ("expert", "zhi"), 0, 0, tiled=True)
    rows = arrived.reshape(n_expert * CAP, model_width)

    gate_pre = jnp.dot(rows, gate_full.T, preferred_element_type=jnp.float32)
    up_pre = jnp.dot(rows, up_full.T, preferred_element_type=jnp.float32)
    hidden = (jax.nn.silu(gate_pre) * up_pre).astype(jnp.bfloat16)
    produced = jnp.dot(hidden, down_full, preferred_element_type=jnp.float32).astype(jnp.bfloat16)
    produced = produced.reshape(n_expert, CAP, model_width)
    returned = lax.all_to_all(produced, ("expert", "zhi"), 0, 0, tiled=True)
    back_rows = returned.reshape(n_expert * CAP, model_width)[slot_index]
    weighted = back_rows.astype(jnp.float32).reshape(tok_rows, top_k, model_width) * combine[:, :, None]
    return jnp.sum(weighted, axis=1).astype(jnp.bfloat16)


def solution(mesh):
    groups = mesh.shape["expert"]
    n_x = mesh.shape["fsdp"] // 4
    inner = Mesh(mesh.devices.reshape(groups, n_x, 2, 2), ("expert", "x", "zhi", "core"))
    rows = P(("expert", "x", "zhi", "core"), None)
    weights = P("expert", ("x", "zhi", "core"), None)
    return jax.shard_map(
        per_device,
        mesh=inner,
        in_specs=(rows, rows, rows, weights, weights, weights),
        out_specs=rows,
        check_vma=False,
    )
```

```python
import functools

import jax
import jax.numpy as jnp
from jax import lax
from jax.experimental import pallas as pl
from jax.experimental.pallas import tpu as pltpu
from jax.sharding import Mesh
from jax.sharding import PartitionSpec as P

CAP = 72
MESH_ID = pl.DeviceIdType.MESH


def exchange_peers(n_grp):
    me = lax.axis_index("expert") * 2 + lax.axis_index("zhi")
    peers = []
    for s in range(1, n_grp):
        p = lax.rem(me + s, n_grp)
        peers.append((p, {"expert": p // 2, "zhi": lax.rem(p, 2)}))
    return me, peers


def start_exchange(me, peers, x_ref, y_ref, send_sem, recv_sem, local_sem):
    copies = []
    local = pltpu.make_async_copy(x_ref.at[me], y_ref.at[me], local_sem)
    local.start()
    for k, (p, dev) in enumerate(peers):
        cp = pltpu.make_async_remote_copy(
            src_ref=x_ref.at[p],
            dst_ref=y_ref.at[me],
            send_sem=send_sem.at[k],
            recv_sem=recv_sem.at[me],
            device_id=dev,
            device_id_type=MESH_ID,
        )
        cp.start()
        copies.append(cp)
    return local, copies


def finish_exchange(peers, local, copies, x_ref, y_ref, send_sem, recv_sem):
    for k, (p, dev) in enumerate(peers):
        pltpu.make_async_remote_copy(
            src_ref=x_ref.at[0],
            dst_ref=y_ref.at[p],
            send_sem=send_sem.at[k],
            recv_sem=recv_sem.at[p],
            device_id=dev,
            device_id_type=MESH_ID,
        ).wait_recv()
    for cp in copies:
        cp.wait_send()
    local.wait()


def exchange_kernel(n_grp, x_ref, y_ref, send_sem, recv_sem, local_sem):
    me, peers = exchange_peers(n_grp)
    barrier = pltpu.get_barrier_semaphore()
    for p, dev in peers:
        pl.semaphore_signal(barrier, inc=1, device_id=dev, device_id_type=MESH_ID)
    pl.semaphore_wait(barrier, len(peers))
    local, copies = start_exchange(me, peers, x_ref, y_ref, send_sem, recv_sem, local_sem.at[0])
    finish_exchange(peers, local, copies, x_ref, y_ref, send_sem, recv_sem)


def exchange(x, n_grp, collective_id):
    any_spec = pl.BlockSpec(memory_space=pl.ANY)
    return pl.pallas_call(
        functools.partial(exchange_kernel, n_grp),
        out_shape=jax.ShapeDtypeStruct(x.shape, x.dtype),
        in_specs=[any_spec],
        out_specs=any_spec,
        scratch_shapes=[
            pltpu.SemaphoreType.DMA((n_grp,)),
            pltpu.SemaphoreType.DMA((n_grp,)),
            pltpu.SemaphoreType.DMA((1,)),
        ],
        compiler_params=pltpu.CompilerParams(collective_id=collective_id, has_side_effects=True),
        cost_estimate=pl.CostEstimate(flops=0, transcendentals=0, bytes_accessed=2 * x.size * 2),
    )(x)


def weight_kernel(n_x, n_grp, g_in, u_in, d_in, t_in, g_out, u_out, d_out, t_out, send_sem, recv_sem,
                  local_sem, t_send, t_recv):
    ins = (g_in, u_in, d_in)
    outs = (g_out, u_out, d_out)
    x = lax.axis_index("x")
    h = lax.axis_index("zhi")
    c = lax.axis_index("core")

    def block(xx, hh, cc):
        return (xx * 2 + hh) * 2 + cc

    me = block(x, h, c)
    x_peers = [lax.rem(x + s, n_x) for s in range(1, n_x)]
    partner = {"core": 1 - c}
    z_peer = {"zhi": 1 - h}
    x_devs = [{"x": xp} for xp in x_peers]

    t_me, t_peers = exchange_peers(n_grp)
    barrier = pltpu.get_barrier_semaphore()
    greet = [partner] + x_devs + [dev for p, dev in t_peers]
    for dev in greet:
        pl.semaphore_signal(barrier, inc=1, device_id=dev, device_id_type=MESH_ID)
    pl.semaphore_wait(barrier, len(greet))
    t_local, t_copies = start_exchange(t_me, t_peers, t_in, t_out, t_send, t_recv, local_sem.at[3])

    count = [0]

    def send(src_of, blk, dev):
        k = count[0]
        count[0] += 1
        copies = []
        for m in range(3):
            cp = pltpu.make_async_remote_copy(
                src_ref=src_of(m),
                dst_ref=outs[m].at[blk],
                send_sem=send_sem.at[m, k],
                recv_sem=recv_sem.at[m, blk],
                device_id=dev,
                device_id_type=MESH_ID,
            )
            cp.start()
            copies.append(cp)
        return copies

    def wait_in(blk):
        for m in range(3):
            pltpu.make_async_remote_copy(
                src_ref=ins[m].at[0],
                dst_ref=outs[m].at[blk],
                send_sem=send_sem.at[m, 0],
                recv_sem=recv_sem.at[m, blk],
                device_id=partner,
                device_id_type=MESH_ID,
            ).wait_recv()

    sent = []
    local = []
    for m in range(3):
        cp = pltpu.make_async_copy(ins[m].at[h], outs[m].at[me], local_sem.at[m])
        cp.start()
        local.append(cp)
    sent += send(lambda m: ins[m].at[1 - h], me, z_peer)
    for dev in [partner] + x_devs:
        sent += send(lambda m: ins[m].at[h], me, dev)

    z_blk = block(x, 1 - h, c)
    wait_in(z_blk)
    for dev in [partner] + x_devs:
        sent += send(lambda m: outs[m].at[z_blk], z_blk, dev)

    for xp in x_peers:
        for hh in (h, 1 - h):
            blk = block(xp, hh, c)
            wait_in(blk)
            sent += send(lambda m: outs[m].at[blk], blk, partner)

    for xx in range(n_x):
        for hh in (0, 1):
            wait_in(block(xx, hh, 1 - c))

    for cp in sent:
        cp.wait_send()
    for cp in local:
        cp.wait()
    finish_exchange(t_peers, t_local, t_copies, t_in, t_out, t_send, t_recv)


def gather_weights(gate_weight, up_weight, down_weight, outgoing, n_x, n_grp):
    blk_rows, width = gate_weight.shape[1], gate_weight.shape[2]
    n_blocks = n_x * 4
    n_send = 1 + 2 * n_x + 2 * (n_x - 1)
    shape = jax.ShapeDtypeStruct((n_blocks, blk_rows, width), gate_weight.dtype)
    any_spec = pl.BlockSpec(memory_space=pl.ANY)
    nbytes = 3 * n_blocks * blk_rows * width * 2
    return pl.pallas_call(
        functools.partial(weight_kernel, n_x, n_grp),
        out_shape=(shape, shape, shape, jax.ShapeDtypeStruct(outgoing.shape, outgoing.dtype)),
        in_specs=[any_spec] * 4,
        out_specs=(any_spec, any_spec, any_spec, any_spec),
        scratch_shapes=[
            pltpu.SemaphoreType.DMA((3, n_send)),
            pltpu.SemaphoreType.DMA((3, n_blocks)),
            pltpu.SemaphoreType.DMA((4,)),
            pltpu.SemaphoreType.DMA((n_grp,)),
            pltpu.SemaphoreType.DMA((n_grp,)),
        ],
        compiler_params=pltpu.CompilerParams(collective_id=0, has_side_effects=True),
        cost_estimate=pl.CostEstimate(flops=0, transcendentals=0, bytes_accessed=nbytes),
    )(gate_weight, up_weight, down_weight, outgoing)


def per_device(tokens, expert_ids, combine, gate_weight, up_weight, down_weight):
    n_x = lax.axis_size("x")
    per_group = gate_weight.shape[0]
    groups = lax.axis_size("expert")
    n_expert = per_group * groups
    n_grp = groups * 2
    tok_rows, top_k = expert_ids.shape
    model_width = tokens.shape[1]
    n_slot = n_expert * CAP

    flat_ids = expert_ids.reshape(-1)
    onehot = (flat_ids[:, None] == jnp.arange(n_expert, dtype=jnp.int32)[None, :]).astype(jnp.int32)
    earlier = jnp.cumsum(onehot, axis=0) - onehot
    rank_within = jnp.sum(earlier * onehot, axis=1)
    slot_index = (flat_ids * CAP + rank_within).reshape(tok_rows, top_k)
    hit = slot_index[None, :, :] == jnp.arange(n_slot, dtype=jnp.int32)[:, None, None]
    pick = jnp.any(hit, axis=2).astype(jnp.bfloat16)
    outgoing = jnp.dot(pick, tokens, preferred_element_type=jnp.float32).astype(jnp.bfloat16)
    outgoing = outgoing.reshape(n_expert, CAP, model_width)

    g_all, u_all, d_all, arrived = gather_weights(
        gate_weight, up_weight, down_weight, outgoing, n_x, n_grp
    )
    gate_full = g_all.reshape(-1, model_width)
    up_full = u_all.reshape(-1, model_width)
    down_full = d_all.reshape(-1, model_width)
    rows = arrived.reshape(n_slot, model_width)

    gate_pre = jnp.dot(rows, gate_full.T, preferred_element_type=jnp.float32)
    up_pre = jnp.dot(rows, up_full.T, preferred_element_type=jnp.float32)
    hidden = (jax.nn.silu(gate_pre) * up_pre).astype(jnp.bfloat16)
    produced = jnp.dot(hidden, down_full, preferred_element_type=jnp.float32).astype(jnp.bfloat16)
    produced = produced.reshape(n_expert, CAP, model_width)
    returned = exchange(produced, n_grp, 1).reshape(n_slot, model_width)

    weight_of = jnp.sum(
        jnp.where(hit, combine[None, :, :], jnp.zeros_like(combine)[None, :, :]), axis=2
    ).T
    weight_hi = weight_of.astype(jnp.bfloat16)
    weight_lo = (weight_of - weight_hi.astype(jnp.float32)).astype(jnp.bfloat16)
    mixed = jnp.dot(weight_hi, returned, preferred_element_type=jnp.float32) + jnp.dot(
        weight_lo, returned, preferred_element_type=jnp.float32
    )
    return mixed.astype(jnp.bfloat16)


def solution(mesh):
    groups = mesh.shape["expert"]
    n_x = mesh.shape["fsdp"] // 4
    inner = Mesh(mesh.devices.reshape(groups, n_x, 2, 2), ("expert", "x", "zhi", "core"))
    rows = P(("expert", "x", "zhi", "core"), None)
    weights = P("expert", ("x", "zhi", "core"), None)
    return jax.shard_map(
        per_device,
        mesh=inner,
        in_specs=(rows, rows, rows, weights, weights, weights),
        out_specs=rows,
        check_vma=False,
    )
```

```python
import functools

import jax
import jax.numpy as jnp
from jax import lax
from jax.experimental import pallas as pl
from jax.experimental.pallas import tpu as pltpu
from jax.sharding import Mesh
from jax.sharding import PartitionSpec as P

CAP = 72
MESH_ID = pl.DeviceIdType.MESH


def exchange_peers(n_grp):
    me = lax.axis_index("expert") * 2 + lax.axis_index("zhi")
    peers = []
    for s in range(1, n_grp):
        p = lax.rem(me + s, n_grp)
        peers.append((p, {"expert": p // 2, "zhi": lax.rem(p, 2)}))
    return me, peers


def start_exchange(me, peers, x_ref, y_ref, send_sem, recv_sem, local_sem):
    copies = []
    local = pltpu.make_async_copy(x_ref.at[me], y_ref.at[me], local_sem)
    local.start()
    for k, (p, dev) in enumerate(peers):
        cp = pltpu.make_async_remote_copy(
            src_ref=x_ref.at[p],
            dst_ref=y_ref.at[me],
            send_sem=send_sem.at[k],
            recv_sem=recv_sem.at[me],
            device_id=dev,
            device_id_type=MESH_ID,
        )
        cp.start()
        copies.append(cp)
    return local, copies


def finish_exchange(peers, local, copies, x_ref, y_ref, send_sem, recv_sem):
    for k, (p, dev) in enumerate(peers):
        pltpu.make_async_remote_copy(
            src_ref=x_ref.at[0],
            dst_ref=y_ref.at[p],
            send_sem=send_sem.at[k],
            recv_sem=recv_sem.at[p],
            device_id=dev,
            device_id_type=MESH_ID,
        ).wait_recv()
    for cp in copies:
        cp.wait_send()
    local.wait()


def exchange_kernel(n_grp, x_ref, y_ref, send_sem, recv_sem, local_sem):
    me, peers = exchange_peers(n_grp)
    barrier = pltpu.get_barrier_semaphore()
    for p, dev in peers:
        pl.semaphore_signal(barrier, inc=1, device_id=dev, device_id_type=MESH_ID)
    pl.semaphore_wait(barrier, len(peers))
    local, copies = start_exchange(me, peers, x_ref, y_ref, send_sem, recv_sem, local_sem.at[0])
    finish_exchange(peers, local, copies, x_ref, y_ref, send_sem, recv_sem)


def exchange(x, n_grp, collective_id):
    any_spec = pl.BlockSpec(memory_space=pl.ANY)
    return pl.pallas_call(
        functools.partial(exchange_kernel, n_grp),
        out_shape=jax.ShapeDtypeStruct(x.shape, x.dtype),
        in_specs=[any_spec],
        out_specs=any_spec,
        scratch_shapes=[
            pltpu.SemaphoreType.DMA((n_grp,)),
            pltpu.SemaphoreType.DMA((n_grp,)),
            pltpu.SemaphoreType.DMA((1,)),
        ],
        compiler_params=pltpu.CompilerParams(collective_id=collective_id, has_side_effects=True),
        cost_estimate=pl.CostEstimate(flops=0, transcendentals=0, bytes_accessed=2 * x.size * 2),
    )(x)


def weight_kernel(n_x, n_grp, g_in, u_in, d_in, t_in, g_out, u_out, d_out, t_out, send_sem, recv_sem,
                  local_sem, t_send, t_recv):
    ins = (g_in, u_in, d_in)
    outs = (g_out, u_out, d_out)
    x = lax.axis_index("x")
    h = lax.axis_index("zhi")
    c = lax.axis_index("core")

    def block(xx, hh, cc):
        return (xx * 2 + hh) * 2 + cc

    me = block(x, h, c)
    up_x = lax.rem(x + 1, n_x)
    down_x = lax.rem(x + n_x - 1, n_x)
    far_x = lax.rem(x + 2, n_x)
    toward = jnp.where(c == 0, up_x, down_x)
    away = jnp.where(c == 0, down_x, up_x)
    partner = {"core": 1 - c}
    z_peer = {"zhi": 1 - h}
    x_devs = [{"x": up_x}, {"x": down_x}]

    t_me, t_peers = exchange_peers(n_grp)
    barrier = pltpu.get_barrier_semaphore()
    greet = [partner] + x_devs + [dev for p, dev in t_peers]
    for dev in greet:
        pl.semaphore_signal(barrier, inc=1, device_id=dev, device_id_type=MESH_ID)
    pl.semaphore_wait(barrier, len(greet))
    t_local, t_copies = start_exchange(t_me, t_peers, t_in, t_out, t_send, t_recv, local_sem.at[3])

    count = [0]

    def send(src_of, blk, dev):
        k = count[0]
        count[0] += 1
        copies = []
        for m in range(3):
            cp = pltpu.make_async_remote_copy(
                src_ref=src_of(m),
                dst_ref=outs[m].at[blk],
                send_sem=send_sem.at[m, k],
                recv_sem=recv_sem.at[m, blk],
                device_id=dev,
                device_id_type=MESH_ID,
            )
            cp.start()
            copies.append(cp)
        return copies

    def wait_in(blk):
        for m in range(3):
            pltpu.make_async_remote_copy(
                src_ref=ins[m].at[0],
                dst_ref=outs[m].at[blk],
                send_sem=send_sem.at[m, 0],
                recv_sem=recv_sem.at[m, blk],
                device_id=partner,
                device_id_type=MESH_ID,
            ).wait_recv()

    sent = []
    local = []
    for m in range(3):
        cp = pltpu.make_async_copy(ins[m].at[h], outs[m].at[me], local_sem.at[m])
        cp.start()
        local.append(cp)
    sent += send(lambda m: ins[m].at[1 - h], me, z_peer)
    for dev in [partner] + x_devs:
        sent += send(lambda m: ins[m].at[h], me, dev)

    z_blk = block(x, 1 - h, c)
    wait_in(z_blk)
    for dev in [partner] + x_devs:
        sent += send(lambda m: outs[m].at[z_blk], z_blk, dev)

    for hh in (h, 1 - h):
        blk = block(away, hh, c)
        wait_in(blk)
        sent += send(lambda m: outs[m].at[blk], blk, partner)
        sent += send(lambda m: outs[m].at[blk], blk, {"x": toward})
    for xp in (toward, far_x):
        for hh in (h, 1 - h):
            blk = block(xp, hh, c)
            wait_in(blk)
            sent += send(lambda m: outs[m].at[blk], blk, partner)

    for xx in range(n_x):
        for hh in (0, 1):
            wait_in(block(xx, hh, 1 - c))

    for cp in sent:
        cp.wait_send()
    for cp in local:
        cp.wait()
    finish_exchange(t_peers, t_local, t_copies, t_in, t_out, t_send, t_recv)


def gather_weights(gate_weight, up_weight, down_weight, outgoing, n_x, n_grp):
    blk_rows, width = gate_weight.shape[1], gate_weight.shape[2]
    n_blocks = n_x * 4
    n_send = 16
    shape = jax.ShapeDtypeStruct((n_blocks, blk_rows, width), gate_weight.dtype)
    any_spec = pl.BlockSpec(memory_space=pl.ANY)
    nbytes = 3 * n_blocks * blk_rows * width * 2
    return pl.pallas_call(
        functools.partial(weight_kernel, n_x, n_grp),
        out_shape=(shape, shape, shape, jax.ShapeDtypeStruct(outgoing.shape, outgoing.dtype)),
        in_specs=[any_spec] * 4,
        out_specs=(any_spec, any_spec, any_spec, any_spec),
        scratch_shapes=[
            pltpu.SemaphoreType.DMA((3, n_send)),
            pltpu.SemaphoreType.DMA((3, n_blocks)),
            pltpu.SemaphoreType.DMA((4,)),
            pltpu.SemaphoreType.DMA((n_grp,)),
            pltpu.SemaphoreType.DMA((n_grp,)),
        ],
        compiler_params=pltpu.CompilerParams(collective_id=0, has_side_effects=True),
        cost_estimate=pl.CostEstimate(flops=0, transcendentals=0, bytes_accessed=nbytes),
    )(gate_weight, up_weight, down_weight, outgoing)


def per_device(tokens, expert_ids, combine, gate_weight, up_weight, down_weight):
    n_x = lax.axis_size("x")
    assert n_x == 4
    per_group = gate_weight.shape[0]
    groups = lax.axis_size("expert")
    n_expert = per_group * groups
    n_grp = groups * 2
    tok_rows, top_k = expert_ids.shape
    model_width = tokens.shape[1]
    n_slot = n_expert * CAP

    flat_ids = expert_ids.reshape(-1)
    onehot = (flat_ids[:, None] == jnp.arange(n_expert, dtype=jnp.int32)[None, :]).astype(jnp.int32)
    earlier = jnp.cumsum(onehot, axis=0) - onehot
    rank_within = jnp.sum(earlier * onehot, axis=1)
    slot_index = (flat_ids * CAP + rank_within).reshape(tok_rows, top_k)
    hit = slot_index[None, :, :] == jnp.arange(n_slot, dtype=jnp.int32)[:, None, None]
    pick = jnp.any(hit, axis=2).astype(jnp.bfloat16)
    outgoing = jnp.dot(pick, tokens, preferred_element_type=jnp.float32).astype(jnp.bfloat16)
    outgoing = outgoing.reshape(n_expert, CAP, model_width)

    g_all, u_all, d_all, arrived = gather_weights(
        gate_weight, up_weight, down_weight, outgoing, n_x, n_grp
    )
    gate_full = g_all.reshape(-1, model_width)
    up_full = u_all.reshape(-1, model_width)
    down_full = d_all.reshape(-1, model_width)
    rows = arrived.reshape(n_slot, model_width)

    gate_pre = jnp.dot(rows, gate_full.T, preferred_element_type=jnp.float32)
    up_pre = jnp.dot(rows, up_full.T, preferred_element_type=jnp.float32)
    hidden = (jax.nn.silu(gate_pre) * up_pre).astype(jnp.bfloat16)
    produced = jnp.dot(hidden, down_full, preferred_element_type=jnp.float32).astype(jnp.bfloat16)
    produced = produced.reshape(n_expert, CAP, model_width)
    returned = exchange(produced, n_grp, 1).reshape(n_slot, model_width)

    weight_of = jnp.sum(
        jnp.where(hit, combine[None, :, :], jnp.zeros_like(combine)[None, :, :]), axis=2
    ).T
    weight_top = lax.reduce_precision(weight_of, exponent_bits=8, mantissa_bits=7)
    weight_hi = weight_top.astype(jnp.bfloat16)
    weight_lo = (weight_of - weight_top).astype(jnp.bfloat16)
    mixed = jnp.dot(weight_hi, returned, preferred_element_type=jnp.float32) + jnp.dot(
        weight_lo, returned, preferred_element_type=jnp.float32
    )
    return mixed.astype(jnp.bfloat16)


def solution(mesh):
    groups = mesh.shape["expert"]
    n_x = mesh.shape["fsdp"] // 4
    inner = Mesh(mesh.devices.reshape(groups, n_x, 2, 2), ("expert", "x", "zhi", "core"))
    rows = P(("expert", "x", "zhi", "core"), None)
    weights = P("expert", ("x", "zhi", "core"), None)
    return jax.shard_map(
        per_device,
        mesh=inner,
        in_specs=(rows, rows, rows, weights, weights, weights),
        out_specs=rows,
        check_vma=False,
    )
```

```python
import functools

import jax
import jax.numpy as jnp
from jax import lax
from jax.experimental import pallas as pl
from jax.experimental.pallas import tpu as pltpu
from jax.sharding import Mesh
from jax.sharding import PartitionSpec as P

CAP = 72
MESH_ID = pl.DeviceIdType.MESH


def exchange_peers(n_grp):
    me = lax.axis_index("expert") * 2 + lax.axis_index("zhi")
    peers = []
    for s in range(1, n_grp):
        p = lax.rem(me + s, n_grp)
        peers.append((p, {"expert": p // 2, "zhi": lax.rem(p, 2)}))
    return me, peers


def start_exchange(me, peers, x_ref, y_ref, send_sem, recv_sem, local_sem):
    copies = []
    local = pltpu.make_async_copy(x_ref.at[me], y_ref.at[me], local_sem)
    local.start()
    for k, (p, dev) in enumerate(peers):
        cp = pltpu.make_async_remote_copy(
            src_ref=x_ref.at[p],
            dst_ref=y_ref.at[me],
            send_sem=send_sem.at[k],
            recv_sem=recv_sem.at[me],
            device_id=dev,
            device_id_type=MESH_ID,
        )
        cp.start()
        copies.append(cp)
    return local, copies


def finish_exchange(peers, local, copies, x_ref, y_ref, send_sem, recv_sem):
    for k, (p, dev) in enumerate(peers):
        pltpu.make_async_remote_copy(
            src_ref=x_ref.at[0],
            dst_ref=y_ref.at[p],
            send_sem=send_sem.at[k],
            recv_sem=recv_sem.at[p],
            device_id=dev,
            device_id_type=MESH_ID,
        ).wait_recv()
    for cp in copies:
        cp.wait_send()
    local.wait()


def exchange_kernel(n_grp, x_ref, y_ref, send_sem, recv_sem, local_sem):
    me, peers = exchange_peers(n_grp)
    barrier = pltpu.get_barrier_semaphore()
    for p, dev in peers:
        pl.semaphore_signal(barrier, inc=1, device_id=dev, device_id_type=MESH_ID)
    pl.semaphore_wait(barrier, len(peers))
    local, copies = start_exchange(me, peers, x_ref, y_ref, send_sem, recv_sem, local_sem.at[0])
    finish_exchange(peers, local, copies, x_ref, y_ref, send_sem, recv_sem)


def exchange(x, n_grp, collective_id):
    any_spec = pl.BlockSpec(memory_space=pl.ANY)
    return pl.pallas_call(
        functools.partial(exchange_kernel, n_grp),
        out_shape=jax.ShapeDtypeStruct(x.shape, x.dtype),
        in_specs=[any_spec],
        out_specs=any_spec,
        scratch_shapes=[
            pltpu.SemaphoreType.DMA((n_grp,)),
            pltpu.SemaphoreType.DMA((n_grp,)),
            pltpu.SemaphoreType.DMA((1,)),
        ],
        compiler_params=pltpu.CompilerParams(collective_id=collective_id, has_side_effects=True),
        cost_estimate=pl.CostEstimate(flops=0, transcendentals=0, bytes_accessed=2 * x.size * 2),
    )(x)


def weight_kernel(n_x, n_grp, g_in, u_in, d_in, t_in, g_out, u_out, d_out, t_out, send_sem, recv_sem,
                  local_sem, t_send, t_recv):
    ins = (g_in, u_in, d_in)
    outs = (g_out, u_out, d_out)
    x = lax.axis_index("x")
    h = lax.axis_index("zhi")
    c = lax.axis_index("core")

    def block(xx, hh, cc):
        return (xx * 2 + hh) * 2 + cc

    me = block(x, h, c)
    up_x = lax.rem(x + 1, n_x)
    down_x = lax.rem(x + n_x - 1, n_x)
    far_x = lax.rem(x + 2, n_x)
    toward = jnp.where(c == 0, up_x, down_x)
    away = jnp.where(c == 0, down_x, up_x)
    partner = {"core": 1 - c}
    z_peer = {"zhi": 1 - h}
    x_devs = [{"x": up_x}, {"x": down_x}]

    t_me, t_peers = exchange_peers(n_grp)
    barrier = pltpu.get_barrier_semaphore()
    greet = [partner] + x_devs + [dev for p, dev in t_peers]
    for dev in greet:
        pl.semaphore_signal(barrier, inc=1, device_id=dev, device_id_type=MESH_ID)
    pl.semaphore_wait(barrier, len(greet))

    count = [0]

    def send(src_of, blk, dev):
        k = count[0]
        count[0] += 1
        copies = []
        for m in range(3):
            cp = pltpu.make_async_remote_copy(
                src_ref=src_of(m),
                dst_ref=outs[m].at[blk],
                send_sem=send_sem.at[m, k],
                recv_sem=recv_sem.at[m, blk],
                device_id=dev,
                device_id_type=MESH_ID,
            )
            cp.start()
            copies.append(cp)
        return copies

    def wait_in(blk):
        for m in range(3):
            pltpu.make_async_remote_copy(
                src_ref=ins[m].at[0],
                dst_ref=outs[m].at[blk],
                send_sem=send_sem.at[m, 0],
                recv_sem=recv_sem.at[m, blk],
                device_id=partner,
                device_id_type=MESH_ID,
            ).wait_recv()

    sent = []
    local = []
    for m in range(3):
        cp = pltpu.make_async_copy(ins[m].at[h], outs[m].at[me], local_sem.at[m])
        cp.start()
        local.append(cp)
    sent += send(lambda m: ins[m].at[1 - h], me, z_peer)
    for dev in [partner] + x_devs:
        sent += send(lambda m: ins[m].at[h], me, dev)
    t_local, t_copies = start_exchange(t_me, t_peers, t_in, t_out, t_send, t_recv, local_sem.at[3])

    z_blk = block(x, 1 - h, c)
    wait_in(z_blk)
    for dev in [partner] + x_devs:
        sent += send(lambda m: outs[m].at[z_blk], z_blk, dev)

    for hh in (h, 1 - h):
        blk = block(away, hh, c)
        wait_in(blk)
        sent += send(lambda m: outs[m].at[blk], blk, partner)
        sent += send(lambda m: outs[m].at[blk], blk, {"x": toward})
    for xp in (toward, far_x):
        for hh in (h, 1 - h):
            blk = block(xp, hh, c)
            wait_in(blk)
            sent += send(lambda m: outs[m].at[blk], blk, partner)

    for xx in range(n_x):
        for hh in (0, 1):
            wait_in(block(xx, hh, 1 - c))

    for cp in sent:
        cp.wait_send()
    for cp in local:
        cp.wait()
    finish_exchange(t_peers, t_local, t_copies, t_in, t_out, t_send, t_recv)


def gather_weights(gate_weight, up_weight, down_weight, outgoing, n_x, n_grp):
    blk_rows, width = gate_weight.shape[1], gate_weight.shape[2]
    n_blocks = n_x * 4
    n_send = 16
    shape = jax.ShapeDtypeStruct((n_blocks, blk_rows, width), gate_weight.dtype)
    any_spec = pl.BlockSpec(memory_space=pl.ANY)
    nbytes = 3 * n_blocks * blk_rows * width * 2
    return pl.pallas_call(
        functools.partial(weight_kernel, n_x, n_grp),
        out_shape=(shape, shape, shape, jax.ShapeDtypeStruct(outgoing.shape, outgoing.dtype)),
        in_specs=[any_spec] * 4,
        out_specs=(any_spec, any_spec, any_spec, any_spec),
        scratch_shapes=[
            pltpu.SemaphoreType.DMA((3, n_send)),
            pltpu.SemaphoreType.DMA((3, n_blocks)),
            pltpu.SemaphoreType.DMA((4,)),
            pltpu.SemaphoreType.DMA((n_grp,)),
            pltpu.SemaphoreType.DMA((n_grp,)),
        ],
        compiler_params=pltpu.CompilerParams(collective_id=0, has_side_effects=True),
        cost_estimate=pl.CostEstimate(flops=0, transcendentals=0, bytes_accessed=nbytes),
    )(gate_weight, up_weight, down_weight, outgoing)


def per_device(tokens, expert_ids, combine, gate_weight, up_weight, down_weight):
    n_x = lax.axis_size("x")
    assert n_x == 4
    per_group = gate_weight.shape[0]
    groups = lax.axis_size("expert")
    n_expert = per_group * groups
    n_grp = groups * 2
    tok_rows, top_k = expert_ids.shape
    model_width = tokens.shape[1]
    n_slot = n_expert * CAP

    flat_ids = expert_ids.reshape(-1)
    onehot = (flat_ids[:, None] == jnp.arange(n_expert, dtype=jnp.int32)[None, :]).astype(jnp.int32)
    earlier = jnp.cumsum(onehot, axis=0) - onehot
    rank_within = jnp.sum(earlier * onehot, axis=1)
    slot_index = (flat_ids * CAP + rank_within).reshape(tok_rows, top_k)
    hit = slot_index[None, :, :] == jnp.arange(n_slot, dtype=jnp.int32)[:, None, None]
    pick = jnp.any(hit, axis=2).astype(jnp.bfloat16)
    outgoing = jnp.dot(pick, tokens, preferred_element_type=jnp.float32).astype(jnp.bfloat16)
    outgoing = outgoing.reshape(n_expert, CAP, model_width)

    g_all, u_all, d_all, arrived = gather_weights(
        gate_weight, up_weight, down_weight, outgoing, n_x, n_grp
    )
    gate_full = g_all.reshape(-1, model_width)
    up_full = u_all.reshape(-1, model_width)
    down_full = d_all.reshape(-1, model_width)
    rows = arrived.reshape(n_slot, model_width)

    gate_pre = jnp.dot(rows, gate_full.T, preferred_element_type=jnp.float32)
    up_pre = jnp.dot(rows, up_full.T, preferred_element_type=jnp.float32)
    hidden = (jax.nn.silu(gate_pre) * up_pre).astype(jnp.bfloat16)
    produced = jnp.dot(hidden, down_full, preferred_element_type=jnp.float32).astype(jnp.bfloat16)
    produced = produced.reshape(n_expert, CAP, model_width)
    returned = exchange(produced, n_grp, 1).reshape(n_slot, model_width)

    weight_of = jnp.sum(
        jnp.where(hit, combine[None, :, :], jnp.zeros_like(combine)[None, :, :]), axis=2
    ).T
    weight_top = lax.reduce_precision(weight_of, exponent_bits=8, mantissa_bits=7)
    weight_hi = weight_top.astype(jnp.bfloat16)
    weight_lo = (weight_of - weight_top).astype(jnp.bfloat16)
    mixed = jnp.dot(weight_hi, returned, preferred_element_type=jnp.float32) + jnp.dot(
        weight_lo, returned, preferred_element_type=jnp.float32
    )
    return mixed.astype(jnp.bfloat16)


def solution(mesh):
    groups = mesh.shape["expert"]
    n_x = mesh.shape["fsdp"] // 4
    inner = Mesh(mesh.devices.reshape(groups, n_x, 2, 2), ("expert", "x", "zhi", "core"))
    rows = P(("expert", "x", "zhi", "core"), None)
    weights = P("expert", ("x", "zhi", "core"), None)
    return jax.shard_map(
        per_device,
        mesh=inner,
        in_specs=(rows, rows, rows, weights, weights, weights),
        out_specs=rows,
        check_vma=False,
    )
```

```python
import functools

import jax
import jax.numpy as jnp
from jax import lax
from jax.experimental import pallas as pl
from jax.experimental.pallas import tpu as pltpu
from jax.sharding import Mesh
from jax.sharding import PartitionSpec as P

CAP = 72
MESH_ID = pl.DeviceIdType.MESH


def exchange_peers(n_grp):
    me = lax.axis_index("expert") * 2 + lax.axis_index("zhi")
    peers = []
    for s in range(1, n_grp):
        p = lax.rem(me + s, n_grp)
        peers.append((p, {"expert": p // 2, "zhi": lax.rem(p, 2)}))
    return me, peers


def start_exchange(me, peers, x_ref, y_ref, send_sem, recv_sem, local_sem):
    copies = []
    local = pltpu.make_async_copy(x_ref.at[me], y_ref.at[me], local_sem)
    local.start()
    for k, (p, dev) in enumerate(peers):
        cp = pltpu.make_async_remote_copy(
            src_ref=x_ref.at[p],
            dst_ref=y_ref.at[me],
            send_sem=send_sem.at[k],
            recv_sem=recv_sem.at[me],
            device_id=dev,
            device_id_type=MESH_ID,
        )
        cp.start()
        copies.append(cp)
    return local, copies


def finish_exchange(peers, local, copies, x_ref, y_ref, send_sem, recv_sem):
    for k, (p, dev) in enumerate(peers):
        pltpu.make_async_remote_copy(
            src_ref=x_ref.at[0],
            dst_ref=y_ref.at[p],
            send_sem=send_sem.at[k],
            recv_sem=recv_sem.at[p],
            device_id=dev,
            device_id_type=MESH_ID,
        ).wait_recv()
    for cp in copies:
        cp.wait_send()
    local.wait()


def exchange_kernel(n_grp, x_ref, y_ref, send_sem, recv_sem, local_sem):
    me, peers = exchange_peers(n_grp)
    barrier = pltpu.get_barrier_semaphore()
    for p, dev in peers:
        pl.semaphore_signal(barrier, inc=1, device_id=dev, device_id_type=MESH_ID)
    pl.semaphore_wait(barrier, len(peers))
    local, copies = start_exchange(me, peers, x_ref, y_ref, send_sem, recv_sem, local_sem.at[0])
    finish_exchange(peers, local, copies, x_ref, y_ref, send_sem, recv_sem)


def exchange(x, n_grp, collective_id):
    any_spec = pl.BlockSpec(memory_space=pl.ANY)
    return pl.pallas_call(
        functools.partial(exchange_kernel, n_grp),
        out_shape=jax.ShapeDtypeStruct(x.shape, x.dtype),
        in_specs=[any_spec],
        out_specs=any_spec,
        scratch_shapes=[
            pltpu.SemaphoreType.DMA((n_grp,)),
            pltpu.SemaphoreType.DMA((n_grp,)),
            pltpu.SemaphoreType.DMA((1,)),
        ],
        compiler_params=pltpu.CompilerParams(collective_id=collective_id, has_side_effects=True),
        cost_estimate=pl.CostEstimate(flops=0, transcendentals=0, bytes_accessed=2 * x.size * 2),
    )(x)


def down_return_kernel(n_grp, hid_ref, down_ref, y_ref, buf, send_sem, recv_sem, local_sem):
    me, peers = exchange_peers(n_grp)
    barrier = pltpu.get_barrier_semaphore()
    for p, dev in peers:
        pl.semaphore_signal(barrier, inc=1, device_id=dev, device_id_type=MESH_ID)

    def project(k):
        p = lax.rem(me + k, n_grp)
        buf[p] = jnp.dot(hid_ref[p], down_ref[...], preferred_element_type=jnp.float32).astype(
            buf.dtype
        )

    def remote(k):
        p = lax.rem(me + k, n_grp)
        return pltpu.make_async_remote_copy(
            src_ref=buf.at[p],
            dst_ref=y_ref.at[me],
            send_sem=send_sem.at[k],
            recv_sem=recv_sem.at[me],
            device_id={"expert": p // 2, "zhi": lax.rem(p, 2)},
            device_id_type=MESH_ID,
        )

    local = pltpu.make_async_copy(buf.at[me], y_ref.at[me], local_sem.at[0])
    project(0)
    pl.semaphore_wait(barrier, len(peers))

    def step(k, carry):
        project(k)

        @pl.when(k == 1)
        def _():
            local.start()

        @pl.when(k >= 2)
        def _():
            remote(k - 1).start()

        return carry

    lax.fori_loop(1, n_grp, step, 0)
    remote(n_grp - 1).start()

    local.wait()
    for k in range(1, n_grp):
        remote(k).wait_send()
    for p, dev in peers:
        pltpu.make_async_remote_copy(
            src_ref=buf.at[0],
            dst_ref=y_ref.at[p],
            send_sem=send_sem.at[0],
            recv_sem=recv_sem.at[p],
            device_id=dev,
            device_id_type=MESH_ID,
        ).wait_recv()


def down_return(hidden, down_full, n_grp, collective_id):
    n_src, rows, _ = hidden.shape
    width = down_full.shape[1]
    out = jax.ShapeDtypeStruct((n_src, rows, width), jnp.bfloat16)
    vmem = pl.BlockSpec(memory_space=pltpu.VMEM)
    flops = 2 * n_src * rows * hidden.shape[2] * width
    return pl.pallas_call(
        functools.partial(down_return_kernel, n_grp),
        out_shape=out,
        in_specs=[vmem, vmem],
        out_specs=pl.BlockSpec(memory_space=pl.ANY),
        scratch_shapes=[
            pltpu.VMEM((n_src, rows, width), jnp.bfloat16),
            pltpu.SemaphoreType.DMA((n_grp,)),
            pltpu.SemaphoreType.DMA((n_grp,)),
            pltpu.SemaphoreType.DMA((1,)),
        ],
        compiler_params=pltpu.CompilerParams(
            collective_id=collective_id, has_side_effects=True, vmem_limit_bytes=48 * 1024 * 1024
        ),
        cost_estimate=pl.CostEstimate(
            flops=flops, transcendentals=0, bytes_accessed=hidden.size * 2 + down_full.size * 2 + 2 * n_src * rows * width * 2
        ),
    )(hidden, down_full)


def weight_kernel(n_x, n_grp, g_in, u_in, d_in, t_in, g_out, u_out, d_out, t_out, send_sem, recv_sem,
                  local_sem, t_send, t_recv):
    ins = (g_in, u_in, d_in)
    outs = (g_out, u_out, d_out)
    x = lax.axis_index("x")
    h = lax.axis_index("zhi")
    c = lax.axis_index("core")

    def block(xx, hh, cc):
        return (xx * 2 + hh) * 2 + cc

    me = block(x, h, c)
    up_x = lax.rem(x + 1, n_x)
    down_x = lax.rem(x + n_x - 1, n_x)
    far_x = lax.rem(x + 2, n_x)
    toward = jnp.where(c == 0, up_x, down_x)
    away = jnp.where(c == 0, down_x, up_x)
    partner = {"core": 1 - c}
    z_peer = {"zhi": 1 - h}
    x_devs = [{"x": up_x}, {"x": down_x}]

    t_me, t_peers = exchange_peers(n_grp)
    barrier = pltpu.get_barrier_semaphore()
    greet = [partner] + x_devs + [dev for p, dev in t_peers]
    for dev in greet:
        pl.semaphore_signal(barrier, inc=1, device_id=dev, device_id_type=MESH_ID)
    pl.semaphore_wait(barrier, len(greet))

    count = [0]

    def send(src_of, blk, dev):
        k = count[0]
        count[0] += 1
        copies = []
        for m in range(3):
            cp = pltpu.make_async_remote_copy(
                src_ref=src_of(m),
                dst_ref=outs[m].at[blk],
                send_sem=send_sem.at[m, k],
                recv_sem=recv_sem.at[m, blk],
                device_id=dev,
                device_id_type=MESH_ID,
            )
            cp.start()
            copies.append(cp)
        return copies

    def wait_in(blk):
        for m in range(3):
            pltpu.make_async_remote_copy(
                src_ref=ins[m].at[0],
                dst_ref=outs[m].at[blk],
                send_sem=send_sem.at[m, 0],
                recv_sem=recv_sem.at[m, blk],
                device_id=partner,
                device_id_type=MESH_ID,
            ).wait_recv()

    sent = []
    local = []
    for m in range(3):
        cp = pltpu.make_async_copy(ins[m].at[h], outs[m].at[me], local_sem.at[m])
        cp.start()
        local.append(cp)
    sent += send(lambda m: ins[m].at[1 - h], me, z_peer)
    for dev in [partner] + x_devs:
        sent += send(lambda m: ins[m].at[h], me, dev)
    t_local, t_copies = start_exchange(t_me, t_peers, t_in, t_out, t_send, t_recv, local_sem.at[3])

    z_blk = block(x, 1 - h, c)
    wait_in(z_blk)
    for dev in [partner] + x_devs:
        sent += send(lambda m: outs[m].at[z_blk], z_blk, dev)

    for hh in (h, 1 - h):
        blk = block(away, hh, c)
        wait_in(blk)
        sent += send(lambda m: outs[m].at[blk], blk, partner)
        sent += send(lambda m: outs[m].at[blk], blk, {"x": toward})
    for xp in (toward, far_x):
        for hh in (h, 1 - h):
            blk = block(xp, hh, c)
            wait_in(blk)
            sent += send(lambda m: outs[m].at[blk], blk, partner)

    for xx in range(n_x):
        for hh in (0, 1):
            wait_in(block(xx, hh, 1 - c))

    for cp in sent:
        cp.wait_send()
    for cp in local:
        cp.wait()
    finish_exchange(t_peers, t_local, t_copies, t_in, t_out, t_send, t_recv)


def gather_weights(gate_weight, up_weight, down_weight, outgoing, n_x, n_grp):
    blk_rows, width = gate_weight.shape[1], gate_weight.shape[2]
    n_blocks = n_x * 4
    n_send = 16
    shape = jax.ShapeDtypeStruct((n_blocks, blk_rows, width), gate_weight.dtype)
    any_spec = pl.BlockSpec(memory_space=pl.ANY)
    nbytes = 3 * n_blocks * blk_rows * width * 2
    return pl.pallas_call(
        functools.partial(weight_kernel, n_x, n_grp),
        out_shape=(shape, shape, shape, jax.ShapeDtypeStruct(outgoing.shape, outgoing.dtype)),
        in_specs=[any_spec] * 4,
        out_specs=(any_spec, any_spec, any_spec, any_spec),
        scratch_shapes=[
            pltpu.SemaphoreType.DMA((3, n_send)),
            pltpu.SemaphoreType.DMA((3, n_blocks)),
            pltpu.SemaphoreType.DMA((4,)),
            pltpu.SemaphoreType.DMA((n_grp,)),
            pltpu.SemaphoreType.DMA((n_grp,)),
        ],
        compiler_params=pltpu.CompilerParams(collective_id=0, has_side_effects=True),
        cost_estimate=pl.CostEstimate(flops=0, transcendentals=0, bytes_accessed=nbytes),
    )(gate_weight, up_weight, down_weight, outgoing)


def per_device(tokens, expert_ids, combine, gate_weight, up_weight, down_weight):
    n_x = lax.axis_size("x")
    assert n_x == 4
    per_group = gate_weight.shape[0]
    groups = lax.axis_size("expert")
    n_expert = per_group * groups
    n_grp = groups * 2
    tok_rows, top_k = expert_ids.shape
    model_width = tokens.shape[1]
    n_slot = n_expert * CAP

    flat_ids = expert_ids.reshape(-1)
    onehot = (flat_ids[:, None] == jnp.arange(n_expert, dtype=jnp.int32)[None, :]).astype(jnp.int32)
    earlier = jnp.cumsum(onehot, axis=0) - onehot
    rank_within = jnp.sum(earlier * onehot, axis=1)
    slot_index = (flat_ids * CAP + rank_within).reshape(tok_rows, top_k)
    hit = slot_index[None, :, :] == jnp.arange(n_slot, dtype=jnp.int32)[:, None, None]
    pick = jnp.any(hit, axis=2).astype(jnp.bfloat16)
    outgoing = jnp.dot(pick, tokens, preferred_element_type=jnp.float32).astype(jnp.bfloat16)
    outgoing = outgoing.reshape(n_expert, CAP, model_width)

    g_all, u_all, d_all, arrived = gather_weights(
        gate_weight, up_weight, down_weight, outgoing, n_x, n_grp
    )
    gate_full = g_all.reshape(-1, model_width)
    up_full = u_all.reshape(-1, model_width)
    down_full = d_all.reshape(-1, model_width)
    rows = arrived.reshape(n_slot, model_width)

    gate_pre = jnp.dot(rows, gate_full.T, preferred_element_type=jnp.float32)
    up_pre = jnp.dot(rows, up_full.T, preferred_element_type=jnp.float32)
    hidden = (jax.nn.silu(gate_pre) * up_pre).astype(jnp.bfloat16)
    hidden = hidden.reshape(n_expert, CAP, hidden.shape[-1])
    returned = down_return(hidden, down_full, n_grp, 1).reshape(n_slot, model_width)

    weight_of = jnp.sum(
        jnp.where(hit, combine[None, :, :], jnp.zeros_like(combine)[None, :, :]), axis=2
    ).T
    weight_top = lax.reduce_precision(weight_of, exponent_bits=8, mantissa_bits=7)
    weight_hi = weight_top.astype(jnp.bfloat16)
    weight_lo = (weight_of - weight_top).astype(jnp.bfloat16)
    mixed = jnp.dot(weight_hi, returned, preferred_element_type=jnp.float32) + jnp.dot(
        weight_lo, returned, preferred_element_type=jnp.float32
    )
    return mixed.astype(jnp.bfloat16)


def solution(mesh):
    groups = mesh.shape["expert"]
    n_x = mesh.shape["fsdp"] // 4
    inner = Mesh(mesh.devices.reshape(groups, n_x, 2, 2), ("expert", "x", "zhi", "core"))
    rows = P(("expert", "x", "zhi", "core"), None)
    weights = P("expert", ("x", "zhi", "core"), None)
    return jax.shard_map(
        per_device,
        mesh=inner,
        in_specs=(rows, rows, rows, weights, weights, weights),
        out_specs=rows,
        check_vma=False,
    )
```

```python
import functools

import jax
import jax.numpy as jnp
from jax import lax
from jax.experimental import pallas as pl
from jax.experimental.pallas import tpu as pltpu
from jax.sharding import Mesh
from jax.sharding import PartitionSpec as P

CAP = 72
MESH_ID = pl.DeviceIdType.MESH


def exchange_peers(n_grp):
    me = lax.axis_index("expert") * 2 + lax.axis_index("zhi")
    peers = []
    for s in range(1, n_grp):
        p = lax.rem(me + s, n_grp)
        peers.append((p, {"expert": p // 2, "zhi": lax.rem(p, 2)}))
    return me, peers


def start_exchange(me, peers, x_ref, y_ref, send_sem, recv_sem, local_sem):
    copies = []
    local = pltpu.make_async_copy(x_ref.at[me], y_ref.at[me], local_sem)
    local.start()
    for k, (p, dev) in enumerate(peers):
        cp = pltpu.make_async_remote_copy(
            src_ref=x_ref.at[p],
            dst_ref=y_ref.at[me],
            send_sem=send_sem.at[k],
            recv_sem=recv_sem.at[me],
            device_id=dev,
            device_id_type=MESH_ID,
        )
        cp.start()
        copies.append(cp)
    return local, copies


def finish_exchange(peers, local, copies, x_ref, y_ref, send_sem, recv_sem):
    for k, (p, dev) in enumerate(peers):
        pltpu.make_async_remote_copy(
            src_ref=x_ref.at[0],
            dst_ref=y_ref.at[p],
            send_sem=send_sem.at[k],
            recv_sem=recv_sem.at[p],
            device_id=dev,
            device_id_type=MESH_ID,
        ).wait_recv()
    for cp in copies:
        cp.wait_send()
    local.wait()


def exchange_kernel(n_grp, x_ref, y_ref, send_sem, recv_sem, local_sem):
    me, peers = exchange_peers(n_grp)
    barrier = pltpu.get_barrier_semaphore()
    for p, dev in peers:
        pl.semaphore_signal(barrier, inc=1, device_id=dev, device_id_type=MESH_ID)
    pl.semaphore_wait(barrier, len(peers))
    local, copies = start_exchange(me, peers, x_ref, y_ref, send_sem, recv_sem, local_sem.at[0])
    finish_exchange(peers, local, copies, x_ref, y_ref, send_sem, recv_sem)


def exchange(x, n_grp, collective_id):
    any_spec = pl.BlockSpec(memory_space=pl.ANY)
    return pl.pallas_call(
        functools.partial(exchange_kernel, n_grp),
        out_shape=jax.ShapeDtypeStruct(x.shape, x.dtype),
        in_specs=[any_spec],
        out_specs=any_spec,
        scratch_shapes=[
            pltpu.SemaphoreType.DMA((n_grp,)),
            pltpu.SemaphoreType.DMA((n_grp,)),
            pltpu.SemaphoreType.DMA((1,)),
        ],
        compiler_params=pltpu.CompilerParams(collective_id=collective_id, has_side_effects=True),
        cost_estimate=pl.CostEstimate(flops=0, transcendentals=0, bytes_accessed=2 * x.size * 2),
    )(x)


def expert_return_kernel(n_grp, rows_ref, gate_ref, up_ref, down_ref, y_ref, buf, send_sem, recv_sem,
                         local_sem):
    me, peers = exchange_peers(n_grp)
    barrier = pltpu.get_barrier_semaphore()
    for p, dev in peers:
        pl.semaphore_signal(barrier, inc=1, device_id=dev, device_id_type=MESH_ID)

    def project(k):
        p = lax.rem(me + k, n_grp)
        r = rows_ref[p]
        nt = (((1,), (1,)), ((), ()))
        gate_pre = lax.dot_general(r, gate_ref[...], nt, preferred_element_type=jnp.float32)
        up_pre = lax.dot_general(r, up_ref[...], nt, preferred_element_type=jnp.float32)
        hidden = (jax.nn.silu(gate_pre) * up_pre).astype(jnp.bfloat16)
        buf[p] = jnp.dot(hidden, down_ref[...], preferred_element_type=jnp.float32).astype(buf.dtype)

    def remote(k):
        p = lax.rem(me + k, n_grp)
        return pltpu.make_async_remote_copy(
            src_ref=buf.at[p],
            dst_ref=y_ref.at[me],
            send_sem=send_sem.at[k],
            recv_sem=recv_sem.at[me],
            device_id={"expert": p // 2, "zhi": lax.rem(p, 2)},
            device_id_type=MESH_ID,
        )

    local = pltpu.make_async_copy(buf.at[me], y_ref.at[me], local_sem.at[0])
    project(0)
    pl.semaphore_wait(barrier, len(peers))

    def step(k, carry):
        project(k)

        @pl.when(k == 1)
        def _():
            local.start()

        @pl.when(k >= 2)
        def _():
            remote(k - 1).start()

        return carry

    lax.fori_loop(1, n_grp, step, 0)
    remote(n_grp - 1).start()

    local.wait()
    for k in range(1, n_grp):
        remote(k).wait_send()
    for p, dev in peers:
        pltpu.make_async_remote_copy(
            src_ref=buf.at[0],
            dst_ref=y_ref.at[p],
            send_sem=send_sem.at[0],
            recv_sem=recv_sem.at[p],
            device_id=dev,
            device_id_type=MESH_ID,
        ).wait_recv()


def expert_return(rows, gate_full, up_full, down_full, n_grp, collective_id):
    n_src, cap, width = rows.shape
    ff = gate_full.shape[0]
    out = jax.ShapeDtypeStruct((n_src, cap, width), jnp.bfloat16)
    vmem = pl.BlockSpec(memory_space=pltpu.VMEM)
    flops = 6 * n_src * cap * ff * width
    nbytes = rows.size * 2 + 3 * gate_full.size * 2 + 2 * n_src * cap * width * 2
    return pl.pallas_call(
        functools.partial(expert_return_kernel, n_grp),
        out_shape=out,
        in_specs=[vmem] * 4,
        out_specs=pl.BlockSpec(memory_space=pl.ANY),
        scratch_shapes=[
            pltpu.VMEM((n_src, cap, width), jnp.bfloat16),
            pltpu.SemaphoreType.DMA((n_grp,)),
            pltpu.SemaphoreType.DMA((n_grp,)),
            pltpu.SemaphoreType.DMA((1,)),
        ],
        compiler_params=pltpu.CompilerParams(
            collective_id=collective_id, has_side_effects=True, vmem_limit_bytes=56 * 1024 * 1024
        ),
        cost_estimate=pl.CostEstimate(flops=flops, transcendentals=n_src * cap * ff, bytes_accessed=nbytes),
    )(rows, gate_full, up_full, down_full)


def weight_kernel(n_x, n_grp, g_in, u_in, d_in, t_in, g_out, u_out, d_out, t_out, send_sem, recv_sem,
                  local_sem, t_send, t_recv):
    ins = (g_in, u_in, d_in)
    outs = (g_out, u_out, d_out)
    x = lax.axis_index("x")
    h = lax.axis_index("zhi")
    c = lax.axis_index("core")

    def block(xx, hh, cc):
        return (xx * 2 + hh) * 2 + cc

    me = block(x, h, c)
    up_x = lax.rem(x + 1, n_x)
    down_x = lax.rem(x + n_x - 1, n_x)
    far_x = lax.rem(x + 2, n_x)
    toward = jnp.where(c == 0, up_x, down_x)
    away = jnp.where(c == 0, down_x, up_x)
    partner = {"core": 1 - c}
    z_peer = {"zhi": 1 - h}
    x_devs = [{"x": up_x}, {"x": down_x}]

    t_me, t_peers = exchange_peers(n_grp)
    barrier = pltpu.get_barrier_semaphore()
    greet = [partner] + x_devs + [dev for p, dev in t_peers]
    for dev in greet:
        pl.semaphore_signal(barrier, inc=1, device_id=dev, device_id_type=MESH_ID)
    pl.semaphore_wait(barrier, len(greet))

    count = [0]

    def send(src_of, blk, dev):
        k = count[0]
        count[0] += 1
        copies = []
        for m in range(3):
            cp = pltpu.make_async_remote_copy(
                src_ref=src_of(m),
                dst_ref=outs[m].at[blk],
                send_sem=send_sem.at[m, k],
                recv_sem=recv_sem.at[m, blk],
                device_id=dev,
                device_id_type=MESH_ID,
            )
            cp.start()
            copies.append(cp)
        return copies

    def wait_in(blk):
        for m in range(3):
            pltpu.make_async_remote_copy(
                src_ref=ins[m].at[0],
                dst_ref=outs[m].at[blk],
                send_sem=send_sem.at[m, 0],
                recv_sem=recv_sem.at[m, blk],
                device_id=partner,
                device_id_type=MESH_ID,
            ).wait_recv()

    sent = []
    local = []
    for m in range(3):
        cp = pltpu.make_async_copy(ins[m].at[h], outs[m].at[me], local_sem.at[m])
        cp.start()
        local.append(cp)
    sent += send(lambda m: ins[m].at[1 - h], me, z_peer)
    for dev in [partner] + x_devs:
        sent += send(lambda m: ins[m].at[h], me, dev)
    t_local, t_copies = start_exchange(t_me, t_peers, t_in, t_out, t_send, t_recv, local_sem.at[3])

    z_blk = block(x, 1 - h, c)
    wait_in(z_blk)
    for dev in [partner] + x_devs:
        sent += send(lambda m: outs[m].at[z_blk], z_blk, dev)

    for hh in (h, 1 - h):
        blk = block(away, hh, c)
        wait_in(blk)
        sent += send(lambda m: outs[m].at[blk], blk, partner)
        sent += send(lambda m: outs[m].at[blk], blk, {"x": toward})
    for xp in (toward, far_x):
        for hh in (h, 1 - h):
            blk = block(xp, hh, c)
            wait_in(blk)
            sent += send(lambda m: outs[m].at[blk], blk, partner)

    for xx in range(n_x):
        for hh in (0, 1):
            wait_in(block(xx, hh, 1 - c))

    for cp in sent:
        cp.wait_send()
    for cp in local:
        cp.wait()
    finish_exchange(t_peers, t_local, t_copies, t_in, t_out, t_send, t_recv)


def gather_weights(gate_weight, up_weight, down_weight, outgoing, n_x, n_grp):
    blk_rows, width = gate_weight.shape[1], gate_weight.shape[2]
    n_blocks = n_x * 4
    n_send = 16
    shape = jax.ShapeDtypeStruct((n_blocks, blk_rows, width), gate_weight.dtype)
    any_spec = pl.BlockSpec(memory_space=pl.ANY)
    nbytes = 3 * n_blocks * blk_rows * width * 2
    return pl.pallas_call(
        functools.partial(weight_kernel, n_x, n_grp),
        out_shape=(shape, shape, shape, jax.ShapeDtypeStruct(outgoing.shape, outgoing.dtype)),
        in_specs=[any_spec] * 4,
        out_specs=(any_spec, any_spec, any_spec, any_spec),
        scratch_shapes=[
            pltpu.SemaphoreType.DMA((3, n_send)),
            pltpu.SemaphoreType.DMA((3, n_blocks)),
            pltpu.SemaphoreType.DMA((4,)),
            pltpu.SemaphoreType.DMA((n_grp,)),
            pltpu.SemaphoreType.DMA((n_grp,)),
        ],
        compiler_params=pltpu.CompilerParams(collective_id=0, has_side_effects=True),
        cost_estimate=pl.CostEstimate(flops=0, transcendentals=0, bytes_accessed=nbytes),
    )(gate_weight, up_weight, down_weight, outgoing)


def per_device(tokens, expert_ids, combine, gate_weight, up_weight, down_weight):
    n_x = lax.axis_size("x")
    assert n_x == 4
    per_group = gate_weight.shape[0]
    groups = lax.axis_size("expert")
    n_expert = per_group * groups
    n_grp = groups * 2
    tok_rows, top_k = expert_ids.shape
    model_width = tokens.shape[1]
    n_slot = n_expert * CAP

    flat_ids = expert_ids.reshape(-1)
    onehot = (flat_ids[:, None] == jnp.arange(n_expert, dtype=jnp.int32)[None, :]).astype(jnp.int32)
    earlier = jnp.cumsum(onehot, axis=0) - onehot
    rank_within = jnp.sum(earlier * onehot, axis=1)
    slot_index = (flat_ids * CAP + rank_within).reshape(tok_rows, top_k)
    hit = slot_index[None, :, :] == jnp.arange(n_slot, dtype=jnp.int32)[:, None, None]
    pick = jnp.any(hit, axis=2).astype(jnp.bfloat16)
    outgoing = jnp.dot(pick, tokens, preferred_element_type=jnp.float32).astype(jnp.bfloat16)
    outgoing = outgoing.reshape(n_expert, CAP, model_width)

    g_all, u_all, d_all, arrived = gather_weights(
        gate_weight, up_weight, down_weight, outgoing, n_x, n_grp
    )
    gate_full = g_all.reshape(-1, model_width)
    up_full = u_all.reshape(-1, model_width)
    down_full = d_all.reshape(-1, model_width)
    returned = expert_return(arrived, gate_full, up_full, down_full, n_grp, 1)
    returned = returned.reshape(n_slot, model_width)

    weight_of = jnp.sum(
        jnp.where(hit, combine[None, :, :], jnp.zeros_like(combine)[None, :, :]), axis=2
    ).T
    weight_top = lax.reduce_precision(weight_of, exponent_bits=8, mantissa_bits=7)
    weight_hi = weight_top.astype(jnp.bfloat16)
    weight_lo = (weight_of - weight_top).astype(jnp.bfloat16)
    mixed = jnp.dot(weight_hi, returned, preferred_element_type=jnp.float32) + jnp.dot(
        weight_lo, returned, preferred_element_type=jnp.float32
    )
    return mixed.astype(jnp.bfloat16)


def solution(mesh):
    groups = mesh.shape["expert"]
    n_x = mesh.shape["fsdp"] // 4
    inner = Mesh(mesh.devices.reshape(groups, n_x, 2, 2), ("expert", "x", "zhi", "core"))
    rows = P(("expert", "x", "zhi", "core"), None)
    weights = P("expert", ("x", "zhi", "core"), None)
    return jax.shard_map(
        per_device,
        mesh=inner,
        in_specs=(rows, rows, rows, weights, weights, weights),
        out_specs=rows,
        check_vma=False,
    )
```

```python
import functools

import jax
import jax.numpy as jnp
from jax import lax
from jax.experimental import pallas as pl
from jax.experimental.pallas import tpu as pltpu
from jax.sharding import Mesh
from jax.sharding import PartitionSpec as P

CAP = 72
MESH_ID = pl.DeviceIdType.MESH


def exchange_peers(n_grp):
    me = lax.axis_index("expert") * 2 + lax.axis_index("zhi")
    peers = []
    for s in range(1, n_grp):
        p = lax.rem(me + s, n_grp)
        peers.append((p, {"expert": p // 2, "zhi": lax.rem(p, 2)}))
    return me, peers


def start_exchange(me, peers, x_ref, y_ref, send_sem, recv_sem, local_sem):
    copies = []
    local = pltpu.make_async_copy(x_ref.at[me], y_ref.at[me], local_sem)
    local.start()
    for k, (p, dev) in enumerate(peers):
        cp = pltpu.make_async_remote_copy(
            src_ref=x_ref.at[p],
            dst_ref=y_ref.at[me],
            send_sem=send_sem.at[k],
            recv_sem=recv_sem.at[me],
            device_id=dev,
            device_id_type=MESH_ID,
        )
        cp.start()
        copies.append(cp)
    return local, copies


def finish_exchange(peers, local, copies, x_ref, y_ref, send_sem, recv_sem):
    for k, (p, dev) in enumerate(peers):
        pltpu.make_async_remote_copy(
            src_ref=x_ref.at[0],
            dst_ref=y_ref.at[p],
            send_sem=send_sem.at[k],
            recv_sem=recv_sem.at[p],
            device_id=dev,
            device_id_type=MESH_ID,
        ).wait_recv()
    for cp in copies:
        cp.wait_send()
    local.wait()


def plane_plan(n_grp):
    e_idx = lax.axis_index("expert")
    h = lax.axis_index("zhi")
    c = lax.axis_index("core")
    y = e_idx // 2
    z = h * 2 + lax.rem(e_idx, 2)
    s = 1 - 2 * c

    def at(dy, dz):
        yy = lax.rem(y + dy + 4, 4)
        zz = lax.rem(z + dz + 4, 4)
        p = (yy * 2 + lax.rem(zz, 2)) * 2 + zz // 2
        return p, {"expert": yy * 2 + lax.rem(zz, 2), "zhi": zz // 2}

    direct = [(dy, dz) for dy in (0, 1, 3) for dz in (0, 1, 3) if (dy, dz) != (0, 0)]
    relayed = [((2, dz), (s, 0)) for dz in (0, 1, 3)]
    relayed += [((dy, 2), (0, s)) for dy in (0, 1, 3)]
    relayed += [((2, 2), (s, s))]
    me = (y * 2 + lax.rem(z, 2)) * 2 + z // 2
    return me, at, direct, relayed


def start_plane(n_grp, x_ref, y_ref, stage, send_sem, recv_sem, stage_sem, local_sem):
    me, at, direct, relayed = plane_plan(n_grp)
    copies = []
    local = pltpu.make_async_copy(x_ref.at[me], y_ref.at[me], local_sem)
    local.start()
    k = 0
    for j, (off, rel) in enumerate(relayed):
        p, _ = at(*off)
        _, dev = at(*rel)
        cp = pltpu.make_async_remote_copy(
            src_ref=x_ref.at[p], dst_ref=stage.at[j], send_sem=send_sem.at[k],
            recv_sem=stage_sem.at[j], device_id=dev, device_id_type=MESH_ID,
        )
        cp.start()
        copies.append(cp)
        k += 1
    for off in direct:
        p, dev = at(*off)
        cp = pltpu.make_async_remote_copy(
            src_ref=x_ref.at[p], dst_ref=y_ref.at[me], send_sem=send_sem.at[k],
            recv_sem=recv_sem.at[me], device_id=dev, device_id_type=MESH_ID,
        )
        cp.start()
        copies.append(cp)
        k += 1
    return local, copies, k


def relay_plane(n_grp, k, x_ref, y_ref, stage, send_sem, recv_sem, stage_sem):
    me, at, direct, relayed = plane_plan(n_grp)
    copies = []
    for j, (off, rel) in enumerate(relayed):
        src_p, _ = at(-rel[0], -rel[1])
        _, dev = at(off[0] - rel[0], off[1] - rel[1])
        pltpu.make_async_remote_copy(
            src_ref=x_ref.at[0], dst_ref=stage.at[j], send_sem=send_sem.at[0],
            recv_sem=stage_sem.at[j], device_id=dev, device_id_type=MESH_ID,
        ).wait_recv()
        cp = pltpu.make_async_remote_copy(
            src_ref=stage.at[j], dst_ref=y_ref.at[src_p], send_sem=send_sem.at[k],
            recv_sem=recv_sem.at[src_p], device_id=dev, device_id_type=MESH_ID,
        )
        cp.start()
        copies.append(cp)
        k += 1
    return copies


def plane_devices(n_grp):
    me, at, direct, relayed = plane_plan(n_grp)
    return [at(*off)[1] for off in direct]


def exchange_kernel(n_grp, x_ref, y_ref, send_sem, recv_sem, local_sem):
    me, peers = exchange_peers(n_grp)
    barrier = pltpu.get_barrier_semaphore()
    for p, dev in peers:
        pl.semaphore_signal(barrier, inc=1, device_id=dev, device_id_type=MESH_ID)
    pl.semaphore_wait(barrier, len(peers))
    local, copies = start_exchange(me, peers, x_ref, y_ref, send_sem, recv_sem, local_sem.at[0])
    finish_exchange(peers, local, copies, x_ref, y_ref, send_sem, recv_sem)


def exchange(x, n_grp, collective_id):
    any_spec = pl.BlockSpec(memory_space=pl.ANY)
    return pl.pallas_call(
        functools.partial(exchange_kernel, n_grp),
        out_shape=jax.ShapeDtypeStruct(x.shape, x.dtype),
        in_specs=[any_spec],
        out_specs=any_spec,
        scratch_shapes=[
            pltpu.SemaphoreType.DMA((n_grp,)),
            pltpu.SemaphoreType.DMA((n_grp,)),
            pltpu.SemaphoreType.DMA((1,)),
        ],
        compiler_params=pltpu.CompilerParams(collective_id=collective_id, has_side_effects=True),
        cost_estimate=pl.CostEstimate(flops=0, transcendentals=0, bytes_accessed=2 * x.size * 2),
    )(x)


def expert_return_kernel(n_grp, rows_ref, gate_ref, up_ref, down_ref, y_ref, buf, send_sem, recv_sem,
                         local_sem):
    me, peers = exchange_peers(n_grp)
    barrier = pltpu.get_barrier_semaphore()
    for p, dev in peers:
        pl.semaphore_signal(barrier, inc=1, device_id=dev, device_id_type=MESH_ID)

    def project(k):
        p = lax.rem(me + k, n_grp)
        r = rows_ref[p]
        nt = (((1,), (1,)), ((), ()))
        gate_pre = lax.dot_general(r, gate_ref[...], nt, preferred_element_type=jnp.float32)
        up_pre = lax.dot_general(r, up_ref[...], nt, preferred_element_type=jnp.float32)
        hidden = (jax.nn.silu(gate_pre) * up_pre).astype(jnp.bfloat16)
        buf[p] = jnp.dot(hidden, down_ref[...], preferred_element_type=jnp.float32).astype(buf.dtype)

    def remote(k):
        p = lax.rem(me + k, n_grp)
        return pltpu.make_async_remote_copy(
            src_ref=buf.at[p],
            dst_ref=y_ref.at[me],
            send_sem=send_sem.at[k],
            recv_sem=recv_sem.at[me],
            device_id={"expert": p // 2, "zhi": lax.rem(p, 2)},
            device_id_type=MESH_ID,
        )

    local = pltpu.make_async_copy(buf.at[me], y_ref.at[me], local_sem.at[0])
    project(0)
    pl.semaphore_wait(barrier, len(peers))

    def step(k, carry):
        project(k)

        @pl.when(k == 1)
        def _():
            local.start()

        @pl.when(k >= 2)
        def _():
            remote(k - 1).start()

        return carry

    lax.fori_loop(1, n_grp, step, 0)
    remote(n_grp - 1).start()

    local.wait()
    for k in range(1, n_grp):
        remote(k).wait_send()
    for p, dev in peers:
        pltpu.make_async_remote_copy(
            src_ref=buf.at[0],
            dst_ref=y_ref.at[p],
            send_sem=send_sem.at[0],
            recv_sem=recv_sem.at[p],
            device_id=dev,
            device_id_type=MESH_ID,
        ).wait_recv()


def expert_return(rows, gate_full, up_full, down_full, n_grp, collective_id):
    n_src, cap, width = rows.shape
    ff = gate_full.shape[0]
    out = jax.ShapeDtypeStruct((n_src, cap, width), jnp.bfloat16)
    vmem = pl.BlockSpec(memory_space=pltpu.VMEM)
    flops = 6 * n_src * cap * ff * width
    nbytes = rows.size * 2 + 3 * gate_full.size * 2 + 2 * n_src * cap * width * 2
    return pl.pallas_call(
        functools.partial(expert_return_kernel, n_grp),
        out_shape=out,
        in_specs=[vmem] * 4,
        out_specs=pl.BlockSpec(memory_space=pl.ANY),
        scratch_shapes=[
            pltpu.VMEM((n_src, cap, width), jnp.bfloat16),
            pltpu.SemaphoreType.DMA((n_grp,)),
            pltpu.SemaphoreType.DMA((n_grp,)),
            pltpu.SemaphoreType.DMA((1,)),
        ],
        compiler_params=pltpu.CompilerParams(
            collective_id=collective_id, has_side_effects=True, vmem_limit_bytes=56 * 1024 * 1024
        ),
        cost_estimate=pl.CostEstimate(flops=flops, transcendentals=n_src * cap * ff, bytes_accessed=nbytes),
    )(rows, gate_full, up_full, down_full)


def weight_kernel(n_x, n_grp, g_in, u_in, d_in, t_in, g_out, u_out, d_out, t_out, send_sem, recv_sem,
                  local_sem, t_send, t_recv, stage, stage_sem):
    ins = (g_in, u_in, d_in)
    outs = (g_out, u_out, d_out)
    x = lax.axis_index("x")
    h = lax.axis_index("zhi")
    c = lax.axis_index("core")

    def block(xx, hh, cc):
        return (xx * 2 + hh) * 2 + cc

    me = block(x, h, c)
    up_x = lax.rem(x + 1, n_x)
    down_x = lax.rem(x + n_x - 1, n_x)
    far_x = lax.rem(x + 2, n_x)
    toward = jnp.where(c == 0, up_x, down_x)
    away = jnp.where(c == 0, down_x, up_x)
    partner = {"core": 1 - c}
    z_peer = {"zhi": 1 - h}
    x_devs = [{"x": up_x}, {"x": down_x}]

    t_me, t_peers = exchange_peers(n_grp)
    barrier = pltpu.get_barrier_semaphore()
    greet = [partner, z_peer] + x_devs + plane_devices(n_grp)
    for dev in greet:
        pl.semaphore_signal(barrier, inc=1, device_id=dev, device_id_type=MESH_ID)
    pl.semaphore_wait(barrier, len(greet))

    count = [0]

    def send(src_of, blk, dev):
        k = count[0]
        count[0] += 1
        copies = []
        for m in range(3):
            cp = pltpu.make_async_remote_copy(
                src_ref=src_of(m),
                dst_ref=outs[m].at[blk],
                send_sem=send_sem.at[m, k],
                recv_sem=recv_sem.at[m, blk],
                device_id=dev,
                device_id_type=MESH_ID,
            )
            cp.start()
            copies.append(cp)
        return copies

    def wait_in(blk):
        for m in range(3):
            pltpu.make_async_remote_copy(
                src_ref=ins[m].at[0],
                dst_ref=outs[m].at[blk],
                send_sem=send_sem.at[m, 0],
                recv_sem=recv_sem.at[m, blk],
                device_id=partner,
                device_id_type=MESH_ID,
            ).wait_recv()

    sent = []
    local = []
    for m in range(3):
        cp = pltpu.make_async_copy(ins[m].at[h], outs[m].at[me], local_sem.at[m])
        cp.start()
        local.append(cp)
    sent += send(lambda m: ins[m].at[1 - h], me, z_peer)
    for dev in [partner] + x_devs:
        sent += send(lambda m: ins[m].at[h], me, dev)
    t_local, t_copies, t_k = start_plane(
        n_grp, t_in, t_out, stage, t_send, t_recv, stage_sem, local_sem.at[3]
    )

    z_blk = block(x, 1 - h, c)
    wait_in(z_blk)
    for dev in [partner] + x_devs:
        sent += send(lambda m: outs[m].at[z_blk], z_blk, dev)
    t_copies += relay_plane(n_grp, t_k, t_in, t_out, stage, t_send, t_recv, stage_sem)

    for hh in (h, 1 - h):
        blk = block(away, hh, c)
        wait_in(blk)
        sent += send(lambda m: outs[m].at[blk], blk, partner)
        sent += send(lambda m: outs[m].at[blk], blk, {"x": toward})
    for xp in (toward, far_x):
        for hh in (h, 1 - h):
            blk = block(xp, hh, c)
            wait_in(blk)
            sent += send(lambda m: outs[m].at[blk], blk, partner)

    for xx in range(n_x):
        for hh in (0, 1):
            wait_in(block(xx, hh, 1 - c))

    for cp in sent:
        cp.wait_send()
    for cp in local:
        cp.wait()
    finish_exchange(t_peers, t_local, t_copies, t_in, t_out, t_send, t_recv)


def gather_weights(gate_weight, up_weight, down_weight, outgoing, n_x, n_grp):
    blk_rows, width = gate_weight.shape[1], gate_weight.shape[2]
    n_blocks = n_x * 4
    n_send = 16
    shape = jax.ShapeDtypeStruct((n_blocks, blk_rows, width), gate_weight.dtype)
    any_spec = pl.BlockSpec(memory_space=pl.ANY)
    nbytes = 3 * n_blocks * blk_rows * width * 2
    return pl.pallas_call(
        functools.partial(weight_kernel, n_x, n_grp),
        out_shape=(shape, shape, shape, jax.ShapeDtypeStruct(outgoing.shape, outgoing.dtype)),
        in_specs=[any_spec] * 4,
        out_specs=(any_spec, any_spec, any_spec, any_spec),
        scratch_shapes=[
            pltpu.SemaphoreType.DMA((3, n_send)),
            pltpu.SemaphoreType.DMA((3, n_blocks)),
            pltpu.SemaphoreType.DMA((4,)),
            pltpu.SemaphoreType.DMA((n_grp + 8,)),
            pltpu.SemaphoreType.DMA((n_grp,)),
            pltpu.VMEM((7,) + outgoing.shape[1:], outgoing.dtype),
            pltpu.SemaphoreType.DMA((7,)),
        ],
        compiler_params=pltpu.CompilerParams(collective_id=0, has_side_effects=True),
        cost_estimate=pl.CostEstimate(flops=0, transcendentals=0, bytes_accessed=nbytes),
    )(gate_weight, up_weight, down_weight, outgoing)


def per_device(tokens, expert_ids, combine, gate_weight, up_weight, down_weight):
    n_x = lax.axis_size("x")
    assert n_x == 4
    per_group = gate_weight.shape[0]
    groups = lax.axis_size("expert")
    n_expert = per_group * groups
    n_grp = groups * 2
    assert n_grp == 16
    tok_rows, top_k = expert_ids.shape
    model_width = tokens.shape[1]
    n_slot = n_expert * CAP

    flat_ids = expert_ids.reshape(-1)
    onehot = (flat_ids[:, None] == jnp.arange(n_expert, dtype=jnp.int32)[None, :]).astype(jnp.int32)
    earlier = jnp.cumsum(onehot, axis=0) - onehot
    rank_within = jnp.sum(earlier * onehot, axis=1)
    slot_index = (flat_ids * CAP + rank_within).reshape(tok_rows, top_k)
    hit = slot_index[None, :, :] == jnp.arange(n_slot, dtype=jnp.int32)[:, None, None]
    pick = jnp.any(hit, axis=2).astype(jnp.bfloat16)
    outgoing = jnp.dot(pick, tokens, preferred_element_type=jnp.float32).astype(jnp.bfloat16)
    outgoing = outgoing.reshape(n_expert, CAP, model_width)

    g_all, u_all, d_all, arrived = gather_weights(
        gate_weight, up_weight, down_weight, outgoing, n_x, n_grp
    )
    gate_full = g_all.reshape(-1, model_width)
    up_full = u_all.reshape(-1, model_width)
    down_full = d_all.reshape(-1, model_width)
    returned = expert_return(arrived, gate_full, up_full, down_full, n_grp, 1)
    returned = returned.reshape(n_slot, model_width)

    weight_of = jnp.sum(
        jnp.where(hit, combine[None, :, :], jnp.zeros_like(combine)[None, :, :]), axis=2
    ).T
    weight_top = lax.reduce_precision(weight_of, exponent_bits=8, mantissa_bits=7)
    weight_hi = weight_top.astype(jnp.bfloat16)
    weight_lo = (weight_of - weight_top).astype(jnp.bfloat16)
    mixed = jnp.dot(weight_hi, returned, preferred_element_type=jnp.float32) + jnp.dot(
        weight_lo, returned, preferred_element_type=jnp.float32
    )
    return mixed.astype(jnp.bfloat16)


def solution(mesh):
    groups = mesh.shape["expert"]
    n_x = mesh.shape["fsdp"] // 4
    inner = Mesh(mesh.devices.reshape(groups, n_x, 2, 2), ("expert", "x", "zhi", "core"))
    rows = P(("expert", "x", "zhi", "core"), None)
    weights = P("expert", ("x", "zhi", "core"), None)
    return jax.shard_map(
        per_device,
        mesh=inner,
        in_specs=(rows, rows, rows, weights, weights, weights),
        out_specs=rows,
        check_vma=False,
    )
```

```python
import functools

import jax
import jax.numpy as jnp
from jax import lax
from jax.experimental import pallas as pl
from jax.experimental.pallas import tpu as pltpu
from jax.sharding import Mesh
from jax.sharding import PartitionSpec as P

CAP = 72
MESH_ID = pl.DeviceIdType.MESH


def exchange_peers(n_grp):
    me = lax.axis_index("expert") * 2 + lax.axis_index("zhi")
    peers = []
    for s in range(1, n_grp):
        p = lax.rem(me + s, n_grp)
        peers.append((p, {"expert": p // 2, "zhi": lax.rem(p, 2)}))
    return me, peers


def start_exchange(me, peers, x_ref, y_ref, send_sem, recv_sem, local_sem):
    copies = []
    local = pltpu.make_async_copy(x_ref.at[me], y_ref.at[me], local_sem)
    local.start()
    for k, (p, dev) in enumerate(peers):
        cp = pltpu.make_async_remote_copy(
            src_ref=x_ref.at[p],
            dst_ref=y_ref.at[me],
            send_sem=send_sem.at[k],
            recv_sem=recv_sem.at[me],
            device_id=dev,
            device_id_type=MESH_ID,
        )
        cp.start()
        copies.append(cp)
    return local, copies


def finish_exchange(peers, local, copies, x_ref, y_ref, send_sem, recv_sem):
    for k, (p, dev) in enumerate(peers):
        pltpu.make_async_remote_copy(
            src_ref=x_ref.at[0],
            dst_ref=y_ref.at[p],
            send_sem=send_sem.at[k],
            recv_sem=recv_sem.at[p],
            device_id=dev,
            device_id_type=MESH_ID,
        ).wait_recv()
    for cp in copies:
        cp.wait_send()
    local.wait()


def plane_plan(n_grp):
    e_idx = lax.axis_index("expert")
    h = lax.axis_index("zhi")
    c = lax.axis_index("core")
    y = e_idx // 2
    z = h * 2 + lax.rem(e_idx, 2)
    s = 1 - 2 * c

    def at(dy, dz):
        yy = lax.rem(y + dy + 4, 4)
        zz = lax.rem(z + dz + 4, 4)
        p = (yy * 2 + lax.rem(zz, 2)) * 2 + zz // 2
        return p, {"expert": yy * 2 + lax.rem(zz, 2), "zhi": zz // 2}

    direct = [(dy, dz) for dy in (0, 1, 3) for dz in (0, 1, 3) if (dy, dz) != (0, 0)]
    relayed = [((2, dz), (s, 0)) for dz in (0, 1, 3)]
    relayed += [((dy, 2), (0, s)) for dy in (0, 1, 3)]
    relayed += [((2, 2), (s, s))]
    me = (y * 2 + lax.rem(z, 2)) * 2 + z // 2
    return me, at, direct, relayed


def start_plane(n_grp, x_ref, y_ref, stage, send_sem, recv_sem, stage_sem, local_sem):
    me, at, direct, relayed = plane_plan(n_grp)
    copies = []
    local = pltpu.make_async_copy(x_ref.at[me], y_ref.at[me], local_sem)
    local.start()
    k = 0
    for j, (off, rel) in enumerate(relayed):
        p, _ = at(*off)
        _, dev = at(*rel)
        cp = pltpu.make_async_remote_copy(
            src_ref=x_ref.at[p], dst_ref=stage.at[j], send_sem=send_sem.at[k],
            recv_sem=stage_sem.at[j], device_id=dev, device_id_type=MESH_ID,
        )
        cp.start()
        copies.append(cp)
        k += 1
    for off in direct:
        p, dev = at(*off)
        cp = pltpu.make_async_remote_copy(
            src_ref=x_ref.at[p], dst_ref=y_ref.at[me], send_sem=send_sem.at[k],
            recv_sem=recv_sem.at[me], device_id=dev, device_id_type=MESH_ID,
        )
        cp.start()
        copies.append(cp)
        k += 1
    return local, copies, k


def relay_plane(n_grp, k, x_ref, y_ref, stage, send_sem, recv_sem, stage_sem):
    me, at, direct, relayed = plane_plan(n_grp)
    copies = []
    for j, (off, rel) in enumerate(relayed):
        src_p, _ = at(-rel[0], -rel[1])
        _, dev = at(off[0] - rel[0], off[1] - rel[1])
        pltpu.make_async_remote_copy(
            src_ref=x_ref.at[0], dst_ref=stage.at[j], send_sem=send_sem.at[0],
            recv_sem=stage_sem.at[j], device_id=dev, device_id_type=MESH_ID,
        ).wait_recv()
        cp = pltpu.make_async_remote_copy(
            src_ref=stage.at[j], dst_ref=y_ref.at[src_p], send_sem=send_sem.at[k],
            recv_sem=recv_sem.at[src_p], device_id=dev, device_id_type=MESH_ID,
        )
        cp.start()
        copies.append(cp)
        k += 1
    return copies


def plane_devices(n_grp):
    me, at, direct, relayed = plane_plan(n_grp)
    return [at(*off)[1] for off in direct]


def exchange_kernel(n_grp, x_ref, y_ref, send_sem, recv_sem, local_sem):
    me, peers = exchange_peers(n_grp)
    barrier = pltpu.get_barrier_semaphore()
    for p, dev in peers:
        pl.semaphore_signal(barrier, inc=1, device_id=dev, device_id_type=MESH_ID)
    pl.semaphore_wait(barrier, len(peers))
    local, copies = start_exchange(me, peers, x_ref, y_ref, send_sem, recv_sem, local_sem.at[0])
    finish_exchange(peers, local, copies, x_ref, y_ref, send_sem, recv_sem)


def exchange(x, n_grp, collective_id):
    any_spec = pl.BlockSpec(memory_space=pl.ANY)
    return pl.pallas_call(
        functools.partial(exchange_kernel, n_grp),
        out_shape=jax.ShapeDtypeStruct(x.shape, x.dtype),
        in_specs=[any_spec],
        out_specs=any_spec,
        scratch_shapes=[
            pltpu.SemaphoreType.DMA((n_grp,)),
            pltpu.SemaphoreType.DMA((n_grp,)),
            pltpu.SemaphoreType.DMA((1,)),
        ],
        compiler_params=pltpu.CompilerParams(collective_id=collective_id, has_side_effects=True),
        cost_estimate=pl.CostEstimate(flops=0, transcendentals=0, bytes_accessed=2 * x.size * 2),
    )(x)


def expert_return_kernel(n_grp, rows_ref, gate_ref, up_ref, down_ref, y_ref, buf, stage, send_sem,
                         recv_sem, stage_sem, local_sem):
    me, at, direct, relayed = plane_plan(n_grp)
    n_rel = len(relayed)
    order = [off for off, rel in relayed] + direct + [(0, 0)]
    rel_of = [rel for off, rel in relayed]
    barrier = pltpu.get_barrier_semaphore()
    peers = plane_devices(n_grp)
    for dev in peers:
        pl.semaphore_signal(barrier, inc=1, device_id=dev, device_id_type=MESH_ID)

    def pick(k, values):
        out = values[-1]
        for i in range(len(values) - 2, -1, -1):
            out = jnp.where(k == i, values[i], out)
        return out

    def chunk_of(k):
        dy = pick(k, [o[0] for o in order])
        dz = pick(k, [o[1] for o in order])
        return at(dy, dz)

    def project(k):
        p, _ = chunk_of(k)
        r = rows_ref[p]
        nt = (((1,), (1,)), ((), ()))
        gate_pre = lax.dot_general(r, gate_ref[...], nt, preferred_element_type=jnp.float32)
        up_pre = lax.dot_general(r, up_ref[...], nt, preferred_element_type=jnp.float32)
        hidden = (jax.nn.silu(gate_pre) * up_pre).astype(jnp.bfloat16)
        buf[p] = jnp.dot(hidden, down_ref[...], preferred_element_type=jnp.float32).astype(buf.dtype)

    def first_hop(k):
        p, _ = chunk_of(k)
        ry = pick(k, [r[0] for r in rel_of])
        rz = pick(k, [r[1] for r in rel_of])
        _, dev = at(ry, rz)
        return pltpu.make_async_remote_copy(
            src_ref=buf.at[p], dst_ref=stage.at[k], send_sem=send_sem.at[k],
            recv_sem=stage_sem.at[k], device_id=dev, device_id_type=MESH_ID,
        )

    def direct_send(k):
        p, dev = chunk_of(k)
        return pltpu.make_async_remote_copy(
            src_ref=buf.at[p], dst_ref=y_ref.at[me], send_sem=send_sem.at[k],
            recv_sem=recv_sem.at[me], device_id=dev, device_id_type=MESH_ID,
        )

    def forwards():
        for j, (off, rel) in enumerate(relayed):
            src_p, _ = at(-rel[0], -rel[1])
            _, dev = at(off[0] - rel[0], off[1] - rel[1])
            pltpu.make_async_remote_copy(
                src_ref=buf.at[0], dst_ref=stage.at[j], send_sem=send_sem.at[0],
                recv_sem=stage_sem.at[j], device_id=dev, device_id_type=MESH_ID,
            ).wait_recv()
            pltpu.make_async_remote_copy(
                src_ref=stage.at[j], dst_ref=y_ref.at[src_p], send_sem=send_sem.at[n_grp - 1 + j],
                recv_sem=recv_sem.at[src_p], device_id=dev, device_id_type=MESH_ID,
            ).start()

    local = pltpu.make_async_copy(buf.at[me], y_ref.at[me], local_sem.at[0])
    project(0)
    pl.semaphore_wait(barrier, len(peers))

    def step(k, carry):
        project(k)

        @pl.when(k - 1 < n_rel)
        def _():
            first_hop(k - 1).start()

        @pl.when(k - 1 >= n_rel)
        def _():
            direct_send(k - 1).start()

        @pl.when(k == n_rel + 4)
        def _():
            forwards()

        return carry

    lax.fori_loop(1, n_grp, step, 0)
    local.start()

    local.wait()
    for k in range(n_grp - 1):
        if k < n_rel:
            first_hop(k).wait_send()
        else:
            direct_send(k).wait_send()
    for j, (off, rel) in enumerate(relayed):
        _, dev = at(off[0] - rel[0], off[1] - rel[1])
        pltpu.make_async_remote_copy(
            src_ref=stage.at[j], dst_ref=y_ref.at[0], send_sem=send_sem.at[n_grp - 1 + j],
            recv_sem=recv_sem.at[0], device_id=dev, device_id_type=MESH_ID,
        ).wait_send()
    for s in range(1, n_grp):
        q = lax.rem(me + s, n_grp)
        pltpu.make_async_remote_copy(
            src_ref=buf.at[0], dst_ref=y_ref.at[q], send_sem=send_sem.at[0],
            recv_sem=recv_sem.at[q], device_id=peers[0], device_id_type=MESH_ID,
        ).wait_recv()


def expert_return(rows, gate_full, up_full, down_full, n_grp, collective_id):
    n_src, cap, width = rows.shape
    ff = gate_full.shape[0]
    out = jax.ShapeDtypeStruct((n_src, cap, width), jnp.bfloat16)
    vmem = pl.BlockSpec(memory_space=pltpu.VMEM)
    flops = 6 * n_src * cap * ff * width
    nbytes = rows.size * 2 + 3 * gate_full.size * 2 + 2 * n_src * cap * width * 2
    return pl.pallas_call(
        functools.partial(expert_return_kernel, n_grp),
        out_shape=out,
        in_specs=[vmem] * 4,
        out_specs=pl.BlockSpec(memory_space=pl.ANY),
        scratch_shapes=[
            pltpu.VMEM((n_src, cap, width), jnp.bfloat16),
            pltpu.VMEM((7, cap, width), jnp.bfloat16),
            pltpu.SemaphoreType.DMA((n_grp + 8,)),
            pltpu.SemaphoreType.DMA((n_grp,)),
            pltpu.SemaphoreType.DMA((7,)),
            pltpu.SemaphoreType.DMA((1,)),
        ],
        compiler_params=pltpu.CompilerParams(
            collective_id=collective_id, has_side_effects=True, vmem_limit_bytes=56 * 1024 * 1024
        ),
        cost_estimate=pl.CostEstimate(flops=flops, transcendentals=n_src * cap * ff, bytes_accessed=nbytes),
    )(rows, gate_full, up_full, down_full)


def weight_kernel(n_x, n_grp, g_in, u_in, d_in, t_in, g_out, u_out, d_out, t_out, send_sem, recv_sem,
                  local_sem, t_send, t_recv, stage, stage_sem):
    ins = (g_in, u_in, d_in)
    outs = (g_out, u_out, d_out)
    x = lax.axis_index("x")
    h = lax.axis_index("zhi")
    c = lax.axis_index("core")

    def block(xx, hh, cc):
        return (xx * 2 + hh) * 2 + cc

    me = block(x, h, c)
    up_x = lax.rem(x + 1, n_x)
    down_x = lax.rem(x + n_x - 1, n_x)
    far_x = lax.rem(x + 2, n_x)
    toward = jnp.where(c == 0, up_x, down_x)
    away = jnp.where(c == 0, down_x, up_x)
    partner = {"core": 1 - c}
    z_peer = {"zhi": 1 - h}
    x_devs = [{"x": up_x}, {"x": down_x}]

    t_me, t_peers = exchange_peers(n_grp)
    barrier = pltpu.get_barrier_semaphore()
    greet = [partner, z_peer] + x_devs + plane_devices(n_grp)
    for dev in greet:
        pl.semaphore_signal(barrier, inc=1, device_id=dev, device_id_type=MESH_ID)
    pl.semaphore_wait(barrier, len(greet))

    count = [0]

    def send(src_of, blk, dev):
        k = count[0]
        count[0] += 1
        copies = []
        for m in range(3):
            cp = pltpu.make_async_remote_copy(
                src_ref=src_of(m),
                dst_ref=outs[m].at[blk],
                send_sem=send_sem.at[m, k],
                recv_sem=recv_sem.at[m, blk],
                device_id=dev,
                device_id_type=MESH_ID,
            )
            cp.start()
            copies.append(cp)
        return copies

    def wait_in(blk):
        for m in range(3):
            pltpu.make_async_remote_copy(
                src_ref=ins[m].at[0],
                dst_ref=outs[m].at[blk],
                send_sem=send_sem.at[m, 0],
                recv_sem=recv_sem.at[m, blk],
                device_id=partner,
                device_id_type=MESH_ID,
            ).wait_recv()

    sent = []
    local = []
    for m in range(3):
        cp = pltpu.make_async_copy(ins[m].at[h], outs[m].at[me], local_sem.at[m])
        cp.start()
        local.append(cp)
    sent += send(lambda m: ins[m].at[1 - h], me, z_peer)
    for dev in [partner] + x_devs:
        sent += send(lambda m: ins[m].at[h], me, dev)
    t_local, t_copies, t_k = start_plane(
        n_grp, t_in, t_out, stage, t_send, t_recv, stage_sem, local_sem.at[3]
    )

    z_blk = block(x, 1 - h, c)
    wait_in(z_blk)
    for dev in [partner] + x_devs:
        sent += send(lambda m: outs[m].at[z_blk], z_blk, dev)
    t_copies += relay_plane(n_grp, t_k, t_in, t_out, stage, t_send, t_recv, stage_sem)

    for hh in (h, 1 - h):
        blk = block(away, hh, c)
        wait_in(blk)
        sent += send(lambda m: outs[m].at[blk], blk, partner)
        sent += send(lambda m: outs[m].at[blk], blk, {"x": toward})
    for xp in (toward, far_x):
        for hh in (h, 1 - h):
            blk = block(xp, hh, c)
            wait_in(blk)
            sent += send(lambda m: outs[m].at[blk], blk, partner)

    for xx in range(n_x):
        for hh in (0, 1):
            wait_in(block(xx, hh, 1 - c))

    for cp in sent:
        cp.wait_send()
    for cp in local:
        cp.wait()
    finish_exchange(t_peers, t_local, t_copies, t_in, t_out, t_send, t_recv)


def gather_weights(gate_weight, up_weight, down_weight, outgoing, n_x, n_grp):
    blk_rows, width = gate_weight.shape[1], gate_weight.shape[2]
    n_blocks = n_x * 4
    n_send = 16
    shape = jax.ShapeDtypeStruct((n_blocks, blk_rows, width), gate_weight.dtype)
    any_spec = pl.BlockSpec(memory_space=pl.ANY)
    nbytes = 3 * n_blocks * blk_rows * width * 2
    return pl.pallas_call(
        functools.partial(weight_kernel, n_x, n_grp),
        out_shape=(shape, shape, shape, jax.ShapeDtypeStruct(outgoing.shape, outgoing.dtype)),
        in_specs=[any_spec] * 4,
        out_specs=(any_spec, any_spec, any_spec, any_spec),
        scratch_shapes=[
            pltpu.SemaphoreType.DMA((3, n_send)),
            pltpu.SemaphoreType.DMA((3, n_blocks)),
            pltpu.SemaphoreType.DMA((4,)),
            pltpu.SemaphoreType.DMA((n_grp + 8,)),
            pltpu.SemaphoreType.DMA((n_grp,)),
            pltpu.VMEM((7,) + outgoing.shape[1:], outgoing.dtype),
            pltpu.SemaphoreType.DMA((7,)),
        ],
        compiler_params=pltpu.CompilerParams(collective_id=0, has_side_effects=True),
        cost_estimate=pl.CostEstimate(flops=0, transcendentals=0, bytes_accessed=nbytes),
    )(gate_weight, up_weight, down_weight, outgoing)


def per_device(tokens, expert_ids, combine, gate_weight, up_weight, down_weight):
    n_x = lax.axis_size("x")
    assert n_x == 4
    per_group = gate_weight.shape[0]
    groups = lax.axis_size("expert")
    n_expert = per_group * groups
    n_grp = groups * 2
    assert n_grp == 16
    tok_rows, top_k = expert_ids.shape
    model_width = tokens.shape[1]
    n_slot = n_expert * CAP

    flat_ids = expert_ids.reshape(-1)
    onehot = (flat_ids[:, None] == jnp.arange(n_expert, dtype=jnp.int32)[None, :]).astype(jnp.int32)
    earlier = jnp.cumsum(onehot, axis=0) - onehot
    rank_within = jnp.sum(earlier * onehot, axis=1)
    slot_index = (flat_ids * CAP + rank_within).reshape(tok_rows, top_k)
    hit = slot_index[None, :, :] == jnp.arange(n_slot, dtype=jnp.int32)[:, None, None]
    pick = jnp.any(hit, axis=2).astype(jnp.bfloat16)
    outgoing = jnp.dot(pick, tokens, preferred_element_type=jnp.float32).astype(jnp.bfloat16)
    outgoing = outgoing.reshape(n_expert, CAP, model_width)

    g_all, u_all, d_all, arrived = gather_weights(
        gate_weight, up_weight, down_weight, outgoing, n_x, n_grp
    )
    gate_full = g_all.reshape(-1, model_width)
    up_full = u_all.reshape(-1, model_width)
    down_full = d_all.reshape(-1, model_width)
    returned = expert_return(arrived, gate_full, up_full, down_full, n_grp, 1)
    returned = returned.reshape(n_slot, model_width)

    weight_of = jnp.sum(
        jnp.where(hit, combine[None, :, :], jnp.zeros_like(combine)[None, :, :]), axis=2
    ).T
    weight_top = lax.reduce_precision(weight_of, exponent_bits=8, mantissa_bits=7)
    weight_hi = weight_top.astype(jnp.bfloat16)
    weight_lo = (weight_of - weight_top).astype(jnp.bfloat16)
    mixed = jnp.dot(weight_hi, returned, preferred_element_type=jnp.float32) + jnp.dot(
        weight_lo, returned, preferred_element_type=jnp.float32
    )
    return mixed.astype(jnp.bfloat16)


def solution(mesh):
    groups = mesh.shape["expert"]
    n_x = mesh.shape["fsdp"] // 4
    inner = Mesh(mesh.devices.reshape(groups, n_x, 2, 2), ("expert", "x", "zhi", "core"))
    rows = P(("expert", "x", "zhi", "core"), None)
    weights = P("expert", ("x", "zhi", "core"), None)
    return jax.shard_map(
        per_device,
        mesh=inner,
        in_specs=(rows, rows, rows, weights, weights, weights),
        out_specs=rows,
        check_vma=False,
    )
```

```python
import functools

import jax
import jax.numpy as jnp
from jax import lax
from jax.experimental import pallas as pl
from jax.experimental.pallas import tpu as pltpu
from jax.sharding import Mesh
from jax.sharding import PartitionSpec as P

CAP = 72
MESH_ID = pl.DeviceIdType.MESH


def exchange_peers(n_grp):
    me = lax.axis_index("expert") * 2 + lax.axis_index("zhi")
    peers = []
    for s in range(1, n_grp):
        p = lax.rem(me + s, n_grp)
        peers.append((p, {"expert": p // 2, "zhi": lax.rem(p, 2)}))
    return me, peers


def start_exchange(me, peers, x_ref, y_ref, send_sem, recv_sem, local_sem):
    copies = []
    local = pltpu.make_async_copy(x_ref.at[me], y_ref.at[me], local_sem)
    local.start()
    for k, (p, dev) in enumerate(peers):
        cp = pltpu.make_async_remote_copy(
            src_ref=x_ref.at[p],
            dst_ref=y_ref.at[me],
            send_sem=send_sem.at[k],
            recv_sem=recv_sem.at[me],
            device_id=dev,
            device_id_type=MESH_ID,
        )
        cp.start()
        copies.append(cp)
    return local, copies


def finish_exchange(peers, local, copies, x_ref, y_ref, send_sem, recv_sem):
    for k, (p, dev) in enumerate(peers):
        pltpu.make_async_remote_copy(
            src_ref=x_ref.at[0],
            dst_ref=y_ref.at[p],
            send_sem=send_sem.at[k],
            recv_sem=recv_sem.at[p],
            device_id=dev,
            device_id_type=MESH_ID,
        ).wait_recv()
    for cp in copies:
        cp.wait_send()
    local.wait()


def plane_plan(n_grp):
    e_idx = lax.axis_index("expert")
    h = lax.axis_index("zhi")
    c = lax.axis_index("core")
    y = e_idx // 2
    z = h * 2 + lax.rem(e_idx, 2)
    s = 1 - 2 * c

    def at(dy, dz):
        yy = lax.rem(y + dy + 4, 4)
        zz = lax.rem(z + dz + 4, 4)
        p = (yy * 2 + lax.rem(zz, 2)) * 2 + zz // 2
        return p, {"expert": yy * 2 + lax.rem(zz, 2), "zhi": zz // 2}

    direct = [(dy, dz) for dy in (0, 1, 3) for dz in (0, 1, 3) if (dy, dz) != (0, 0)]
    relayed = [((2, dz), (s, 0)) for dz in (0, 1, 3)]
    relayed += [((dy, 2), (0, s)) for dy in (0, 1, 3)]
    relayed += [((2, 2), (s, s))]
    me = (y * 2 + lax.rem(z, 2)) * 2 + z // 2
    return me, at, direct, relayed


def start_plane(n_grp, x_ref, y_ref, stage, send_sem, recv_sem, stage_sem, local_sem):
    me, at, direct, relayed = plane_plan(n_grp)
    copies = []
    local = pltpu.make_async_copy(x_ref.at[me], y_ref.at[me], local_sem)
    local.start()
    k = 0
    for j, (off, rel) in enumerate(relayed):
        p, _ = at(*off)
        _, dev = at(*rel)
        cp = pltpu.make_async_remote_copy(
            src_ref=x_ref.at[p], dst_ref=stage.at[j], send_sem=send_sem.at[k],
            recv_sem=stage_sem.at[j], device_id=dev, device_id_type=MESH_ID,
        )
        cp.start()
        copies.append(cp)
        k += 1
    for off in direct:
        p, dev = at(*off)
        cp = pltpu.make_async_remote_copy(
            src_ref=x_ref.at[p], dst_ref=y_ref.at[me], send_sem=send_sem.at[k],
            recv_sem=recv_sem.at[me], device_id=dev, device_id_type=MESH_ID,
        )
        cp.start()
        copies.append(cp)
        k += 1
    return local, copies, k


def relay_plane(n_grp, k, x_ref, y_ref, stage, send_sem, recv_sem, stage_sem):
    me, at, direct, relayed = plane_plan(n_grp)
    copies = []
    for j, (off, rel) in enumerate(relayed):
        src_p, _ = at(-rel[0], -rel[1])
        _, dev = at(off[0] - rel[0], off[1] - rel[1])
        pltpu.make_async_remote_copy(
            src_ref=x_ref.at[0], dst_ref=stage.at[j], send_sem=send_sem.at[0],
            recv_sem=stage_sem.at[j], device_id=dev, device_id_type=MESH_ID,
        ).wait_recv()
        cp = pltpu.make_async_remote_copy(
            src_ref=stage.at[j], dst_ref=y_ref.at[src_p], send_sem=send_sem.at[k],
            recv_sem=recv_sem.at[src_p], device_id=dev, device_id_type=MESH_ID,
        )
        cp.start()
        copies.append(cp)
        k += 1
    return copies


def plane_devices(n_grp):
    me, at, direct, relayed = plane_plan(n_grp)
    return [at(*off)[1] for off in direct]


def exchange_kernel(n_grp, x_ref, y_ref, send_sem, recv_sem, local_sem):
    me, peers = exchange_peers(n_grp)
    barrier = pltpu.get_barrier_semaphore()
    for p, dev in peers:
        pl.semaphore_signal(barrier, inc=1, device_id=dev, device_id_type=MESH_ID)
    pl.semaphore_wait(barrier, len(peers))
    local, copies = start_exchange(me, peers, x_ref, y_ref, send_sem, recv_sem, local_sem.at[0])
    finish_exchange(peers, local, copies, x_ref, y_ref, send_sem, recv_sem)


def exchange(x, n_grp, collective_id):
    any_spec = pl.BlockSpec(memory_space=pl.ANY)
    return pl.pallas_call(
        functools.partial(exchange_kernel, n_grp),
        out_shape=jax.ShapeDtypeStruct(x.shape, x.dtype),
        in_specs=[any_spec],
        out_specs=any_spec,
        scratch_shapes=[
            pltpu.SemaphoreType.DMA((n_grp,)),
            pltpu.SemaphoreType.DMA((n_grp,)),
            pltpu.SemaphoreType.DMA((1,)),
        ],
        compiler_params=pltpu.CompilerParams(collective_id=collective_id, has_side_effects=True),
        cost_estimate=pl.CostEstimate(flops=0, transcendentals=0, bytes_accessed=2 * x.size * 2),
    )(x)


def expert_return_kernel(n_grp, hid_ref, down_ref, y_ref, buf, stage, send_sem, recv_sem, stage_sem,
                         local_sem):
    me, at, direct, relayed = plane_plan(n_grp)
    n_rel = len(relayed)
    order = [off for off, rel in relayed] + direct + [(0, 0)]
    rel_of = [rel for off, rel in relayed]
    barrier = pltpu.get_barrier_semaphore()
    peers = plane_devices(n_grp)
    for dev in peers:
        pl.semaphore_signal(barrier, inc=1, device_id=dev, device_id_type=MESH_ID)

    def pick(k, values):
        out = values[-1]
        for i in range(len(values) - 2, -1, -1):
            out = jnp.where(k == i, values[i], out)
        return out

    def chunk_of(k):
        dy = pick(k, [o[0] for o in order])
        dz = pick(k, [o[1] for o in order])
        return at(dy, dz)

    def project(k):
        p, _ = chunk_of(k)
        buf[p] = jnp.dot(hid_ref[p], down_ref[...], preferred_element_type=jnp.float32).astype(buf.dtype)

    def first_hop(k):
        p, _ = chunk_of(k)
        ry = pick(k, [r[0] for r in rel_of])
        rz = pick(k, [r[1] for r in rel_of])
        _, dev = at(ry, rz)
        return pltpu.make_async_remote_copy(
            src_ref=buf.at[p], dst_ref=stage.at[k], send_sem=send_sem.at[k],
            recv_sem=stage_sem.at[k], device_id=dev, device_id_type=MESH_ID,
        )

    def direct_send(k):
        p, dev = chunk_of(k)
        return pltpu.make_async_remote_copy(
            src_ref=buf.at[p], dst_ref=y_ref.at[me], send_sem=send_sem.at[k],
            recv_sem=recv_sem.at[me], device_id=dev, device_id_type=MESH_ID,
        )

    def forwards():
        for j, (off, rel) in enumerate(relayed):
            src_p, _ = at(-rel[0], -rel[1])
            _, dev = at(off[0] - rel[0], off[1] - rel[1])
            pltpu.make_async_remote_copy(
                src_ref=buf.at[0], dst_ref=stage.at[j], send_sem=send_sem.at[0],
                recv_sem=stage_sem.at[j], device_id=dev, device_id_type=MESH_ID,
            ).wait_recv()
            pltpu.make_async_remote_copy(
                src_ref=stage.at[j], dst_ref=y_ref.at[src_p], send_sem=send_sem.at[n_grp - 1 + j],
                recv_sem=recv_sem.at[src_p], device_id=dev, device_id_type=MESH_ID,
            ).start()

    local = pltpu.make_async_copy(buf.at[me], y_ref.at[me], local_sem.at[0])
    project(0)
    pl.semaphore_wait(barrier, len(peers))

    def step(k, carry):
        project(k)

        @pl.when(k - 1 < n_rel)
        def _():
            first_hop(k - 1).start()

        @pl.when(k - 1 >= n_rel)
        def _():
            direct_send(k - 1).start()

        @pl.when(k == n_rel + 4)
        def _():
            forwards()

        return carry

    lax.fori_loop(1, n_grp, step, 0)
    local.start()

    local.wait()
    for k in range(n_grp - 1):
        if k < n_rel:
            first_hop(k).wait_send()
        else:
            direct_send(k).wait_send()
    for j, (off, rel) in enumerate(relayed):
        _, dev = at(off[0] - rel[0], off[1] - rel[1])
        pltpu.make_async_remote_copy(
            src_ref=stage.at[j], dst_ref=y_ref.at[0], send_sem=send_sem.at[n_grp - 1 + j],
            recv_sem=recv_sem.at[0], device_id=dev, device_id_type=MESH_ID,
        ).wait_send()
    for s in range(1, n_grp):
        q = lax.rem(me + s, n_grp)
        pltpu.make_async_remote_copy(
            src_ref=buf.at[0], dst_ref=y_ref.at[q], send_sem=send_sem.at[0],
            recv_sem=recv_sem.at[q], device_id=peers[0], device_id_type=MESH_ID,
        ).wait_recv()


def expert_return(hidden, down_full, n_grp, collective_id):
    n_src, cap, ff = hidden.shape
    width = down_full.shape[1]
    out = jax.ShapeDtypeStruct((n_src, cap, width), jnp.bfloat16)
    vmem = pl.BlockSpec(memory_space=pltpu.VMEM)
    flops = 2 * n_src * cap * ff * width
    nbytes = hidden.size * 2 + down_full.size * 2 + 2 * n_src * cap * width * 2
    return pl.pallas_call(
        functools.partial(expert_return_kernel, n_grp),
        out_shape=out,
        in_specs=[vmem] * 2,
        out_specs=pl.BlockSpec(memory_space=pl.ANY),
        scratch_shapes=[
            pltpu.VMEM((n_src, cap, width), jnp.bfloat16),
            pltpu.VMEM((7, cap, width), jnp.bfloat16),
            pltpu.SemaphoreType.DMA((n_grp + 8,)),
            pltpu.SemaphoreType.DMA((n_grp,)),
            pltpu.SemaphoreType.DMA((7,)),
            pltpu.SemaphoreType.DMA((1,)),
        ],
        compiler_params=pltpu.CompilerParams(
            collective_id=collective_id, has_side_effects=True, vmem_limit_bytes=56 * 1024 * 1024
        ),
        cost_estimate=pl.CostEstimate(flops=flops, transcendentals=0, bytes_accessed=nbytes),
    )(hidden, down_full)


def weight_kernel(n_x, n_grp, g_in, u_in, d_in, t_in, g_out, u_out, d_out, t_out, send_sem, recv_sem,
                  local_sem, t_send, t_recv, stage, stage_sem):
    ins = (g_in, u_in, d_in)
    outs = (g_out, u_out, d_out)
    x = lax.axis_index("x")
    h = lax.axis_index("zhi")
    c = lax.axis_index("core")

    def block(xx, hh, cc):
        return (xx * 2 + hh) * 2 + cc

    me = block(x, h, c)
    up_x = lax.rem(x + 1, n_x)
    down_x = lax.rem(x + n_x - 1, n_x)
    far_x = lax.rem(x + 2, n_x)
    toward = jnp.where(c == 0, up_x, down_x)
    away = jnp.where(c == 0, down_x, up_x)
    partner = {"core": 1 - c}
    z_peer = {"zhi": 1 - h}
    x_devs = [{"x": up_x}, {"x": down_x}]

    t_me, t_peers = exchange_peers(n_grp)
    barrier = pltpu.get_barrier_semaphore()
    greet = [partner, z_peer] + x_devs + plane_devices(n_grp)
    for dev in greet:
        pl.semaphore_signal(barrier, inc=1, device_id=dev, device_id_type=MESH_ID)
    pl.semaphore_wait(barrier, len(greet))

    count = [0]

    def send(src_of, blk, dev):
        k = count[0]
        count[0] += 1
        copies = []
        for m in range(3):
            cp = pltpu.make_async_remote_copy(
                src_ref=src_of(m),
                dst_ref=outs[m].at[blk],
                send_sem=send_sem.at[m, k],
                recv_sem=recv_sem.at[m, blk],
                device_id=dev,
                device_id_type=MESH_ID,
            )
            cp.start()
            copies.append(cp)
        return copies

    def wait_in(blk):
        for m in range(3):
            pltpu.make_async_remote_copy(
                src_ref=ins[m].at[0],
                dst_ref=outs[m].at[blk],
                send_sem=send_sem.at[m, 0],
                recv_sem=recv_sem.at[m, blk],
                device_id=partner,
                device_id_type=MESH_ID,
            ).wait_recv()

    sent = []
    local = []
    for m in range(3):
        cp = pltpu.make_async_copy(ins[m].at[h], outs[m].at[me], local_sem.at[m])
        cp.start()
        local.append(cp)
    sent += send(lambda m: ins[m].at[1 - h], me, z_peer)
    for dev in [partner] + x_devs:
        sent += send(lambda m: ins[m].at[h], me, dev)
    t_local, t_copies, t_k = start_plane(
        n_grp, t_in, t_out, stage, t_send, t_recv, stage_sem, local_sem.at[3]
    )

    z_blk = block(x, 1 - h, c)
    wait_in(z_blk)
    for dev in [partner] + x_devs:
        sent += send(lambda m: outs[m].at[z_blk], z_blk, dev)
    t_copies += relay_plane(n_grp, t_k, t_in, t_out, stage, t_send, t_recv, stage_sem)

    for hh in (h, 1 - h):
        blk = block(away, hh, c)
        wait_in(blk)
        sent += send(lambda m: outs[m].at[blk], blk, partner)
        sent += send(lambda m: outs[m].at[blk], blk, {"x": toward})
    for xp in (toward, far_x):
        for hh in (h, 1 - h):
            blk = block(xp, hh, c)
            wait_in(blk)
            sent += send(lambda m: outs[m].at[blk], blk, partner)

    for xx in range(n_x):
        for hh in (0, 1):
            wait_in(block(xx, hh, 1 - c))

    for cp in sent:
        cp.wait_send()
    for cp in local:
        cp.wait()
    finish_exchange(t_peers, t_local, t_copies, t_in, t_out, t_send, t_recv)


def gather_weights(gate_weight, up_weight, down_weight, outgoing, n_x, n_grp):
    blk_rows, width = gate_weight.shape[1], gate_weight.shape[2]
    n_blocks = n_x * 4
    n_send = 16
    shape = jax.ShapeDtypeStruct((n_blocks, blk_rows, width), gate_weight.dtype)
    any_spec = pl.BlockSpec(memory_space=pl.ANY)
    nbytes = 3 * n_blocks * blk_rows * width * 2
    return pl.pallas_call(
        functools.partial(weight_kernel, n_x, n_grp),
        out_shape=(shape, shape, shape, jax.ShapeDtypeStruct(outgoing.shape, outgoing.dtype)),
        in_specs=[any_spec] * 4,
        out_specs=(any_spec, any_spec, any_spec, any_spec),
        scratch_shapes=[
            pltpu.SemaphoreType.DMA((3, n_send)),
            pltpu.SemaphoreType.DMA((3, n_blocks)),
            pltpu.SemaphoreType.DMA((4,)),
            pltpu.SemaphoreType.DMA((n_grp + 8,)),
            pltpu.SemaphoreType.DMA((n_grp,)),
            pltpu.VMEM((7,) + outgoing.shape[1:], outgoing.dtype),
            pltpu.SemaphoreType.DMA((7,)),
        ],
        compiler_params=pltpu.CompilerParams(collective_id=0, has_side_effects=True),
        cost_estimate=pl.CostEstimate(flops=0, transcendentals=0, bytes_accessed=nbytes),
    )(gate_weight, up_weight, down_weight, outgoing)


def per_device(tokens, expert_ids, combine, gate_weight, up_weight, down_weight):
    n_x = lax.axis_size("x")
    assert n_x == 4
    per_group = gate_weight.shape[0]
    groups = lax.axis_size("expert")
    n_expert = per_group * groups
    n_grp = groups * 2
    assert n_grp == 16
    tok_rows, top_k = expert_ids.shape
    model_width = tokens.shape[1]
    n_slot = n_expert * CAP

    flat_ids = expert_ids.reshape(-1)
    onehot = (flat_ids[:, None] == jnp.arange(n_expert, dtype=jnp.int32)[None, :]).astype(jnp.int32)
    earlier = jnp.cumsum(onehot, axis=0) - onehot
    rank_within = jnp.sum(earlier * onehot, axis=1)
    slot_index = (flat_ids * CAP + rank_within).reshape(tok_rows, top_k)
    hit = slot_index[None, :, :] == jnp.arange(n_slot, dtype=jnp.int32)[:, None, None]
    pick = jnp.any(hit, axis=2).astype(jnp.bfloat16)
    outgoing = jnp.dot(pick, tokens, preferred_element_type=jnp.float32).astype(jnp.bfloat16)
    outgoing = outgoing.reshape(n_expert, CAP, model_width)

    g_all, u_all, d_all, arrived = gather_weights(
        gate_weight, up_weight, down_weight, outgoing, n_x, n_grp
    )
    gate_full = g_all.reshape(-1, model_width)
    up_full = u_all.reshape(-1, model_width)
    down_full = d_all.reshape(-1, model_width)
    gate_pre = jnp.einsum("scd,fd->scf", arrived, gate_full, preferred_element_type=jnp.float32)
    up_pre = jnp.einsum("scd,fd->scf", arrived, up_full, preferred_element_type=jnp.float32)
    hidden = (jax.nn.silu(gate_pre) * up_pre).astype(jnp.bfloat16)
    returned = expert_return(hidden, down_full, n_grp, 1)
    returned = returned.reshape(n_slot, model_width)

    weight_of = jnp.sum(
        jnp.where(hit, combine[None, :, :], jnp.zeros_like(combine)[None, :, :]), axis=2
    ).T
    weight_top = lax.reduce_precision(weight_of, exponent_bits=8, mantissa_bits=7)
    weight_hi = weight_top.astype(jnp.bfloat16)
    weight_lo = (weight_of - weight_top).astype(jnp.bfloat16)
    mixed = jnp.dot(weight_hi, returned, preferred_element_type=jnp.float32) + jnp.dot(
        weight_lo, returned, preferred_element_type=jnp.float32
    )
    return mixed.astype(jnp.bfloat16)


def solution(mesh):
    groups = mesh.shape["expert"]
    n_x = mesh.shape["fsdp"] // 4
    inner = Mesh(mesh.devices.reshape(groups, n_x, 2, 2), ("expert", "x", "zhi", "core"))
    rows = P(("expert", "x", "zhi", "core"), None)
    weights = P("expert", ("x", "zhi", "core"), None)
    return jax.shard_map(
        per_device,
        mesh=inner,
        in_specs=(rows, rows, rows, weights, weights, weights),
        out_specs=rows,
        check_vma=False,
    )
```

```python
import functools

import jax
import jax.numpy as jnp
from jax import lax
from jax.experimental import pallas as pl
from jax.experimental.pallas import tpu as pltpu
from jax.sharding import Mesh
from jax.sharding import PartitionSpec as P

CAP = 72
MESH_ID = pl.DeviceIdType.MESH


def exchange_peers(n_grp):
    me = lax.axis_index("expert") * 2 + lax.axis_index("zhi")
    peers = []
    for s in range(1, n_grp):
        p = lax.rem(me + s, n_grp)
        peers.append((p, {"expert": p // 2, "zhi": lax.rem(p, 2)}))
    return me, peers


def start_exchange(me, peers, x_ref, y_ref, send_sem, recv_sem, local_sem):
    copies = []
    local = pltpu.make_async_copy(x_ref.at[me], y_ref.at[me], local_sem)
    local.start()
    for k, (p, dev) in enumerate(peers):
        cp = pltpu.make_async_remote_copy(
            src_ref=x_ref.at[p],
            dst_ref=y_ref.at[me],
            send_sem=send_sem.at[k],
            recv_sem=recv_sem.at[me],
            device_id=dev,
            device_id_type=MESH_ID,
        )
        cp.start()
        copies.append(cp)
    return local, copies


def finish_exchange(peers, local, copies, x_ref, y_ref, send_sem, recv_sem):
    for k, (p, dev) in enumerate(peers):
        pltpu.make_async_remote_copy(
            src_ref=x_ref.at[0],
            dst_ref=y_ref.at[p],
            send_sem=send_sem.at[k],
            recv_sem=recv_sem.at[p],
            device_id=dev,
            device_id_type=MESH_ID,
        ).wait_recv()
    for cp in copies:
        cp.wait_send()
    local.wait()


def plane_plan(n_grp):
    e_idx = lax.axis_index("expert")
    h = lax.axis_index("zhi")
    c = lax.axis_index("core")
    y = e_idx // 2
    z = h * 2 + lax.rem(e_idx, 2)
    s = 1 - 2 * c

    def at(dy, dz):
        yy = lax.rem(y + dy + 4, 4)
        zz = lax.rem(z + dz + 4, 4)
        p = (yy * 2 + lax.rem(zz, 2)) * 2 + zz // 2
        return p, {"expert": yy * 2 + lax.rem(zz, 2), "zhi": zz // 2}

    direct = [(dy, dz) for dy in (0, 1, 3) for dz in (0, 1, 3) if (dy, dz) != (0, 0)]
    relayed = [((2, dz), (s, 0)) for dz in (0, 1, 3)]
    relayed += [((dy, 2), (0, s)) for dy in (0, 1, 3)]
    relayed += [((2, 2), (s, s))]
    me = (y * 2 + lax.rem(z, 2)) * 2 + z // 2
    return me, at, direct, relayed


def start_plane(n_grp, x_ref, y_ref, stage, send_sem, recv_sem, stage_sem, local_sem):
    me, at, direct, relayed = plane_plan(n_grp)
    copies = []
    local = pltpu.make_async_copy(x_ref.at[me], y_ref.at[me], local_sem)
    local.start()
    k = 0
    for j, (off, rel) in enumerate(relayed):
        p, _ = at(*off)
        _, dev = at(*rel)
        cp = pltpu.make_async_remote_copy(
            src_ref=x_ref.at[p], dst_ref=stage.at[j], send_sem=send_sem.at[k],
            recv_sem=stage_sem.at[j], device_id=dev, device_id_type=MESH_ID,
        )
        cp.start()
        copies.append(cp)
        k += 1
    for off in direct:
        p, dev = at(*off)
        cp = pltpu.make_async_remote_copy(
            src_ref=x_ref.at[p], dst_ref=y_ref.at[me], send_sem=send_sem.at[k],
            recv_sem=recv_sem.at[me], device_id=dev, device_id_type=MESH_ID,
        )
        cp.start()
        copies.append(cp)
        k += 1
    return local, copies, k


def relay_plane(n_grp, k, x_ref, y_ref, stage, send_sem, recv_sem, stage_sem):
    me, at, direct, relayed = plane_plan(n_grp)
    copies = []
    for j, (off, rel) in enumerate(relayed):
        src_p, _ = at(-rel[0], -rel[1])
        _, dev = at(off[0] - rel[0], off[1] - rel[1])
        pltpu.make_async_remote_copy(
            src_ref=x_ref.at[0], dst_ref=stage.at[j], send_sem=send_sem.at[0],
            recv_sem=stage_sem.at[j], device_id=dev, device_id_type=MESH_ID,
        ).wait_recv()
        cp = pltpu.make_async_remote_copy(
            src_ref=stage.at[j], dst_ref=y_ref.at[src_p], send_sem=send_sem.at[k],
            recv_sem=recv_sem.at[src_p], device_id=dev, device_id_type=MESH_ID,
        )
        cp.start()
        copies.append(cp)
        k += 1
    return copies


def plane_devices(n_grp):
    me, at, direct, relayed = plane_plan(n_grp)
    return [at(*off)[1] for off in direct]


def exchange_kernel(n_grp, x_ref, y_ref, send_sem, recv_sem, local_sem):
    me, peers = exchange_peers(n_grp)
    barrier = pltpu.get_barrier_semaphore()
    for p, dev in peers:
        pl.semaphore_signal(barrier, inc=1, device_id=dev, device_id_type=MESH_ID)
    pl.semaphore_wait(barrier, len(peers))
    local, copies = start_exchange(me, peers, x_ref, y_ref, send_sem, recv_sem, local_sem.at[0])
    finish_exchange(peers, local, copies, x_ref, y_ref, send_sem, recv_sem)


def exchange(x, n_grp, collective_id):
    any_spec = pl.BlockSpec(memory_space=pl.ANY)
    return pl.pallas_call(
        functools.partial(exchange_kernel, n_grp),
        out_shape=jax.ShapeDtypeStruct(x.shape, x.dtype),
        in_specs=[any_spec],
        out_specs=any_spec,
        scratch_shapes=[
            pltpu.SemaphoreType.DMA((n_grp,)),
            pltpu.SemaphoreType.DMA((n_grp,)),
            pltpu.SemaphoreType.DMA((1,)),
        ],
        compiler_params=pltpu.CompilerParams(collective_id=collective_id, has_side_effects=True),
        cost_estimate=pl.CostEstimate(flops=0, transcendentals=0, bytes_accessed=2 * x.size * 2),
    )(x)


def expert_return_kernel(n_grp, gate_ref, up_ref, down_ref, y_ref, buf, stage, send_sem, recv_sem,
                         stage_sem, local_sem):
    me, at, direct, relayed = plane_plan(n_grp)
    n_rel = len(relayed)
    order = [off for off, rel in relayed] + direct + [(0, 0)]
    rel_of = [rel for off, rel in relayed]
    barrier = pltpu.get_barrier_semaphore()
    peers = plane_devices(n_grp)
    for dev in peers:
        pl.semaphore_signal(barrier, inc=1, device_id=dev, device_id_type=MESH_ID)

    def pick(k, values):
        out = values[-1]
        for i in range(len(values) - 2, -1, -1):
            out = jnp.where(k == i, values[i], out)
        return out

    def chunk_of(k):
        dy = pick(k, [o[0] for o in order])
        dz = pick(k, [o[1] for o in order])
        return at(dy, dz)

    def project(k):
        p, _ = chunk_of(k)
        hidden = (jax.nn.silu(gate_ref[p]) * up_ref[p]).astype(jnp.bfloat16)
        buf[p] = jnp.dot(hidden, down_ref[...], preferred_element_type=jnp.float32).astype(buf.dtype)

    def first_hop(k):
        p, _ = chunk_of(k)
        ry = pick(k, [r[0] for r in rel_of])
        rz = pick(k, [r[1] for r in rel_of])
        _, dev = at(ry, rz)
        return pltpu.make_async_remote_copy(
            src_ref=buf.at[p], dst_ref=stage.at[k], send_sem=send_sem.at[k],
            recv_sem=stage_sem.at[k], device_id=dev, device_id_type=MESH_ID,
        )

    def direct_send(k):
        p, dev = chunk_of(k)
        return pltpu.make_async_remote_copy(
            src_ref=buf.at[p], dst_ref=y_ref.at[me], send_sem=send_sem.at[k],
            recv_sem=recv_sem.at[me], device_id=dev, device_id_type=MESH_ID,
        )

    def forwards():
        for j, (off, rel) in enumerate(relayed):
            src_p, _ = at(-rel[0], -rel[1])
            _, dev = at(off[0] - rel[0], off[1] - rel[1])
            pltpu.make_async_remote_copy(
                src_ref=buf.at[0], dst_ref=stage.at[j], send_sem=send_sem.at[0],
                recv_sem=stage_sem.at[j], device_id=dev, device_id_type=MESH_ID,
            ).wait_recv()
            pltpu.make_async_remote_copy(
                src_ref=stage.at[j], dst_ref=y_ref.at[src_p], send_sem=send_sem.at[n_grp - 1 + j],
                recv_sem=recv_sem.at[src_p], device_id=dev, device_id_type=MESH_ID,
            ).start()

    local = pltpu.make_async_copy(buf.at[me], y_ref.at[me], local_sem.at[0])
    project(0)
    pl.semaphore_wait(barrier, len(peers))

    def step(k, carry):
        project(k)

        @pl.when(k - 1 < n_rel)
        def _():
            first_hop(k - 1).start()

        @pl.when(k - 1 >= n_rel)
        def _():
            direct_send(k - 1).start()

        @pl.when(k == n_rel + 4)
        def _():
            forwards()

        return carry

    lax.fori_loop(1, n_grp, step, 0)
    local.start()

    local.wait()
    for k in range(n_grp - 1):
        if k < n_rel:
            first_hop(k).wait_send()
        else:
            direct_send(k).wait_send()
    for j, (off, rel) in enumerate(relayed):
        _, dev = at(off[0] - rel[0], off[1] - rel[1])
        pltpu.make_async_remote_copy(
            src_ref=stage.at[j], dst_ref=y_ref.at[0], send_sem=send_sem.at[n_grp - 1 + j],
            recv_sem=recv_sem.at[0], device_id=dev, device_id_type=MESH_ID,
        ).wait_send()
    for s in range(1, n_grp):
        q = lax.rem(me + s, n_grp)
        pltpu.make_async_remote_copy(
            src_ref=buf.at[0], dst_ref=y_ref.at[q], send_sem=send_sem.at[0],
            recv_sem=recv_sem.at[q], device_id=peers[0], device_id_type=MESH_ID,
        ).wait_recv()


def expert_return(gate_pre, up_pre, down_full, n_grp, collective_id):
    n_src, cap, ff = gate_pre.shape
    width = down_full.shape[1]
    out = jax.ShapeDtypeStruct((n_src, cap, width), jnp.bfloat16)
    vmem = pl.BlockSpec(memory_space=pltpu.VMEM)
    flops = 2 * n_src * cap * ff * width
    nbytes = gate_pre.size * 8 + down_full.size * 2 + 2 * n_src * cap * width * 2
    return pl.pallas_call(
        functools.partial(expert_return_kernel, n_grp),
        out_shape=out,
        in_specs=[vmem] * 3,
        out_specs=pl.BlockSpec(memory_space=pl.ANY),
        scratch_shapes=[
            pltpu.VMEM((n_src, cap, width), jnp.bfloat16),
            pltpu.VMEM((7, cap, width), jnp.bfloat16),
            pltpu.SemaphoreType.DMA((n_grp + 8,)),
            pltpu.SemaphoreType.DMA((n_grp,)),
            pltpu.SemaphoreType.DMA((7,)),
            pltpu.SemaphoreType.DMA((1,)),
        ],
        compiler_params=pltpu.CompilerParams(
            collective_id=collective_id, has_side_effects=True, vmem_limit_bytes=56 * 1024 * 1024
        ),
        cost_estimate=pl.CostEstimate(flops=flops, transcendentals=gate_pre.size, bytes_accessed=nbytes),
    )(gate_pre, up_pre, down_full)


def weight_kernel(n_x, n_grp, g_in, u_in, d_in, t_in, g_out, u_out, d_out, t_out, send_sem, recv_sem,
                  local_sem, t_send, t_recv, stage, stage_sem):
    ins = (g_in, u_in, d_in)
    outs = (g_out, u_out, d_out)
    x = lax.axis_index("x")
    h = lax.axis_index("zhi")
    c = lax.axis_index("core")

    def block(xx, hh, cc):
        return (xx * 2 + hh) * 2 + cc

    me = block(x, h, c)
    up_x = lax.rem(x + 1, n_x)
    down_x = lax.rem(x + n_x - 1, n_x)
    far_x = lax.rem(x + 2, n_x)
    toward = jnp.where(c == 0, up_x, down_x)
    away = jnp.where(c == 0, down_x, up_x)
    partner = {"core": 1 - c}
    z_peer = {"zhi": 1 - h}
    x_devs = [{"x": up_x}, {"x": down_x}]

    t_me, t_peers = exchange_peers(n_grp)
    barrier = pltpu.get_barrier_semaphore()
    greet = [partner, z_peer] + x_devs + plane_devices(n_grp)
    for dev in greet:
        pl.semaphore_signal(barrier, inc=1, device_id=dev, device_id_type=MESH_ID)
    pl.semaphore_wait(barrier, len(greet))

    count = [0]

    def send(src_of, blk, dev):
        k = count[0]
        count[0] += 1
        copies = []
        for m in range(3):
            cp = pltpu.make_async_remote_copy(
                src_ref=src_of(m),
                dst_ref=outs[m].at[blk],
                send_sem=send_sem.at[m, k],
                recv_sem=recv_sem.at[m, blk],
                device_id=dev,
                device_id_type=MESH_ID,
            )
            cp.start()
            copies.append(cp)
        return copies

    def wait_in(blk):
        for m in range(3):
            pltpu.make_async_remote_copy(
                src_ref=ins[m].at[0],
                dst_ref=outs[m].at[blk],
                send_sem=send_sem.at[m, 0],
                recv_sem=recv_sem.at[m, blk],
                device_id=partner,
                device_id_type=MESH_ID,
            ).wait_recv()

    sent = []
    local = []
    for m in range(3):
        cp = pltpu.make_async_copy(ins[m].at[h], outs[m].at[me], local_sem.at[m])
        cp.start()
        local.append(cp)
    sent += send(lambda m: ins[m].at[1 - h], me, z_peer)
    for dev in [partner] + x_devs:
        sent += send(lambda m: ins[m].at[h], me, dev)
    t_local, t_copies, t_k = start_plane(
        n_grp, t_in, t_out, stage, t_send, t_recv, stage_sem, local_sem.at[3]
    )

    z_blk = block(x, 1 - h, c)
    wait_in(z_blk)
    for dev in [partner] + x_devs:
        sent += send(lambda m: outs[m].at[z_blk], z_blk, dev)
    t_copies += relay_plane(n_grp, t_k, t_in, t_out, stage, t_send, t_recv, stage_sem)

    for hh in (h, 1 - h):
        blk = block(away, hh, c)
        wait_in(blk)
        sent += send(lambda m: outs[m].at[blk], blk, partner)
        sent += send(lambda m: outs[m].at[blk], blk, {"x": toward})
    for xp in (toward, far_x):
        for hh in (h, 1 - h):
            blk = block(xp, hh, c)
            wait_in(blk)
            sent += send(lambda m: outs[m].at[blk], blk, partner)

    for xx in range(n_x):
        for hh in (0, 1):
            wait_in(block(xx, hh, 1 - c))

    for cp in sent:
        cp.wait_send()
    for cp in local:
        cp.wait()
    finish_exchange(t_peers, t_local, t_copies, t_in, t_out, t_send, t_recv)


def gather_weights(gate_weight, up_weight, down_weight, outgoing, n_x, n_grp):
    blk_rows, width = gate_weight.shape[1], gate_weight.shape[2]
    n_blocks = n_x * 4
    n_send = 16
    shape = jax.ShapeDtypeStruct((n_blocks, blk_rows, width), gate_weight.dtype)
    any_spec = pl.BlockSpec(memory_space=pl.ANY)
    nbytes = 3 * n_blocks * blk_rows * width * 2
    return pl.pallas_call(
        functools.partial(weight_kernel, n_x, n_grp),
        out_shape=(shape, shape, shape, jax.ShapeDtypeStruct(outgoing.shape, outgoing.dtype)),
        in_specs=[any_spec] * 4,
        out_specs=(any_spec, any_spec, any_spec, any_spec),
        scratch_shapes=[
            pltpu.SemaphoreType.DMA((3, n_send)),
            pltpu.SemaphoreType.DMA((3, n_blocks)),
            pltpu.SemaphoreType.DMA((4,)),
            pltpu.SemaphoreType.DMA((n_grp + 8,)),
            pltpu.SemaphoreType.DMA((n_grp,)),
            pltpu.VMEM((7,) + outgoing.shape[1:], outgoing.dtype),
            pltpu.SemaphoreType.DMA((7,)),
        ],
        compiler_params=pltpu.CompilerParams(collective_id=0, has_side_effects=True),
        cost_estimate=pl.CostEstimate(flops=0, transcendentals=0, bytes_accessed=nbytes),
    )(gate_weight, up_weight, down_weight, outgoing)


def per_device(tokens, expert_ids, combine, gate_weight, up_weight, down_weight):
    n_x = lax.axis_size("x")
    assert n_x == 4
    per_group = gate_weight.shape[0]
    groups = lax.axis_size("expert")
    n_expert = per_group * groups
    n_grp = groups * 2
    assert n_grp == 16
    tok_rows, top_k = expert_ids.shape
    model_width = tokens.shape[1]
    n_slot = n_expert * CAP

    flat_ids = expert_ids.reshape(-1)
    onehot = (flat_ids[:, None] == jnp.arange(n_expert, dtype=jnp.int32)[None, :]).astype(jnp.int32)
    earlier = jnp.cumsum(onehot, axis=0) - onehot
    rank_within = jnp.sum(earlier * onehot, axis=1)
    slot_index = (flat_ids * CAP + rank_within).reshape(tok_rows, top_k)
    hit = slot_index[None, :, :] == jnp.arange(n_slot, dtype=jnp.int32)[:, None, None]
    pick = jnp.any(hit, axis=2).astype(jnp.bfloat16)
    outgoing = jnp.dot(pick, tokens, preferred_element_type=jnp.float32).astype(jnp.bfloat16)
    outgoing = outgoing.reshape(n_expert, CAP, model_width)

    g_all, u_all, d_all, arrived = gather_weights(
        gate_weight, up_weight, down_weight, outgoing, n_x, n_grp
    )
    gate_full = g_all.reshape(-1, model_width)
    up_full = u_all.reshape(-1, model_width)
    down_full = d_all.reshape(-1, model_width)
    gate_pre = jnp.einsum("scd,fd->scf", arrived, gate_full, preferred_element_type=jnp.float32)
    up_pre = jnp.einsum("scd,fd->scf", arrived, up_full, preferred_element_type=jnp.float32)
    returned = expert_return(gate_pre, up_pre, down_full, n_grp, 1)
    returned = returned.reshape(n_slot, model_width)

    weight_of = jnp.sum(
        jnp.where(hit, combine[None, :, :], jnp.zeros_like(combine)[None, :, :]), axis=2
    ).T
    weight_top = lax.reduce_precision(weight_of, exponent_bits=8, mantissa_bits=7)
    weight_hi = weight_top.astype(jnp.bfloat16)
    weight_lo = (weight_of - weight_top).astype(jnp.bfloat16)
    mixed = jnp.dot(weight_hi, returned, preferred_element_type=jnp.float32) + jnp.dot(
        weight_lo, returned, preferred_element_type=jnp.float32
    )
    return mixed.astype(jnp.bfloat16)


def solution(mesh):
    groups = mesh.shape["expert"]
    n_x = mesh.shape["fsdp"] // 4
    inner = Mesh(mesh.devices.reshape(groups, n_x, 2, 2), ("expert", "x", "zhi", "core"))
    rows = P(("expert", "x", "zhi", "core"), None)
    weights = P("expert", ("x", "zhi", "core"), None)
    return jax.shard_map(
        per_device,
        mesh=inner,
        in_specs=(rows, rows, rows, weights, weights, weights),
        out_specs=rows,
        check_vma=False,
    )
```

```python
import functools

import jax
import jax.numpy as jnp
from jax import lax
from jax.experimental import pallas as pl
from jax.experimental.pallas import tpu as pltpu
from jax.sharding import Mesh
from jax.sharding import PartitionSpec as P

CAP = 72
MESH_ID = pl.DeviceIdType.MESH


def exchange_peers(n_grp):
    me = lax.axis_index("expert") * 2 + lax.axis_index("zhi")
    peers = []
    for s in range(1, n_grp):
        p = lax.rem(me + s, n_grp)
        peers.append((p, {"expert": p // 2, "zhi": lax.rem(p, 2)}))
    return me, peers


def start_exchange(me, peers, x_ref, y_ref, send_sem, recv_sem, local_sem):
    copies = []
    local = pltpu.make_async_copy(x_ref.at[me], y_ref.at[me], local_sem)
    local.start()
    for k, (p, dev) in enumerate(peers):
        cp = pltpu.make_async_remote_copy(
            src_ref=x_ref.at[p],
            dst_ref=y_ref.at[me],
            send_sem=send_sem.at[k],
            recv_sem=recv_sem.at[me],
            device_id=dev,
            device_id_type=MESH_ID,
        )
        cp.start()
        copies.append(cp)
    return local, copies


def finish_exchange(peers, local, copies, x_ref, y_ref, send_sem, recv_sem):
    for k, (p, dev) in enumerate(peers):
        pltpu.make_async_remote_copy(
            src_ref=x_ref.at[0],
            dst_ref=y_ref.at[p],
            send_sem=send_sem.at[k],
            recv_sem=recv_sem.at[p],
            device_id=dev,
            device_id_type=MESH_ID,
        ).wait_recv()
    for cp in copies:
        cp.wait_send()
    local.wait()


def plane_plan(n_grp):
    e_idx = lax.axis_index("expert")
    h = lax.axis_index("zhi")
    c = lax.axis_index("core")
    y = e_idx // 2
    z = h * 2 + lax.rem(e_idx, 2)
    s = 1 - 2 * c

    def at(dy, dz):
        yy = lax.rem(y + dy + 4, 4)
        zz = lax.rem(z + dz + 4, 4)
        p = (yy * 2 + lax.rem(zz, 2)) * 2 + zz // 2
        return p, {"expert": yy * 2 + lax.rem(zz, 2), "zhi": zz // 2}

    direct = [(dy, dz) for dy in (0, 1, 3) for dz in (0, 1, 3) if (dy, dz) != (0, 0)]
    relayed = [((2, dz), (s, 0)) for dz in (0, 1, 3)]
    relayed += [((dy, 2), (0, s)) for dy in (0, 1, 3)]
    relayed += [((2, 2), (s, s))]
    me = (y * 2 + lax.rem(z, 2)) * 2 + z // 2
    return me, at, direct, relayed


def start_plane(n_grp, x_ref, y_ref, stage, send_sem, recv_sem, stage_sem, local_sem):
    me, at, direct, relayed = plane_plan(n_grp)
    copies = []
    local = pltpu.make_async_copy(x_ref.at[me], y_ref.at[me], local_sem)
    local.start()
    k = 0
    for j, (off, rel) in enumerate(relayed):
        p, _ = at(*off)
        _, dev = at(*rel)
        cp = pltpu.make_async_remote_copy(
            src_ref=x_ref.at[p], dst_ref=stage.at[j], send_sem=send_sem.at[k],
            recv_sem=stage_sem.at[j], device_id=dev, device_id_type=MESH_ID,
        )
        cp.start()
        copies.append(cp)
        k += 1
    for off in direct:
        p, dev = at(*off)
        cp = pltpu.make_async_remote_copy(
            src_ref=x_ref.at[p], dst_ref=y_ref.at[me], send_sem=send_sem.at[k],
            recv_sem=recv_sem.at[me], device_id=dev, device_id_type=MESH_ID,
        )
        cp.start()
        copies.append(cp)
        k += 1
    return local, copies, k


def relay_plane(n_grp, k, x_ref, y_ref, stage, send_sem, recv_sem, stage_sem):
    me, at, direct, relayed = plane_plan(n_grp)
    copies = []
    for j, (off, rel) in enumerate(relayed):
        src_p, _ = at(-rel[0], -rel[1])
        _, dev = at(off[0] - rel[0], off[1] - rel[1])
        pltpu.make_async_remote_copy(
            src_ref=x_ref.at[0], dst_ref=stage.at[j], send_sem=send_sem.at[0],
            recv_sem=stage_sem.at[j], device_id=dev, device_id_type=MESH_ID,
        ).wait_recv()
        cp = pltpu.make_async_remote_copy(
            src_ref=stage.at[j], dst_ref=y_ref.at[src_p], send_sem=send_sem.at[k],
            recv_sem=recv_sem.at[src_p], device_id=dev, device_id_type=MESH_ID,
        )
        cp.start()
        copies.append(cp)
        k += 1
    return copies


def plane_devices(n_grp):
    me, at, direct, relayed = plane_plan(n_grp)
    return [at(*off)[1] for off in direct]


def exchange_kernel(n_grp, x_ref, y_ref, send_sem, recv_sem, local_sem):
    me, peers = exchange_peers(n_grp)
    barrier = pltpu.get_barrier_semaphore()
    for p, dev in peers:
        pl.semaphore_signal(barrier, inc=1, device_id=dev, device_id_type=MESH_ID)
    pl.semaphore_wait(barrier, len(peers))
    local, copies = start_exchange(me, peers, x_ref, y_ref, send_sem, recv_sem, local_sem.at[0])
    finish_exchange(peers, local, copies, x_ref, y_ref, send_sem, recv_sem)


def exchange(x, n_grp, collective_id):
    any_spec = pl.BlockSpec(memory_space=pl.ANY)
    return pl.pallas_call(
        functools.partial(exchange_kernel, n_grp),
        out_shape=jax.ShapeDtypeStruct(x.shape, x.dtype),
        in_specs=[any_spec],
        out_specs=any_spec,
        scratch_shapes=[
            pltpu.SemaphoreType.DMA((n_grp,)),
            pltpu.SemaphoreType.DMA((n_grp,)),
            pltpu.SemaphoreType.DMA((1,)),
        ],
        compiler_params=pltpu.CompilerParams(collective_id=collective_id, has_side_effects=True),
        cost_estimate=pl.CostEstimate(flops=0, transcendentals=0, bytes_accessed=2 * x.size * 2),
    )(x)


def expert_return_kernel(n_grp, hid_ref, down_ref, y_ref, buf, stage, send_sem, recv_sem, stage_sem,
                         local_sem):
    me, at, direct, relayed = plane_plan(n_grp)
    n_rel = len(relayed)
    order = [off for off, rel in relayed] + direct + [(0, 0)]
    rel_of = [rel for off, rel in relayed]
    barrier = pltpu.get_barrier_semaphore()
    peers = plane_devices(n_grp)
    for dev in peers:
        pl.semaphore_signal(barrier, inc=1, device_id=dev, device_id_type=MESH_ID)

    def pick(k, values):
        out = values[-1]
        for i in range(len(values) - 2, -1, -1):
            out = jnp.where(k == i, values[i], out)
        return out

    def chunk_of(k):
        dy = pick(k, [o[0] for o in order])
        dz = pick(k, [o[1] for o in order])
        return at(dy, dz)

    def project(k):
        p, _ = chunk_of(k)
        buf[p] = jnp.dot(hid_ref[p], down_ref[...], preferred_element_type=jnp.float32).astype(buf.dtype)

    def first_hop(k):
        p, _ = chunk_of(k)
        ry = pick(k, [r[0] for r in rel_of])
        rz = pick(k, [r[1] for r in rel_of])
        _, dev = at(ry, rz)
        return pltpu.make_async_remote_copy(
            src_ref=buf.at[p], dst_ref=stage.at[k], send_sem=send_sem.at[k],
            recv_sem=stage_sem.at[k], device_id=dev, device_id_type=MESH_ID,
        )

    def direct_send(k):
        p, dev = chunk_of(k)
        return pltpu.make_async_remote_copy(
            src_ref=buf.at[p], dst_ref=y_ref.at[me], send_sem=send_sem.at[k],
            recv_sem=recv_sem.at[me], device_id=dev, device_id_type=MESH_ID,
        )

    def forwards():
        for j, (off, rel) in enumerate(relayed):
            src_p, _ = at(-rel[0], -rel[1])
            _, dev = at(off[0] - rel[0], off[1] - rel[1])
            pltpu.make_async_remote_copy(
                src_ref=buf.at[0], dst_ref=stage.at[j], send_sem=send_sem.at[0],
                recv_sem=stage_sem.at[j], device_id=dev, device_id_type=MESH_ID,
            ).wait_recv()
            pltpu.make_async_remote_copy(
                src_ref=stage.at[j], dst_ref=y_ref.at[src_p], send_sem=send_sem.at[n_grp - 1 + j],
                recv_sem=recv_sem.at[src_p], device_id=dev, device_id_type=MESH_ID,
            ).start()

    local = pltpu.make_async_copy(buf.at[me], y_ref.at[me], local_sem.at[0])
    project(0)
    pl.semaphore_wait(barrier, len(peers))

    def step(k, carry):
        project(k)

        @pl.when(k - 1 < n_rel)
        def _():
            first_hop(k - 1).start()

        @pl.when(k - 1 >= n_rel)
        def _():
            direct_send(k - 1).start()

        @pl.when(k == n_rel + 4)
        def _():
            forwards()

        return carry

    lax.fori_loop(1, n_grp, step, 0)
    local.start()

    local.wait()
    for k in range(n_grp - 1):
        if k < n_rel:
            first_hop(k).wait_send()
        else:
            direct_send(k).wait_send()
    for j, (off, rel) in enumerate(relayed):
        _, dev = at(off[0] - rel[0], off[1] - rel[1])
        pltpu.make_async_remote_copy(
            src_ref=stage.at[j], dst_ref=y_ref.at[0], send_sem=send_sem.at[n_grp - 1 + j],
            recv_sem=recv_sem.at[0], device_id=dev, device_id_type=MESH_ID,
        ).wait_send()
    for s in range(1, n_grp):
        q = lax.rem(me + s, n_grp)
        pltpu.make_async_remote_copy(
            src_ref=buf.at[0], dst_ref=y_ref.at[q], send_sem=send_sem.at[0],
            recv_sem=recv_sem.at[q], device_id=peers[0], device_id_type=MESH_ID,
        ).wait_recv()


def expert_return(hidden, down_full, n_grp, collective_id):
    n_src, cap, ff = hidden.shape
    width = down_full.shape[1]
    out = jax.ShapeDtypeStruct((n_src, cap, width), jnp.bfloat16)
    vmem = pl.BlockSpec(memory_space=pltpu.VMEM)
    flops = 2 * n_src * cap * ff * width
    nbytes = hidden.size * 2 + down_full.size * 2 + 2 * n_src * cap * width * 2
    return pl.pallas_call(
        functools.partial(expert_return_kernel, n_grp),
        out_shape=out,
        in_specs=[vmem] * 2,
        out_specs=pl.BlockSpec(memory_space=pl.ANY),
        scratch_shapes=[
            pltpu.VMEM((n_src, cap, width), jnp.bfloat16),
            pltpu.VMEM((7, cap, width), jnp.bfloat16),
            pltpu.SemaphoreType.DMA((n_grp + 8,)),
            pltpu.SemaphoreType.DMA((n_grp,)),
            pltpu.SemaphoreType.DMA((7,)),
            pltpu.SemaphoreType.DMA((1,)),
        ],
        compiler_params=pltpu.CompilerParams(
            collective_id=collective_id, has_side_effects=True, vmem_limit_bytes=56 * 1024 * 1024
        ),
        cost_estimate=pl.CostEstimate(flops=flops, transcendentals=0, bytes_accessed=nbytes),
    )(hidden, down_full)


def weight_kernel(n_x, n_grp, g_in, u_in, d_in, t_in, g_out, u_out, d_out, t_out, send_sem, recv_sem,
                  local_sem, t_send, t_recv, stage, stage_sem):
    ins = (g_in, u_in, d_in)
    outs = (g_out, u_out, d_out)
    x = lax.axis_index("x")
    h = lax.axis_index("zhi")
    c = lax.axis_index("core")

    def block(xx, hh, cc):
        return (xx * 2 + hh) * 2 + cc

    me = block(x, h, c)
    up_x = lax.rem(x + 1, n_x)
    down_x = lax.rem(x + n_x - 1, n_x)
    far_x = lax.rem(x + 2, n_x)
    toward = jnp.where(c == 0, up_x, down_x)
    away = jnp.where(c == 0, down_x, up_x)
    partner = {"core": 1 - c}
    z_peer = {"zhi": 1 - h}
    x_devs = [{"x": up_x}, {"x": down_x}]

    t_me, t_peers = exchange_peers(n_grp)
    barrier = pltpu.get_barrier_semaphore()
    greet = [partner, z_peer] + x_devs + plane_devices(n_grp)
    for dev in greet:
        pl.semaphore_signal(barrier, inc=1, device_id=dev, device_id_type=MESH_ID)
    pl.semaphore_wait(barrier, len(greet))

    count = [0]

    def send(src_of, blk, dev):
        k = count[0]
        count[0] += 1
        copies = []
        for m in range(3):
            cp = pltpu.make_async_remote_copy(
                src_ref=src_of(m),
                dst_ref=outs[m].at[blk],
                send_sem=send_sem.at[m, k],
                recv_sem=recv_sem.at[m, blk],
                device_id=dev,
                device_id_type=MESH_ID,
            )
            cp.start()
            copies.append(cp)
        return copies

    def wait_in(blk):
        for m in range(3):
            pltpu.make_async_remote_copy(
                src_ref=ins[m].at[0],
                dst_ref=outs[m].at[blk],
                send_sem=send_sem.at[m, 0],
                recv_sem=recv_sem.at[m, blk],
                device_id=partner,
                device_id_type=MESH_ID,
            ).wait_recv()

    sent = []
    local = []
    for m in range(3):
        cp = pltpu.make_async_copy(ins[m].at[h], outs[m].at[me], local_sem.at[m])
        cp.start()
        local.append(cp)
    sent += send(lambda m: ins[m].at[1 - h], me, z_peer)
    for dev in [partner] + x_devs:
        sent += send(lambda m: ins[m].at[h], me, dev)

    z_blk = block(x, 1 - h, c)
    wait_in(z_blk)
    for dev in [partner] + x_devs:
        sent += send(lambda m: outs[m].at[z_blk], z_blk, dev)
    t_local, t_copies, t_k = start_plane(
        n_grp, t_in, t_out, stage, t_send, t_recv, stage_sem, local_sem.at[3]
    )
    t_copies += relay_plane(n_grp, t_k, t_in, t_out, stage, t_send, t_recv, stage_sem)

    for hh in (h, 1 - h):
        blk = block(away, hh, c)
        wait_in(blk)
        sent += send(lambda m: outs[m].at[blk], blk, partner)
        sent += send(lambda m: outs[m].at[blk], blk, {"x": toward})
    for xp in (toward, far_x):
        for hh in (h, 1 - h):
            blk = block(xp, hh, c)
            wait_in(blk)
            sent += send(lambda m: outs[m].at[blk], blk, partner)

    for xx in range(n_x):
        for hh in (0, 1):
            wait_in(block(xx, hh, 1 - c))

    for cp in sent:
        cp.wait_send()
    for cp in local:
        cp.wait()
    finish_exchange(t_peers, t_local, t_copies, t_in, t_out, t_send, t_recv)


def gather_weights(gate_weight, up_weight, down_weight, outgoing, n_x, n_grp):
    blk_rows, width = gate_weight.shape[1], gate_weight.shape[2]
    n_blocks = n_x * 4
    n_send = 16
    shape = jax.ShapeDtypeStruct((n_blocks, blk_rows, width), gate_weight.dtype)
    any_spec = pl.BlockSpec(memory_space=pl.ANY)
    nbytes = 3 * n_blocks * blk_rows * width * 2
    return pl.pallas_call(
        functools.partial(weight_kernel, n_x, n_grp),
        out_shape=(shape, shape, shape, jax.ShapeDtypeStruct(outgoing.shape, outgoing.dtype)),
        in_specs=[any_spec] * 4,
        out_specs=(any_spec, any_spec, any_spec, any_spec),
        scratch_shapes=[
            pltpu.SemaphoreType.DMA((3, n_send)),
            pltpu.SemaphoreType.DMA((3, n_blocks)),
            pltpu.SemaphoreType.DMA((4,)),
            pltpu.SemaphoreType.DMA((n_grp + 8,)),
            pltpu.SemaphoreType.DMA((n_grp,)),
            pltpu.VMEM((7,) + outgoing.shape[1:], outgoing.dtype),
            pltpu.SemaphoreType.DMA((7,)),
        ],
        compiler_params=pltpu.CompilerParams(collective_id=0, has_side_effects=True),
        cost_estimate=pl.CostEstimate(flops=0, transcendentals=0, bytes_accessed=nbytes),
    )(gate_weight, up_weight, down_weight, outgoing)


def per_device(tokens, expert_ids, combine, gate_weight, up_weight, down_weight):
    n_x = lax.axis_size("x")
    assert n_x == 4
    per_group = gate_weight.shape[0]
    groups = lax.axis_size("expert")
    n_expert = per_group * groups
    n_grp = groups * 2
    assert n_grp == 16
    tok_rows, top_k = expert_ids.shape
    model_width = tokens.shape[1]
    n_slot = n_expert * CAP

    flat_ids = expert_ids.reshape(-1)
    onehot = (flat_ids[:, None] == jnp.arange(n_expert, dtype=jnp.int32)[None, :]).astype(jnp.int32)
    earlier = jnp.cumsum(onehot, axis=0) - onehot
    rank_within = jnp.sum(earlier * onehot, axis=1)
    slot_index = (flat_ids * CAP + rank_within).reshape(tok_rows, top_k)
    hit = slot_index[None, :, :] == jnp.arange(n_slot, dtype=jnp.int32)[:, None, None]
    pick = jnp.any(hit, axis=2).astype(jnp.bfloat16)
    outgoing = jnp.dot(pick, tokens, preferred_element_type=jnp.float32).astype(jnp.bfloat16)
    outgoing = outgoing.reshape(n_expert, CAP, model_width)

    g_all, u_all, d_all, arrived = gather_weights(
        gate_weight, up_weight, down_weight, outgoing, n_x, n_grp
    )
    gate_full = g_all.reshape(-1, model_width)
    up_full = u_all.reshape(-1, model_width)
    down_full = d_all.reshape(-1, model_width)
    gate_pre = jnp.einsum("scd,fd->scf", arrived, gate_full, preferred_element_type=jnp.float32)
    up_pre = jnp.einsum("scd,fd->scf", arrived, up_full, preferred_element_type=jnp.float32)
    hidden = (jax.nn.silu(gate_pre) * up_pre).astype(jnp.bfloat16)
    returned = expert_return(hidden, down_full, n_grp, 1)
    returned = returned.reshape(n_slot, model_width)

    weight_of = jnp.sum(
        jnp.where(hit, combine[None, :, :], jnp.zeros_like(combine)[None, :, :]), axis=2
    ).T
    weight_top = lax.reduce_precision(weight_of, exponent_bits=8, mantissa_bits=7)
    weight_hi = weight_top.astype(jnp.bfloat16)
    weight_lo = (weight_of - weight_top).astype(jnp.bfloat16)
    mixed = jnp.dot(weight_hi, returned, preferred_element_type=jnp.float32) + jnp.dot(
        weight_lo, returned, preferred_element_type=jnp.float32
    )
    return mixed.astype(jnp.bfloat16)


def solution(mesh):
    groups = mesh.shape["expert"]
    n_x = mesh.shape["fsdp"] // 4
    inner = Mesh(mesh.devices.reshape(groups, n_x, 2, 2), ("expert", "x", "zhi", "core"))
    rows = P(("expert", "x", "zhi", "core"), None)
    weights = P("expert", ("x", "zhi", "core"), None)
    return jax.shard_map(
        per_device,
        mesh=inner,
        in_specs=(rows, rows, rows, weights, weights, weights),
        out_specs=rows,
        check_vma=False,
    )
```

```python
import functools

import jax
import jax.numpy as jnp
from jax import lax
from jax.experimental import pallas as pl
from jax.experimental.pallas import tpu as pltpu
from jax.sharding import Mesh
from jax.sharding import PartitionSpec as P

CAP = 72
MESH_ID = pl.DeviceIdType.MESH


def exchange_peers(n_grp):
    me = lax.axis_index("expert") * 2 + lax.axis_index("zhi")
    peers = []
    for s in range(1, n_grp):
        p = lax.rem(me + s, n_grp)
        peers.append((p, {"expert": p // 2, "zhi": lax.rem(p, 2)}))
    return me, peers


def start_exchange(me, peers, x_ref, y_ref, send_sem, recv_sem, local_sem):
    copies = []
    local = pltpu.make_async_copy(x_ref.at[me], y_ref.at[me], local_sem)
    local.start()
    for k, (p, dev) in enumerate(peers):
        cp = pltpu.make_async_remote_copy(
            src_ref=x_ref.at[p],
            dst_ref=y_ref.at[me],
            send_sem=send_sem.at[k],
            recv_sem=recv_sem.at[me],
            device_id=dev,
            device_id_type=MESH_ID,
        )
        cp.start()
        copies.append(cp)
    return local, copies


def finish_exchange(peers, local, copies, x_ref, y_ref, send_sem, recv_sem):
    for k, (p, dev) in enumerate(peers):
        pltpu.make_async_remote_copy(
            src_ref=x_ref.at[0],
            dst_ref=y_ref.at[p],
            send_sem=send_sem.at[k],
            recv_sem=recv_sem.at[p],
            device_id=dev,
            device_id_type=MESH_ID,
        ).wait_recv()
    for cp in copies:
        cp.wait_send()
    local.wait()


def plane_plan(n_grp):
    e_idx = lax.axis_index("expert")
    h = lax.axis_index("zhi")
    c = lax.axis_index("core")
    y = e_idx // 2
    z = h * 2 + lax.rem(e_idx, 2)
    s = 1 - 2 * c

    def at(dy, dz):
        yy = lax.rem(y + dy + 4, 4)
        zz = lax.rem(z + dz + 4, 4)
        p = (yy * 2 + lax.rem(zz, 2)) * 2 + zz // 2
        return p, {"expert": yy * 2 + lax.rem(zz, 2), "zhi": zz // 2}

    direct = [(dy, dz) for dy in (0, 1, 3) for dz in (0, 1, 3) if (dy, dz) != (0, 0)]
    relayed = [((2, dz), (s, 0)) for dz in (0, 1, 3)]
    relayed += [((dy, 2), (0, s)) for dy in (0, 1, 3)]
    relayed += [((2, 2), (s, s))]
    me = (y * 2 + lax.rem(z, 2)) * 2 + z // 2
    return me, at, direct, relayed


def start_plane(n_grp, x_ref, y_ref, stage, send_sem, recv_sem, stage_sem, local_sem):
    me, at, direct, relayed = plane_plan(n_grp)
    copies = []
    local = pltpu.make_async_copy(x_ref.at[me], y_ref.at[me], local_sem)
    local.start()
    k = 0
    for j, (off, rel) in enumerate(relayed):
        p, _ = at(*off)
        _, dev = at(*rel)
        cp = pltpu.make_async_remote_copy(
            src_ref=x_ref.at[p], dst_ref=stage.at[j], send_sem=send_sem.at[k],
            recv_sem=stage_sem.at[j], device_id=dev, device_id_type=MESH_ID,
        )
        cp.start()
        copies.append(cp)
        k += 1
    for off in direct:
        p, dev = at(*off)
        cp = pltpu.make_async_remote_copy(
            src_ref=x_ref.at[p], dst_ref=y_ref.at[me], send_sem=send_sem.at[k],
            recv_sem=recv_sem.at[me], device_id=dev, device_id_type=MESH_ID,
        )
        cp.start()
        copies.append(cp)
        k += 1
    return local, copies, k


def relay_plane(n_grp, k, x_ref, y_ref, stage, send_sem, recv_sem, stage_sem):
    me, at, direct, relayed = plane_plan(n_grp)
    copies = []
    for j, (off, rel) in enumerate(relayed):
        src_p, _ = at(-rel[0], -rel[1])
        _, dev = at(off[0] - rel[0], off[1] - rel[1])
        pltpu.make_async_remote_copy(
            src_ref=x_ref.at[0], dst_ref=stage.at[j], send_sem=send_sem.at[0],
            recv_sem=stage_sem.at[j], device_id=dev, device_id_type=MESH_ID,
        ).wait_recv()
        cp = pltpu.make_async_remote_copy(
            src_ref=stage.at[j], dst_ref=y_ref.at[src_p], send_sem=send_sem.at[k],
            recv_sem=recv_sem.at[src_p], device_id=dev, device_id_type=MESH_ID,
        )
        cp.start()
        copies.append(cp)
        k += 1
    return copies


def plane_devices(n_grp):
    me, at, direct, relayed = plane_plan(n_grp)
    return [at(*off)[1] for off in direct]


def exchange_kernel(n_grp, x_ref, y_ref, send_sem, recv_sem, local_sem):
    me, peers = exchange_peers(n_grp)
    barrier = pltpu.get_barrier_semaphore()
    for p, dev in peers:
        pl.semaphore_signal(barrier, inc=1, device_id=dev, device_id_type=MESH_ID)
    pl.semaphore_wait(barrier, len(peers))
    local, copies = start_exchange(me, peers, x_ref, y_ref, send_sem, recv_sem, local_sem.at[0])
    finish_exchange(peers, local, copies, x_ref, y_ref, send_sem, recv_sem)


def exchange(x, n_grp, collective_id):
    any_spec = pl.BlockSpec(memory_space=pl.ANY)
    return pl.pallas_call(
        functools.partial(exchange_kernel, n_grp),
        out_shape=jax.ShapeDtypeStruct(x.shape, x.dtype),
        in_specs=[any_spec],
        out_specs=any_spec,
        scratch_shapes=[
            pltpu.SemaphoreType.DMA((n_grp,)),
            pltpu.SemaphoreType.DMA((n_grp,)),
            pltpu.SemaphoreType.DMA((1,)),
        ],
        compiler_params=pltpu.CompilerParams(collective_id=collective_id, has_side_effects=True),
        cost_estimate=pl.CostEstimate(flops=0, transcendentals=0, bytes_accessed=2 * x.size * 2),
    )(x)


def expert_return_kernel(n_grp, hid_ref, down_ref, y_ref, buf, stage, send_sem, recv_sem, stage_sem,
                         local_sem):
    me, at, direct, relayed = plane_plan(n_grp)
    n_rel = len(relayed)
    order = [off for off, rel in relayed] + direct + [(0, 0)]
    rel_of = [rel for off, rel in relayed]
    barrier = pltpu.get_barrier_semaphore()
    peers = plane_devices(n_grp)
    for dev in peers:
        pl.semaphore_signal(barrier, inc=1, device_id=dev, device_id_type=MESH_ID)

    def pick(k, values):
        out = values[-1]
        for i in range(len(values) - 2, -1, -1):
            out = jnp.where(k == i, values[i], out)
        return out

    def chunk_of(k):
        dy = pick(k, [o[0] for o in order])
        dz = pick(k, [o[1] for o in order])
        return at(dy, dz)

    def project(k):
        p, _ = chunk_of(k)
        buf[p] = jnp.dot(hid_ref[p], down_ref[...], preferred_element_type=jnp.float32).astype(buf.dtype)

    def first_hop(k):
        p, _ = chunk_of(k)
        ry = pick(k, [r[0] for r in rel_of])
        rz = pick(k, [r[1] for r in rel_of])
        _, dev = at(ry, rz)
        return pltpu.make_async_remote_copy(
            src_ref=buf.at[p], dst_ref=stage.at[k], send_sem=send_sem.at[k],
            recv_sem=stage_sem.at[k], device_id=dev, device_id_type=MESH_ID,
        )

    def direct_send(k):
        p, dev = chunk_of(k)
        return pltpu.make_async_remote_copy(
            src_ref=buf.at[p], dst_ref=y_ref.at[me], send_sem=send_sem.at[k],
            recv_sem=recv_sem.at[me], device_id=dev, device_id_type=MESH_ID,
        )

    def forwards():
        for j, (off, rel) in enumerate(relayed):
            src_p, _ = at(-rel[0], -rel[1])
            _, dev = at(off[0] - rel[0], off[1] - rel[1])
            pltpu.make_async_remote_copy(
                src_ref=buf.at[0], dst_ref=stage.at[j], send_sem=send_sem.at[0],
                recv_sem=stage_sem.at[j], device_id=dev, device_id_type=MESH_ID,
            ).wait_recv()
            pltpu.make_async_remote_copy(
                src_ref=stage.at[j], dst_ref=y_ref.at[src_p], send_sem=send_sem.at[n_grp - 1 + j],
                recv_sem=recv_sem.at[src_p], device_id=dev, device_id_type=MESH_ID,
            ).start()

    local = pltpu.make_async_copy(buf.at[me], y_ref.at[me], local_sem.at[0])
    project(0)
    pl.semaphore_wait(barrier, len(peers))

    def step(k, carry):
        project(k)

        @pl.when(k - 1 < n_rel)
        def _():
            first_hop(k - 1).start()

        @pl.when(k - 1 >= n_rel)
        def _():
            direct_send(k - 1).start()

        @pl.when(k == n_rel + 4)
        def _():
            forwards()

        return carry

    lax.fori_loop(1, n_grp, step, 0)
    local.start()

    local.wait()
    for k in range(n_grp - 1):
        if k < n_rel:
            first_hop(k).wait_send()
        else:
            direct_send(k).wait_send()
    for j, (off, rel) in enumerate(relayed):
        _, dev = at(off[0] - rel[0], off[1] - rel[1])
        pltpu.make_async_remote_copy(
            src_ref=stage.at[j], dst_ref=y_ref.at[0], send_sem=send_sem.at[n_grp - 1 + j],
            recv_sem=recv_sem.at[0], device_id=dev, device_id_type=MESH_ID,
        ).wait_send()
    for s in range(1, n_grp):
        q = lax.rem(me + s, n_grp)
        pltpu.make_async_remote_copy(
            src_ref=buf.at[0], dst_ref=y_ref.at[q], send_sem=send_sem.at[0],
            recv_sem=recv_sem.at[q], device_id=peers[0], device_id_type=MESH_ID,
        ).wait_recv()


def expert_return(hidden, down_full, n_grp, collective_id):
    n_src, cap, ff = hidden.shape
    width = down_full.shape[1]
    out = jax.ShapeDtypeStruct((n_src, cap, width), jnp.bfloat16)
    vmem = pl.BlockSpec(memory_space=pltpu.VMEM)
    flops = 2 * n_src * cap * ff * width
    nbytes = hidden.size * 2 + down_full.size * 2 + 2 * n_src * cap * width * 2
    return pl.pallas_call(
        functools.partial(expert_return_kernel, n_grp),
        out_shape=out,
        in_specs=[vmem] * 2,
        out_specs=pl.BlockSpec(memory_space=pl.ANY),
        scratch_shapes=[
            pltpu.VMEM((n_src, cap, width), jnp.bfloat16),
            pltpu.VMEM((7, cap, width), jnp.bfloat16),
            pltpu.SemaphoreType.DMA((n_grp + 8,)),
            pltpu.SemaphoreType.DMA((n_grp,)),
            pltpu.SemaphoreType.DMA((7,)),
            pltpu.SemaphoreType.DMA((1,)),
        ],
        compiler_params=pltpu.CompilerParams(
            collective_id=collective_id, has_side_effects=True, vmem_limit_bytes=56 * 1024 * 1024
        ),
        cost_estimate=pl.CostEstimate(flops=flops, transcendentals=0, bytes_accessed=nbytes),
    )(hidden, down_full)


def weight_kernel(n_x, n_grp, g_in, u_in, d_in, t_in, g_out, u_out, d_out, t_out, send_sem, recv_sem,
                  local_sem, t_send, t_recv, stage, stage_sem):
    ins = (g_in, u_in, d_in)
    outs = (g_out, u_out, d_out)
    x = lax.axis_index("x")
    h = lax.axis_index("zhi")
    c = lax.axis_index("core")

    def block(xx, hh, cc):
        return (xx * 2 + hh) * 2 + cc

    me = block(x, h, c)
    up_x = lax.rem(x + 1, n_x)
    down_x = lax.rem(x + n_x - 1, n_x)
    far_x = lax.rem(x + 2, n_x)
    toward = jnp.where(c == 0, up_x, down_x)
    away = jnp.where(c == 0, down_x, up_x)
    partner = {"core": 1 - c}
    z_peer = {"zhi": 1 - h}
    x_devs = [{"x": up_x}, {"x": down_x}]

    t_me, t_peers = exchange_peers(n_grp)
    barrier = pltpu.get_barrier_semaphore()
    greet = [partner, z_peer] + x_devs + plane_devices(n_grp)
    for dev in greet:
        pl.semaphore_signal(barrier, inc=1, device_id=dev, device_id_type=MESH_ID)
    pl.semaphore_wait(barrier, len(greet))

    count = [0]

    def send(src_of, blk, dev):
        k = count[0]
        count[0] += 1
        copies = []
        for m in range(3):
            cp = pltpu.make_async_remote_copy(
                src_ref=src_of(m),
                dst_ref=outs[m].at[blk],
                send_sem=send_sem.at[m, k],
                recv_sem=recv_sem.at[m, blk],
                device_id=dev,
                device_id_type=MESH_ID,
            )
            cp.start()
            copies.append(cp)
        return copies

    def wait_in(blk):
        for m in range(3):
            pltpu.make_async_remote_copy(
                src_ref=ins[m].at[0],
                dst_ref=outs[m].at[blk],
                send_sem=send_sem.at[m, 0],
                recv_sem=recv_sem.at[m, blk],
                device_id=partner,
                device_id_type=MESH_ID,
            ).wait_recv()

    sent = []
    local = []
    for m in range(3):
        cp = pltpu.make_async_copy(ins[m].at[h], outs[m].at[me], local_sem.at[m])
        cp.start()
        local.append(cp)
    sent += send(lambda m: ins[m].at[1 - h], me, z_peer)
    for dev in [partner] + x_devs:
        sent += send(lambda m: ins[m].at[h], me, dev)

    z_blk = block(x, 1 - h, c)
    wait_in(z_blk)
    for dev in [partner] + x_devs:
        sent += send(lambda m: outs[m].at[z_blk], z_blk, dev)
    t_local, t_copies, t_k = start_plane(
        n_grp, t_in, t_out, stage, t_send, t_recv, stage_sem, local_sem.at[3]
    )

    for hh in (h, 1 - h):
        blk = block(away, hh, c)
        wait_in(blk)
        sent += send(lambda m: outs[m].at[blk], blk, partner)
        sent += send(lambda m: outs[m].at[blk], blk, {"x": toward})
    t_copies += relay_plane(n_grp, t_k, t_in, t_out, stage, t_send, t_recv, stage_sem)
    for xp in (toward, far_x):
        for hh in (h, 1 - h):
            blk = block(xp, hh, c)
            wait_in(blk)
            sent += send(lambda m: outs[m].at[blk], blk, partner)

    for xx in range(n_x):
        for hh in (0, 1):
            wait_in(block(xx, hh, 1 - c))

    for cp in sent:
        cp.wait_send()
    for cp in local:
        cp.wait()
    finish_exchange(t_peers, t_local, t_copies, t_in, t_out, t_send, t_recv)


def gather_weights(gate_weight, up_weight, down_weight, outgoing, n_x, n_grp):
    blk_rows, width = gate_weight.shape[1], gate_weight.shape[2]
    n_blocks = n_x * 4
    n_send = 16
    shape = jax.ShapeDtypeStruct((n_blocks, blk_rows, width), gate_weight.dtype)
    any_spec = pl.BlockSpec(memory_space=pl.ANY)
    nbytes = 3 * n_blocks * blk_rows * width * 2
    return pl.pallas_call(
        functools.partial(weight_kernel, n_x, n_grp),
        out_shape=(shape, shape, shape, jax.ShapeDtypeStruct(outgoing.shape, outgoing.dtype)),
        in_specs=[any_spec] * 4,
        out_specs=(any_spec, any_spec, any_spec, any_spec),
        scratch_shapes=[
            pltpu.SemaphoreType.DMA((3, n_send)),
            pltpu.SemaphoreType.DMA((3, n_blocks)),
            pltpu.SemaphoreType.DMA((4,)),
            pltpu.SemaphoreType.DMA((n_grp + 8,)),
            pltpu.SemaphoreType.DMA((n_grp,)),
            pltpu.VMEM((7,) + outgoing.shape[1:], outgoing.dtype),
            pltpu.SemaphoreType.DMA((7,)),
        ],
        compiler_params=pltpu.CompilerParams(collective_id=0, has_side_effects=True),
        cost_estimate=pl.CostEstimate(flops=0, transcendentals=0, bytes_accessed=nbytes),
    )(gate_weight, up_weight, down_weight, outgoing)


def per_device(tokens, expert_ids, combine, gate_weight, up_weight, down_weight):
    n_x = lax.axis_size("x")
    assert n_x == 4
    per_group = gate_weight.shape[0]
    groups = lax.axis_size("expert")
    n_expert = per_group * groups
    n_grp = groups * 2
    assert n_grp == 16
    tok_rows, top_k = expert_ids.shape
    model_width = tokens.shape[1]
    n_slot = n_expert * CAP

    flat_ids = expert_ids.reshape(-1)
    onehot = (flat_ids[:, None] == jnp.arange(n_expert, dtype=jnp.int32)[None, :]).astype(jnp.int32)
    earlier = jnp.cumsum(onehot, axis=0) - onehot
    rank_within = jnp.sum(earlier * onehot, axis=1)
    slot_index = (flat_ids * CAP + rank_within).reshape(tok_rows, top_k)
    hit = slot_index[None, :, :] == jnp.arange(n_slot, dtype=jnp.int32)[:, None, None]
    pick = jnp.any(hit, axis=2).astype(jnp.bfloat16)
    outgoing = jnp.dot(pick, tokens, preferred_element_type=jnp.float32).astype(jnp.bfloat16)
    outgoing = outgoing.reshape(n_expert, CAP, model_width)

    g_all, u_all, d_all, arrived = gather_weights(
        gate_weight, up_weight, down_weight, outgoing, n_x, n_grp
    )
    gate_full = g_all.reshape(-1, model_width)
    up_full = u_all.reshape(-1, model_width)
    down_full = d_all.reshape(-1, model_width)
    gate_pre = jnp.einsum("scd,fd->scf", arrived, gate_full, preferred_element_type=jnp.float32)
    up_pre = jnp.einsum("scd,fd->scf", arrived, up_full, preferred_element_type=jnp.float32)
    hidden = (jax.nn.silu(gate_pre) * up_pre).astype(jnp.bfloat16)
    returned = expert_return(hidden, down_full, n_grp, 1)
    returned = returned.reshape(n_slot, model_width)

    weight_of = jnp.sum(
        jnp.where(hit, combine[None, :, :], jnp.zeros_like(combine)[None, :, :]), axis=2
    ).T
    weight_top = lax.reduce_precision(weight_of, exponent_bits=8, mantissa_bits=7)
    weight_hi = weight_top.astype(jnp.bfloat16)
    weight_lo = (weight_of - weight_top).astype(jnp.bfloat16)
    mixed = jnp.dot(weight_hi, returned, preferred_element_type=jnp.float32) + jnp.dot(
        weight_lo, returned, preferred_element_type=jnp.float32
    )
    return mixed.astype(jnp.bfloat16)


def solution(mesh):
    groups = mesh.shape["expert"]
    n_x = mesh.shape["fsdp"] // 4
    inner = Mesh(mesh.devices.reshape(groups, n_x, 2, 2), ("expert", "x", "zhi", "core"))
    rows = P(("expert", "x", "zhi", "core"), None)
    weights = P("expert", ("x", "zhi", "core"), None)
    return jax.shard_map(
        per_device,
        mesh=inner,
        in_specs=(rows, rows, rows, weights, weights, weights),
        out_specs=rows,
        check_vma=False,
    )
```

```python
import functools

import jax
import jax.numpy as jnp
from jax import lax
from jax.experimental import pallas as pl
from jax.experimental.pallas import tpu as pltpu
from jax.sharding import Mesh
from jax.sharding import PartitionSpec as P

CAP = 72
MESH_ID = pl.DeviceIdType.MESH


def exchange_peers(n_grp):
    me = lax.axis_index("expert") * 2 + lax.axis_index("zhi")
    peers = []
    for s in range(1, n_grp):
        p = lax.rem(me + s, n_grp)
        peers.append((p, {"expert": p // 2, "zhi": lax.rem(p, 2)}))
    return me, peers


def start_exchange(me, peers, x_ref, y_ref, send_sem, recv_sem, local_sem):
    copies = []
    local = pltpu.make_async_copy(x_ref.at[me], y_ref.at[me], local_sem)
    local.start()
    for k, (p, dev) in enumerate(peers):
        cp = pltpu.make_async_remote_copy(
            src_ref=x_ref.at[p],
            dst_ref=y_ref.at[me],
            send_sem=send_sem.at[k],
            recv_sem=recv_sem.at[me],
            device_id=dev,
            device_id_type=MESH_ID,
        )
        cp.start()
        copies.append(cp)
    return local, copies


def finish_exchange(peers, local, copies, x_ref, y_ref, send_sem, recv_sem):
    for k, (p, dev) in enumerate(peers):
        pltpu.make_async_remote_copy(
            src_ref=x_ref.at[0],
            dst_ref=y_ref.at[p],
            send_sem=send_sem.at[k],
            recv_sem=recv_sem.at[p],
            device_id=dev,
            device_id_type=MESH_ID,
        ).wait_recv()
    for cp in copies:
        cp.wait_send()
    local.wait()


def plane_plan(n_grp):
    e_idx = lax.axis_index("expert")
    h = lax.axis_index("zhi")
    c = lax.axis_index("core")
    y = e_idx // 2
    z = h * 2 + lax.rem(e_idx, 2)
    s = 1 - 2 * c

    def at(dy, dz):
        yy = lax.rem(y + dy + 4, 4)
        zz = lax.rem(z + dz + 4, 4)
        p = (yy * 2 + lax.rem(zz, 2)) * 2 + zz // 2
        return p, {"expert": yy * 2 + lax.rem(zz, 2), "zhi": zz // 2}

    direct = [(dy, dz) for dy in (0, 1, 3) for dz in (0, 1, 3) if (dy, dz) != (0, 0)]
    relayed = [((2, dz), (s, 0)) for dz in (0, 1, 3)]
    relayed += [((dy, 2), (0, s)) for dy in (0, 1, 3)]
    relayed += [((2, 2), (s, s))]
    me = (y * 2 + lax.rem(z, 2)) * 2 + z // 2
    return me, at, direct, relayed


def start_plane(n_grp, x_ref, y_ref, stage, send_sem, recv_sem, stage_sem, local_sem):
    me, at, direct, relayed = plane_plan(n_grp)
    copies = []
    local = pltpu.make_async_copy(x_ref.at[me], y_ref.at[me], local_sem)
    local.start()
    k = 0
    for j, (off, rel) in enumerate(relayed):
        p, _ = at(*off)
        _, dev = at(*rel)
        cp = pltpu.make_async_remote_copy(
            src_ref=x_ref.at[p], dst_ref=stage.at[j], send_sem=send_sem.at[k],
            recv_sem=stage_sem.at[j], device_id=dev, device_id_type=MESH_ID,
        )
        cp.start()
        copies.append(cp)
        k += 1
    for off in direct:
        p, dev = at(*off)
        cp = pltpu.make_async_remote_copy(
            src_ref=x_ref.at[p], dst_ref=y_ref.at[me], send_sem=send_sem.at[k],
            recv_sem=recv_sem.at[me], device_id=dev, device_id_type=MESH_ID,
        )
        cp.start()
        copies.append(cp)
        k += 1
    return local, copies, k


def relay_plane(n_grp, k, x_ref, y_ref, stage, send_sem, recv_sem, stage_sem):
    me, at, direct, relayed = plane_plan(n_grp)
    copies = []
    for j, (off, rel) in enumerate(relayed):
        src_p, _ = at(-rel[0], -rel[1])
        _, dev = at(off[0] - rel[0], off[1] - rel[1])
        pltpu.make_async_remote_copy(
            src_ref=x_ref.at[0], dst_ref=stage.at[j], send_sem=send_sem.at[0],
            recv_sem=stage_sem.at[j], device_id=dev, device_id_type=MESH_ID,
        ).wait_recv()
        cp = pltpu.make_async_remote_copy(
            src_ref=stage.at[j], dst_ref=y_ref.at[src_p], send_sem=send_sem.at[k],
            recv_sem=recv_sem.at[src_p], device_id=dev, device_id_type=MESH_ID,
        )
        cp.start()
        copies.append(cp)
        k += 1
    return copies


def plane_devices(n_grp):
    me, at, direct, relayed = plane_plan(n_grp)
    return [at(*off)[1] for off in direct]


def exchange_kernel(n_grp, x_ref, y_ref, send_sem, recv_sem, local_sem):
    me, peers = exchange_peers(n_grp)
    barrier = pltpu.get_barrier_semaphore()
    for p, dev in peers:
        pl.semaphore_signal(barrier, inc=1, device_id=dev, device_id_type=MESH_ID)
    pl.semaphore_wait(barrier, len(peers))
    local, copies = start_exchange(me, peers, x_ref, y_ref, send_sem, recv_sem, local_sem.at[0])
    finish_exchange(peers, local, copies, x_ref, y_ref, send_sem, recv_sem)


def exchange(x, n_grp, collective_id):
    any_spec = pl.BlockSpec(memory_space=pl.ANY)
    return pl.pallas_call(
        functools.partial(exchange_kernel, n_grp),
        out_shape=jax.ShapeDtypeStruct(x.shape, x.dtype),
        in_specs=[any_spec],
        out_specs=any_spec,
        scratch_shapes=[
            pltpu.SemaphoreType.DMA((n_grp,)),
            pltpu.SemaphoreType.DMA((n_grp,)),
            pltpu.SemaphoreType.DMA((1,)),
        ],
        compiler_params=pltpu.CompilerParams(collective_id=collective_id, has_side_effects=True),
        cost_estimate=pl.CostEstimate(flops=0, transcendentals=0, bytes_accessed=2 * x.size * 2),
    )(x)


def expert_return_kernel(n_grp, hid_ref, down_ref, y_ref, buf, stage, send_sem, recv_sem, stage_sem,
                         local_sem):
    me, at, direct, relayed = plane_plan(n_grp)
    n_rel = len(relayed)
    order = [off for off, rel in relayed] + direct + [(0, 0)]
    rel_of = [rel for off, rel in relayed]
    barrier = pltpu.get_barrier_semaphore()
    peers = plane_devices(n_grp)
    for dev in peers:
        pl.semaphore_signal(barrier, inc=1, device_id=dev, device_id_type=MESH_ID)

    def pick(k, values):
        out = values[-1]
        for i in range(len(values) - 2, -1, -1):
            out = jnp.where(k == i, values[i], out)
        return out

    def chunk_of(k):
        dy = pick(k, [o[0] for o in order])
        dz = pick(k, [o[1] for o in order])
        return at(dy, dz)

    def project(k):
        p, _ = chunk_of(k)
        buf[p] = jnp.dot(hid_ref[p], down_ref[...], preferred_element_type=jnp.float32).astype(buf.dtype)

    def first_hop(k):
        p, _ = chunk_of(k)
        ry = pick(k, [r[0] for r in rel_of])
        rz = pick(k, [r[1] for r in rel_of])
        _, dev = at(ry, rz)
        return pltpu.make_async_remote_copy(
            src_ref=buf.at[p], dst_ref=stage.at[k], send_sem=send_sem.at[k],
            recv_sem=stage_sem.at[k], device_id=dev, device_id_type=MESH_ID,
        )

    def direct_send(k):
        p, dev = chunk_of(k)
        return pltpu.make_async_remote_copy(
            src_ref=buf.at[p], dst_ref=y_ref.at[me], send_sem=send_sem.at[k],
            recv_sem=recv_sem.at[me], device_id=dev, device_id_type=MESH_ID,
        )

    def forwards():
        for j, (off, rel) in enumerate(relayed):
            src_p, _ = at(-rel[0], -rel[1])
            _, dev = at(off[0] - rel[0], off[1] - rel[1])
            pltpu.make_async_remote_copy(
                src_ref=buf.at[0], dst_ref=stage.at[j], send_sem=send_sem.at[0],
                recv_sem=stage_sem.at[j], device_id=dev, device_id_type=MESH_ID,
            ).wait_recv()
            pltpu.make_async_remote_copy(
                src_ref=stage.at[j], dst_ref=y_ref.at[src_p], send_sem=send_sem.at[n_grp - 1 + j],
                recv_sem=recv_sem.at[src_p], device_id=dev, device_id_type=MESH_ID,
            ).start()

    local = pltpu.make_async_copy(buf.at[me], y_ref.at[me], local_sem.at[0])
    project(0)
    pl.semaphore_wait(barrier, len(peers))

    def step(k, carry):
        project(k)

        @pl.when(k - 1 < n_rel)
        def _():
            first_hop(k - 1).start()

        @pl.when(k - 1 >= n_rel)
        def _():
            direct_send(k - 1).start()

        @pl.when(k == n_rel + 2)
        def _():
            forwards()

        return carry

    lax.fori_loop(1, n_grp, step, 0)
    local.start()

    local.wait()
    for k in range(n_grp - 1):
        if k < n_rel:
            first_hop(k).wait_send()
        else:
            direct_send(k).wait_send()
    for j, (off, rel) in enumerate(relayed):
        _, dev = at(off[0] - rel[0], off[1] - rel[1])
        pltpu.make_async_remote_copy(
            src_ref=stage.at[j], dst_ref=y_ref.at[0], send_sem=send_sem.at[n_grp - 1 + j],
            recv_sem=recv_sem.at[0], device_id=dev, device_id_type=MESH_ID,
        ).wait_send()
    for s in range(1, n_grp):
        q = lax.rem(me + s, n_grp)
        pltpu.make_async_remote_copy(
            src_ref=buf.at[0], dst_ref=y_ref.at[q], send_sem=send_sem.at[0],
            recv_sem=recv_sem.at[q], device_id=peers[0], device_id_type=MESH_ID,
        ).wait_recv()


def expert_return(hidden, down_full, n_grp, collective_id):
    n_src, cap, ff = hidden.shape
    width = down_full.shape[1]
    out = jax.ShapeDtypeStruct((n_src, cap, width), jnp.bfloat16)
    vmem = pl.BlockSpec(memory_space=pltpu.VMEM)
    flops = 2 * n_src * cap * ff * width
    nbytes = hidden.size * 2 + down_full.size * 2 + 2 * n_src * cap * width * 2
    return pl.pallas_call(
        functools.partial(expert_return_kernel, n_grp),
        out_shape=out,
        in_specs=[vmem] * 2,
        out_specs=pl.BlockSpec(memory_space=pl.ANY),
        scratch_shapes=[
            pltpu.VMEM((n_src, cap, width), jnp.bfloat16),
            pltpu.VMEM((7, cap, width), jnp.bfloat16),
            pltpu.SemaphoreType.DMA((n_grp + 8,)),
            pltpu.SemaphoreType.DMA((n_grp,)),
            pltpu.SemaphoreType.DMA((7,)),
            pltpu.SemaphoreType.DMA((1,)),
        ],
        compiler_params=pltpu.CompilerParams(
            collective_id=collective_id, has_side_effects=True, vmem_limit_bytes=56 * 1024 * 1024
        ),
        cost_estimate=pl.CostEstimate(flops=flops, transcendentals=0, bytes_accessed=nbytes),
    )(hidden, down_full)


def weight_kernel(n_x, n_grp, g_in, u_in, d_in, t_in, g_out, u_out, d_out, t_out, send_sem, recv_sem,
                  local_sem, t_send, t_recv, stage, stage_sem):
    ins = (g_in, u_in, d_in)
    outs = (g_out, u_out, d_out)
    x = lax.axis_index("x")
    h = lax.axis_index("zhi")
    c = lax.axis_index("core")

    def block(xx, hh, cc):
        return (xx * 2 + hh) * 2 + cc

    me = block(x, h, c)
    up_x = lax.rem(x + 1, n_x)
    down_x = lax.rem(x + n_x - 1, n_x)
    far_x = lax.rem(x + 2, n_x)
    toward = jnp.where(c == 0, up_x, down_x)
    away = jnp.where(c == 0, down_x, up_x)
    partner = {"core": 1 - c}
    z_peer = {"zhi": 1 - h}
    x_devs = [{"x": up_x}, {"x": down_x}]

    t_me, t_peers = exchange_peers(n_grp)
    barrier = pltpu.get_barrier_semaphore()
    greet = [partner, z_peer] + x_devs + plane_devices(n_grp)
    for dev in greet:
        pl.semaphore_signal(barrier, inc=1, device_id=dev, device_id_type=MESH_ID)
    pl.semaphore_wait(barrier, len(greet))

    count = [0]

    def send(src_of, blk, dev):
        k = count[0]
        count[0] += 1
        copies = []
        for m in range(3):
            cp = pltpu.make_async_remote_copy(
                src_ref=src_of(m),
                dst_ref=outs[m].at[blk],
                send_sem=send_sem.at[m, k],
                recv_sem=recv_sem.at[m, blk],
                device_id=dev,
                device_id_type=MESH_ID,
            )
            cp.start()
            copies.append(cp)
        return copies

    def wait_in(blk):
        for m in range(3):
            pltpu.make_async_remote_copy(
                src_ref=ins[m].at[0],
                dst_ref=outs[m].at[blk],
                send_sem=send_sem.at[m, 0],
                recv_sem=recv_sem.at[m, blk],
                device_id=partner,
                device_id_type=MESH_ID,
            ).wait_recv()

    sent = []
    local = []
    for m in range(3):
        cp = pltpu.make_async_copy(ins[m].at[h], outs[m].at[me], local_sem.at[m])
        cp.start()
        local.append(cp)
    sent += send(lambda m: ins[m].at[1 - h], me, z_peer)
    for dev in [partner] + x_devs:
        sent += send(lambda m: ins[m].at[h], me, dev)

    z_blk = block(x, 1 - h, c)
    wait_in(z_blk)
    for dev in [partner] + x_devs:
        sent += send(lambda m: outs[m].at[z_blk], z_blk, dev)
    t_local, t_copies, t_k = start_plane(
        n_grp, t_in, t_out, stage, t_send, t_recv, stage_sem, local_sem.at[3]
    )
    t_copies += relay_plane(n_grp, t_k, t_in, t_out, stage, t_send, t_recv, stage_sem)

    for hh in (h, 1 - h):
        blk = block(away, hh, c)
        wait_in(blk)
        sent += send(lambda m: outs[m].at[blk], blk, partner)
        sent += send(lambda m: outs[m].at[blk], blk, {"x": toward})
    for xp in (toward, far_x):
        for hh in (h, 1 - h):
            blk = block(xp, hh, c)
            wait_in(blk)
            sent += send(lambda m: outs[m].at[blk], blk, partner)

    for xx in range(n_x):
        for hh in (0, 1):
            wait_in(block(xx, hh, 1 - c))

    for cp in sent:
        cp.wait_send()
    for cp in local:
        cp.wait()
    finish_exchange(t_peers, t_local, t_copies, t_in, t_out, t_send, t_recv)


def gather_weights(gate_weight, up_weight, down_weight, outgoing, n_x, n_grp):
    blk_rows, width = gate_weight.shape[1], gate_weight.shape[2]
    n_blocks = n_x * 4
    n_send = 16
    shape = jax.ShapeDtypeStruct((n_blocks, blk_rows, width), gate_weight.dtype)
    any_spec = pl.BlockSpec(memory_space=pl.ANY)
    nbytes = 3 * n_blocks * blk_rows * width * 2
    return pl.pallas_call(
        functools.partial(weight_kernel, n_x, n_grp),
        out_shape=(shape, shape, shape, jax.ShapeDtypeStruct(outgoing.shape, outgoing.dtype)),
        in_specs=[any_spec] * 4,
        out_specs=(any_spec, any_spec, any_spec, any_spec),
        scratch_shapes=[
            pltpu.SemaphoreType.DMA((3, n_send)),
            pltpu.SemaphoreType.DMA((3, n_blocks)),
            pltpu.SemaphoreType.DMA((4,)),
            pltpu.SemaphoreType.DMA((n_grp + 8,)),
            pltpu.SemaphoreType.DMA((n_grp,)),
            pltpu.VMEM((7,) + outgoing.shape[1:], outgoing.dtype),
            pltpu.SemaphoreType.DMA((7,)),
        ],
        compiler_params=pltpu.CompilerParams(collective_id=0, has_side_effects=True),
        cost_estimate=pl.CostEstimate(flops=0, transcendentals=0, bytes_accessed=nbytes),
    )(gate_weight, up_weight, down_weight, outgoing)


def per_device(tokens, expert_ids, combine, gate_weight, up_weight, down_weight):
    n_x = lax.axis_size("x")
    assert n_x == 4
    per_group = gate_weight.shape[0]
    groups = lax.axis_size("expert")
    n_expert = per_group * groups
    n_grp = groups * 2
    assert n_grp == 16
    tok_rows, top_k = expert_ids.shape
    model_width = tokens.shape[1]
    n_slot = n_expert * CAP

    flat_ids = expert_ids.reshape(-1)
    onehot = (flat_ids[:, None] == jnp.arange(n_expert, dtype=jnp.int32)[None, :]).astype(jnp.int32)
    earlier = jnp.cumsum(onehot, axis=0) - onehot
    rank_within = jnp.sum(earlier * onehot, axis=1)
    slot_index = (flat_ids * CAP + rank_within).reshape(tok_rows, top_k)
    hit = slot_index[None, :, :] == jnp.arange(n_slot, dtype=jnp.int32)[:, None, None]
    pick = jnp.any(hit, axis=2).astype(jnp.bfloat16)
    outgoing = jnp.dot(pick, tokens, preferred_element_type=jnp.float32).astype(jnp.bfloat16)
    outgoing = outgoing.reshape(n_expert, CAP, model_width)

    g_all, u_all, d_all, arrived = gather_weights(
        gate_weight, up_weight, down_weight, outgoing, n_x, n_grp
    )
    gate_full = g_all.reshape(-1, model_width)
    up_full = u_all.reshape(-1, model_width)
    down_full = d_all.reshape(-1, model_width)
    gate_pre = jnp.einsum("scd,fd->scf", arrived, gate_full, preferred_element_type=jnp.float32)
    up_pre = jnp.einsum("scd,fd->scf", arrived, up_full, preferred_element_type=jnp.float32)
    hidden = (jax.nn.silu(gate_pre) * up_pre).astype(jnp.bfloat16)
    returned = expert_return(hidden, down_full, n_grp, 1)
    returned = returned.reshape(n_slot, model_width)

    weight_of = jnp.sum(
        jnp.where(hit, combine[None, :, :], jnp.zeros_like(combine)[None, :, :]), axis=2
    ).T
    weight_top = lax.reduce_precision(weight_of, exponent_bits=8, mantissa_bits=7)
    weight_hi = weight_top.astype(jnp.bfloat16)
    weight_lo = (weight_of - weight_top).astype(jnp.bfloat16)
    mixed = jnp.dot(weight_hi, returned, preferred_element_type=jnp.float32) + jnp.dot(
        weight_lo, returned, preferred_element_type=jnp.float32
    )
    return mixed.astype(jnp.bfloat16)


def solution(mesh):
    groups = mesh.shape["expert"]
    n_x = mesh.shape["fsdp"] // 4
    inner = Mesh(mesh.devices.reshape(groups, n_x, 2, 2), ("expert", "x", "zhi", "core"))
    rows = P(("expert", "x", "zhi", "core"), None)
    weights = P("expert", ("x", "zhi", "core"), None)
    return jax.shard_map(
        per_device,
        mesh=inner,
        in_specs=(rows, rows, rows, weights, weights, weights),
        out_specs=rows,
        check_vma=False,
    )
```

```python
import functools

import jax
import jax.numpy as jnp
from jax import lax
from jax.experimental import pallas as pl
from jax.experimental.pallas import tpu as pltpu
from jax.sharding import Mesh
from jax.sharding import PartitionSpec as P

CAP = 72
MESH_ID = pl.DeviceIdType.MESH


def exchange_peers(n_grp):
    me = lax.axis_index("expert") * 2 + lax.axis_index("zhi")
    peers = []
    for s in range(1, n_grp):
        p = lax.rem(me + s, n_grp)
        peers.append((p, {"expert": p // 2, "zhi": lax.rem(p, 2)}))
    return me, peers


def start_exchange(me, peers, x_ref, y_ref, send_sem, recv_sem, local_sem):
    copies = []
    local = pltpu.make_async_copy(x_ref.at[me], y_ref.at[me], local_sem)
    local.start()
    for k, (p, dev) in enumerate(peers):
        cp = pltpu.make_async_remote_copy(
            src_ref=x_ref.at[p],
            dst_ref=y_ref.at[me],
            send_sem=send_sem.at[k],
            recv_sem=recv_sem.at[me],
            device_id=dev,
            device_id_type=MESH_ID,
        )
        cp.start()
        copies.append(cp)
    return local, copies


def finish_exchange(peers, local, copies, x_ref, y_ref, send_sem, recv_sem):
    for k, (p, dev) in enumerate(peers):
        pltpu.make_async_remote_copy(
            src_ref=x_ref.at[0],
            dst_ref=y_ref.at[p],
            send_sem=send_sem.at[k],
            recv_sem=recv_sem.at[p],
            device_id=dev,
            device_id_type=MESH_ID,
        ).wait_recv()
    for cp in copies:
        cp.wait_send()
    local.wait()


def plane_plan(n_grp):
    e_idx = lax.axis_index("expert")
    h = lax.axis_index("zhi")
    c = lax.axis_index("core")
    y = e_idx // 2
    z = h * 2 + lax.rem(e_idx, 2)
    s = 1 - 2 * c

    def at(dy, dz):
        yy = lax.rem(y + dy + 4, 4)
        zz = lax.rem(z + dz + 4, 4)
        p = (yy * 2 + lax.rem(zz, 2)) * 2 + zz // 2
        return p, {"expert": yy * 2 + lax.rem(zz, 2), "zhi": zz // 2}

    direct = [(dy, dz) for dy in (0, 1, 3) for dz in (0, 1, 3) if (dy, dz) != (0, 0)]
    relayed = [((2, dz), (s, 0)) for dz in (0, 1, 3)]
    relayed += [((dy, 2), (0, s)) for dy in (0, 1, 3)]
    relayed += [((2, 2), (s, s))]
    me = (y * 2 + lax.rem(z, 2)) * 2 + z // 2
    return me, at, direct, relayed


def start_plane(n_grp, x_ref, y_ref, stage, send_sem, recv_sem, stage_sem, local_sem, part, k=0):
    me, at, direct, relayed = plane_plan(n_grp)
    copies = []
    if part == "relayed":
        direct = []
    else:
        relayed = []
    for j, (off, rel) in enumerate(relayed):
        p, _ = at(*off)
        _, dev = at(*rel)
        cp = pltpu.make_async_remote_copy(
            src_ref=x_ref.at[p], dst_ref=stage.at[j], send_sem=send_sem.at[k],
            recv_sem=stage_sem.at[j], device_id=dev, device_id_type=MESH_ID,
        )
        cp.start()
        copies.append(cp)
        k += 1
    for off in direct:
        p, dev = at(*off)
        cp = pltpu.make_async_remote_copy(
            src_ref=x_ref.at[p], dst_ref=y_ref.at[me], send_sem=send_sem.at[k],
            recv_sem=recv_sem.at[me], device_id=dev, device_id_type=MESH_ID,
        )
        cp.start()
        copies.append(cp)
        k += 1
    if part == "relayed":
        return copies, k
    local = pltpu.make_async_copy(x_ref.at[me], y_ref.at[me], local_sem)
    local.start()
    return local, copies, k


def relay_plane(n_grp, k, x_ref, y_ref, stage, send_sem, recv_sem, stage_sem):
    me, at, direct, relayed = plane_plan(n_grp)
    copies = []
    for j, (off, rel) in enumerate(relayed):
        src_p, _ = at(-rel[0], -rel[1])
        _, dev = at(off[0] - rel[0], off[1] - rel[1])
        pltpu.make_async_remote_copy(
            src_ref=x_ref.at[0], dst_ref=stage.at[j], send_sem=send_sem.at[0],
            recv_sem=stage_sem.at[j], device_id=dev, device_id_type=MESH_ID,
        ).wait_recv()
        cp = pltpu.make_async_remote_copy(
            src_ref=stage.at[j], dst_ref=y_ref.at[src_p], send_sem=send_sem.at[k],
            recv_sem=recv_sem.at[src_p], device_id=dev, device_id_type=MESH_ID,
        )
        cp.start()
        copies.append(cp)
        k += 1
    return copies


def plane_devices(n_grp):
    me, at, direct, relayed = plane_plan(n_grp)
    return [at(*off)[1] for off in direct]


def exchange_kernel(n_grp, x_ref, y_ref, send_sem, recv_sem, local_sem):
    me, peers = exchange_peers(n_grp)
    barrier = pltpu.get_barrier_semaphore()
    for p, dev in peers:
        pl.semaphore_signal(barrier, inc=1, device_id=dev, device_id_type=MESH_ID)
    pl.semaphore_wait(barrier, len(peers))
    local, copies = start_exchange(me, peers, x_ref, y_ref, send_sem, recv_sem, local_sem.at[0])
    finish_exchange(peers, local, copies, x_ref, y_ref, send_sem, recv_sem)


def exchange(x, n_grp, collective_id):
    any_spec = pl.BlockSpec(memory_space=pl.ANY)
    return pl.pallas_call(
        functools.partial(exchange_kernel, n_grp),
        out_shape=jax.ShapeDtypeStruct(x.shape, x.dtype),
        in_specs=[any_spec],
        out_specs=any_spec,
        scratch_shapes=[
            pltpu.SemaphoreType.DMA((n_grp,)),
            pltpu.SemaphoreType.DMA((n_grp,)),
            pltpu.SemaphoreType.DMA((1,)),
        ],
        compiler_params=pltpu.CompilerParams(collective_id=collective_id, has_side_effects=True),
        cost_estimate=pl.CostEstimate(flops=0, transcendentals=0, bytes_accessed=2 * x.size * 2),
    )(x)


def expert_return_kernel(n_grp, hid_ref, down_ref, y_ref, buf, stage, send_sem, recv_sem, stage_sem,
                         local_sem):
    me, at, direct, relayed = plane_plan(n_grp)
    n_rel = len(relayed)
    order = [off for off, rel in relayed] + direct + [(0, 0)]
    rel_of = [rel for off, rel in relayed]
    barrier = pltpu.get_barrier_semaphore()
    peers = plane_devices(n_grp)
    for dev in peers:
        pl.semaphore_signal(barrier, inc=1, device_id=dev, device_id_type=MESH_ID)

    def pick(k, values):
        out = values[-1]
        for i in range(len(values) - 2, -1, -1):
            out = jnp.where(k == i, values[i], out)
        return out

    def chunk_of(k):
        dy = pick(k, [o[0] for o in order])
        dz = pick(k, [o[1] for o in order])
        return at(dy, dz)

    def project(k):
        p, _ = chunk_of(k)
        buf[p] = jnp.dot(hid_ref[p], down_ref[...], preferred_element_type=jnp.float32).astype(buf.dtype)

    def first_hop(k):
        p, _ = chunk_of(k)
        ry = pick(k, [r[0] for r in rel_of])
        rz = pick(k, [r[1] for r in rel_of])
        _, dev = at(ry, rz)
        return pltpu.make_async_remote_copy(
            src_ref=buf.at[p], dst_ref=stage.at[k], send_sem=send_sem.at[k],
            recv_sem=stage_sem.at[k], device_id=dev, device_id_type=MESH_ID,
        )

    def direct_send(k):
        p, dev = chunk_of(k)
        return pltpu.make_async_remote_copy(
            src_ref=buf.at[p], dst_ref=y_ref.at[me], send_sem=send_sem.at[k],
            recv_sem=recv_sem.at[me], device_id=dev, device_id_type=MESH_ID,
        )

    def forwards():
        for j, (off, rel) in enumerate(relayed):
            src_p, _ = at(-rel[0], -rel[1])
            _, dev = at(off[0] - rel[0], off[1] - rel[1])
            pltpu.make_async_remote_copy(
                src_ref=buf.at[0], dst_ref=stage.at[j], send_sem=send_sem.at[0],
                recv_sem=stage_sem.at[j], device_id=dev, device_id_type=MESH_ID,
            ).wait_recv()
            pltpu.make_async_remote_copy(
                src_ref=stage.at[j], dst_ref=y_ref.at[src_p], send_sem=send_sem.at[n_grp - 1 + j],
                recv_sem=recv_sem.at[src_p], device_id=dev, device_id_type=MESH_ID,
            ).start()

    local = pltpu.make_async_copy(buf.at[me], y_ref.at[me], local_sem.at[0])
    project(0)
    pl.semaphore_wait(barrier, len(peers))

    def step(k, carry):
        project(k)

        @pl.when(k - 1 < n_rel)
        def _():
            first_hop(k - 1).start()

        @pl.when(k - 1 >= n_rel)
        def _():
            direct_send(k - 1).start()

        @pl.when(k == n_rel + 4)
        def _():
            forwards()

        return carry

    lax.fori_loop(1, n_grp, step, 0)
    local.start()

    local.wait()
    for k in range(n_grp - 1):
        if k < n_rel:
            first_hop(k).wait_send()
        else:
            direct_send(k).wait_send()
    for j, (off, rel) in enumerate(relayed):
        _, dev = at(off[0] - rel[0], off[1] - rel[1])
        pltpu.make_async_remote_copy(
            src_ref=stage.at[j], dst_ref=y_ref.at[0], send_sem=send_sem.at[n_grp - 1 + j],
            recv_sem=recv_sem.at[0], device_id=dev, device_id_type=MESH_ID,
        ).wait_send()
    for s in range(1, n_grp):
        q = lax.rem(me + s, n_grp)
        pltpu.make_async_remote_copy(
            src_ref=buf.at[0], dst_ref=y_ref.at[q], send_sem=send_sem.at[0],
            recv_sem=recv_sem.at[q], device_id=peers[0], device_id_type=MESH_ID,
        ).wait_recv()


def expert_return(hidden, down_full, n_grp, collective_id):
    n_src, cap, ff = hidden.shape
    width = down_full.shape[1]
    out = jax.ShapeDtypeStruct((n_src, cap, width), jnp.bfloat16)
    vmem = pl.BlockSpec(memory_space=pltpu.VMEM)
    flops = 2 * n_src * cap * ff * width
    nbytes = hidden.size * 2 + down_full.size * 2 + 2 * n_src * cap * width * 2
    return pl.pallas_call(
        functools.partial(expert_return_kernel, n_grp),
        out_shape=out,
        in_specs=[vmem] * 2,
        out_specs=pl.BlockSpec(memory_space=pl.ANY),
        scratch_shapes=[
            pltpu.VMEM((n_src, cap, width), jnp.bfloat16),
            pltpu.VMEM((7, cap, width), jnp.bfloat16),
            pltpu.SemaphoreType.DMA((n_grp + 8,)),
            pltpu.SemaphoreType.DMA((n_grp,)),
            pltpu.SemaphoreType.DMA((7,)),
            pltpu.SemaphoreType.DMA((1,)),
        ],
        compiler_params=pltpu.CompilerParams(
            collective_id=collective_id, has_side_effects=True, vmem_limit_bytes=56 * 1024 * 1024
        ),
        cost_estimate=pl.CostEstimate(flops=flops, transcendentals=0, bytes_accessed=nbytes),
    )(hidden, down_full)


def weight_kernel(n_x, n_grp, g_in, u_in, d_in, t_in, g_out, u_out, d_out, t_out, send_sem, recv_sem,
                  local_sem, t_send, t_recv, stage, stage_sem):
    ins = (g_in, u_in, d_in)
    outs = (g_out, u_out, d_out)
    x = lax.axis_index("x")
    h = lax.axis_index("zhi")
    c = lax.axis_index("core")

    def block(xx, hh, cc):
        return (xx * 2 + hh) * 2 + cc

    me = block(x, h, c)
    up_x = lax.rem(x + 1, n_x)
    down_x = lax.rem(x + n_x - 1, n_x)
    far_x = lax.rem(x + 2, n_x)
    toward = jnp.where(c == 0, up_x, down_x)
    away = jnp.where(c == 0, down_x, up_x)
    partner = {"core": 1 - c}
    z_peer = {"zhi": 1 - h}
    x_devs = [{"x": up_x}, {"x": down_x}]

    t_me, t_peers = exchange_peers(n_grp)
    barrier = pltpu.get_barrier_semaphore()
    greet = [partner, z_peer] + x_devs + plane_devices(n_grp)
    for dev in greet:
        pl.semaphore_signal(barrier, inc=1, device_id=dev, device_id_type=MESH_ID)
    pl.semaphore_wait(barrier, len(greet))

    count = [0]

    def send(src_of, blk, dev):
        k = count[0]
        count[0] += 1
        copies = []
        for m in range(3):
            cp = pltpu.make_async_remote_copy(
                src_ref=src_of(m),
                dst_ref=outs[m].at[blk],
                send_sem=send_sem.at[m, k],
                recv_sem=recv_sem.at[m, blk],
                device_id=dev,
                device_id_type=MESH_ID,
            )
            cp.start()
            copies.append(cp)
        return copies

    def wait_in(blk):
        for m in range(3):
            pltpu.make_async_remote_copy(
                src_ref=ins[m].at[0],
                dst_ref=outs[m].at[blk],
                send_sem=send_sem.at[m, 0],
                recv_sem=recv_sem.at[m, blk],
                device_id=partner,
                device_id_type=MESH_ID,
            ).wait_recv()

    sent = []
    local = []
    for m in range(3):
        cp = pltpu.make_async_copy(ins[m].at[h], outs[m].at[me], local_sem.at[m])
        cp.start()
        local.append(cp)
    sent += send(lambda m: ins[m].at[1 - h], me, z_peer)
    for dev in [partner] + x_devs:
        sent += send(lambda m: ins[m].at[h], me, dev)
    t_local, t_copies, t_k = start_plane(
        n_grp, t_in, t_out, stage, t_send, t_recv, stage_sem, local_sem.at[3], "direct"
    )

    z_blk = block(x, 1 - h, c)
    wait_in(z_blk)
    for dev in [partner] + x_devs:
        sent += send(lambda m: outs[m].at[z_blk], z_blk, dev)
    more, t_k = start_plane(
        n_grp, t_in, t_out, stage, t_send, t_recv, stage_sem, local_sem.at[3], "relayed", t_k
    )
    t_copies += more
    t_copies += relay_plane(n_grp, t_k, t_in, t_out, stage, t_send, t_recv, stage_sem)

    for hh in (h, 1 - h):
        blk = block(away, hh, c)
        wait_in(blk)
        sent += send(lambda m: outs[m].at[blk], blk, partner)
        sent += send(lambda m: outs[m].at[blk], blk, {"x": toward})
    for xp in (toward, far_x):
        for hh in (h, 1 - h):
            blk = block(xp, hh, c)
            wait_in(blk)
            sent += send(lambda m: outs[m].at[blk], blk, partner)

    for xx in range(n_x):
        for hh in (0, 1):
            wait_in(block(xx, hh, 1 - c))

    for cp in sent:
        cp.wait_send()
    for cp in local:
        cp.wait()
    finish_exchange(t_peers, t_local, t_copies, t_in, t_out, t_send, t_recv)


def gather_weights(gate_weight, up_weight, down_weight, outgoing, n_x, n_grp):
    blk_rows, width = gate_weight.shape[1], gate_weight.shape[2]
    n_blocks = n_x * 4
    n_send = 16
    shape = jax.ShapeDtypeStruct((n_blocks, blk_rows, width), gate_weight.dtype)
    any_spec = pl.BlockSpec(memory_space=pl.ANY)
    nbytes = 3 * n_blocks * blk_rows * width * 2
    return pl.pallas_call(
        functools.partial(weight_kernel, n_x, n_grp),
        out_shape=(shape, shape, shape, jax.ShapeDtypeStruct(outgoing.shape, outgoing.dtype)),
        in_specs=[any_spec] * 4,
        out_specs=(any_spec, any_spec, any_spec, any_spec),
        scratch_shapes=[
            pltpu.SemaphoreType.DMA((3, n_send)),
            pltpu.SemaphoreType.DMA((3, n_blocks)),
            pltpu.SemaphoreType.DMA((4,)),
            pltpu.SemaphoreType.DMA((n_grp + 8,)),
            pltpu.SemaphoreType.DMA((n_grp,)),
            pltpu.VMEM((7,) + outgoing.shape[1:], outgoing.dtype),
            pltpu.SemaphoreType.DMA((7,)),
        ],
        compiler_params=pltpu.CompilerParams(collective_id=0, has_side_effects=True),
        cost_estimate=pl.CostEstimate(flops=0, transcendentals=0, bytes_accessed=nbytes),
    )(gate_weight, up_weight, down_weight, outgoing)


def per_device(tokens, expert_ids, combine, gate_weight, up_weight, down_weight):
    n_x = lax.axis_size("x")
    assert n_x == 4
    per_group = gate_weight.shape[0]
    groups = lax.axis_size("expert")
    n_expert = per_group * groups
    n_grp = groups * 2
    assert n_grp == 16
    tok_rows, top_k = expert_ids.shape
    model_width = tokens.shape[1]
    n_slot = n_expert * CAP

    flat_ids = expert_ids.reshape(-1)
    onehot = (flat_ids[:, None] == jnp.arange(n_expert, dtype=jnp.int32)[None, :]).astype(jnp.int32)
    earlier = jnp.cumsum(onehot, axis=0) - onehot
    rank_within = jnp.sum(earlier * onehot, axis=1)
    slot_index = (flat_ids * CAP + rank_within).reshape(tok_rows, top_k)
    hit = slot_index[None, :, :] == jnp.arange(n_slot, dtype=jnp.int32)[:, None, None]
    pick = jnp.any(hit, axis=2).astype(jnp.bfloat16)
    outgoing = jnp.dot(pick, tokens, preferred_element_type=jnp.float32).astype(jnp.bfloat16)
    outgoing = outgoing.reshape(n_expert, CAP, model_width)

    g_all, u_all, d_all, arrived = gather_weights(
        gate_weight, up_weight, down_weight, outgoing, n_x, n_grp
    )
    gate_full = g_all.reshape(-1, model_width)
    up_full = u_all.reshape(-1, model_width)
    down_full = d_all.reshape(-1, model_width)
    gate_pre = jnp.einsum("scd,fd->scf", arrived, gate_full, preferred_element_type=jnp.float32)
    up_pre = jnp.einsum("scd,fd->scf", arrived, up_full, preferred_element_type=jnp.float32)
    hidden = (jax.nn.silu(gate_pre) * up_pre).astype(jnp.bfloat16)
    returned = expert_return(hidden, down_full, n_grp, 1)
    returned = returned.reshape(n_slot, model_width)

    weight_of = jnp.sum(
        jnp.where(hit, combine[None, :, :], jnp.zeros_like(combine)[None, :, :]), axis=2
    ).T
    weight_top = lax.reduce_precision(weight_of, exponent_bits=8, mantissa_bits=7)
    weight_hi = weight_top.astype(jnp.bfloat16)
    weight_lo = (weight_of - weight_top).astype(jnp.bfloat16)
    mixed = jnp.dot(weight_hi, returned, preferred_element_type=jnp.float32) + jnp.dot(
        weight_lo, returned, preferred_element_type=jnp.float32
    )
    return mixed.astype(jnp.bfloat16)


def solution(mesh):
    groups = mesh.shape["expert"]
    n_x = mesh.shape["fsdp"] // 4
    inner = Mesh(mesh.devices.reshape(groups, n_x, 2, 2), ("expert", "x", "zhi", "core"))
    rows = P(("expert", "x", "zhi", "core"), None)
    weights = P("expert", ("x", "zhi", "core"), None)
    return jax.shard_map(
        per_device,
        mesh=inner,
        in_specs=(rows, rows, rows, weights, weights, weights),
        out_specs=rows,
        check_vma=False,
    )
```

```python
import functools

import jax
import jax.numpy as jnp
from jax import lax
from jax.experimental import pallas as pl
from jax.experimental.pallas import tpu as pltpu
from jax.sharding import Mesh
from jax.sharding import PartitionSpec as P

CAP = 72
MESH_ID = pl.DeviceIdType.MESH


def exchange_peers(n_grp):
    me = lax.axis_index("expert") * 2 + lax.axis_index("zhi")
    peers = []
    for s in range(1, n_grp):
        p = lax.rem(me + s, n_grp)
        peers.append((p, {"expert": p // 2, "zhi": lax.rem(p, 2)}))
    return me, peers


def start_exchange(me, peers, x_ref, y_ref, send_sem, recv_sem, local_sem):
    copies = []
    local = pltpu.make_async_copy(x_ref.at[me], y_ref.at[me], local_sem)
    local.start()
    for k, (p, dev) in enumerate(peers):
        cp = pltpu.make_async_remote_copy(
            src_ref=x_ref.at[p],
            dst_ref=y_ref.at[me],
            send_sem=send_sem.at[k],
            recv_sem=recv_sem.at[me],
            device_id=dev,
            device_id_type=MESH_ID,
        )
        cp.start()
        copies.append(cp)
    return local, copies


def finish_exchange(peers, local, copies, x_ref, y_ref, send_sem, recv_sem):
    for k, (p, dev) in enumerate(peers):
        pltpu.make_async_remote_copy(
            src_ref=x_ref.at[0],
            dst_ref=y_ref.at[p],
            send_sem=send_sem.at[k],
            recv_sem=recv_sem.at[p],
            device_id=dev,
            device_id_type=MESH_ID,
        ).wait_recv()
    for cp in copies:
        cp.wait_send()
    local.wait()


def plane_plan(n_grp):
    e_idx = lax.axis_index("expert")
    h = lax.axis_index("zhi")
    c = lax.axis_index("core")
    y = e_idx // 2
    z = h * 2 + lax.rem(e_idx, 2)
    s = 1 - 2 * c

    def at(dy, dz):
        yy = lax.rem(y + dy + 4, 4)
        zz = lax.rem(z + dz + 4, 4)
        p = (yy * 2 + lax.rem(zz, 2)) * 2 + zz // 2
        return p, {"expert": yy * 2 + lax.rem(zz, 2), "zhi": zz // 2}

    direct = [(dy, dz) for dy in (0, 1, 3) for dz in (0, 1, 3) if (dy, dz) != (0, 0)]
    relayed = [((2, dz), (s, 0)) for dz in (0, 1, 3)]
    relayed += [((dy, 2), (0, s)) for dy in (0, 1, 3)]
    relayed += [((2, 2), (s, s))]
    me = (y * 2 + lax.rem(z, 2)) * 2 + z // 2
    return me, at, direct, relayed


def start_plane(n_grp, x_ref, y_ref, stage, send_sem, recv_sem, stage_sem, local_sem):
    me, at, direct, relayed = plane_plan(n_grp)
    copies = []
    local = pltpu.make_async_copy(x_ref.at[me], y_ref.at[me], local_sem)
    local.start()
    k = 0
    for j, (off, rel) in enumerate(relayed):
        p, _ = at(*off)
        _, dev = at(*rel)
        cp = pltpu.make_async_remote_copy(
            src_ref=x_ref.at[p], dst_ref=stage.at[j], send_sem=send_sem.at[k],
            recv_sem=stage_sem.at[j], device_id=dev, device_id_type=MESH_ID,
        )
        cp.start()
        copies.append(cp)
        k += 1
    for off in direct:
        p, dev = at(*off)
        cp = pltpu.make_async_remote_copy(
            src_ref=x_ref.at[p], dst_ref=y_ref.at[me], send_sem=send_sem.at[k],
            recv_sem=recv_sem.at[me], device_id=dev, device_id_type=MESH_ID,
        )
        cp.start()
        copies.append(cp)
        k += 1
    return local, copies, k


def relay_plane(n_grp, k, x_ref, y_ref, stage, send_sem, recv_sem, stage_sem):
    me, at, direct, relayed = plane_plan(n_grp)
    copies = []
    for j, (off, rel) in enumerate(relayed):
        src_p, _ = at(-rel[0], -rel[1])
        _, dev = at(off[0] - rel[0], off[1] - rel[1])
        pltpu.make_async_remote_copy(
            src_ref=x_ref.at[0], dst_ref=stage.at[j], send_sem=send_sem.at[0],
            recv_sem=stage_sem.at[j], device_id=dev, device_id_type=MESH_ID,
        ).wait_recv()
        cp = pltpu.make_async_remote_copy(
            src_ref=stage.at[j], dst_ref=y_ref.at[src_p], send_sem=send_sem.at[k],
            recv_sem=recv_sem.at[src_p], device_id=dev, device_id_type=MESH_ID,
        )
        cp.start()
        copies.append(cp)
        k += 1
    return copies


def plane_devices(n_grp):
    me, at, direct, relayed = plane_plan(n_grp)
    return [at(*off)[1] for off in direct]


def exchange_kernel(n_grp, x_ref, y_ref, send_sem, recv_sem, local_sem):
    me, peers = exchange_peers(n_grp)
    barrier = pltpu.get_barrier_semaphore()
    for p, dev in peers:
        pl.semaphore_signal(barrier, inc=1, device_id=dev, device_id_type=MESH_ID)
    pl.semaphore_wait(barrier, len(peers))
    local, copies = start_exchange(me, peers, x_ref, y_ref, send_sem, recv_sem, local_sem.at[0])
    finish_exchange(peers, local, copies, x_ref, y_ref, send_sem, recv_sem)


def exchange(x, n_grp, collective_id):
    any_spec = pl.BlockSpec(memory_space=pl.ANY)
    return pl.pallas_call(
        functools.partial(exchange_kernel, n_grp),
        out_shape=jax.ShapeDtypeStruct(x.shape, x.dtype),
        in_specs=[any_spec],
        out_specs=any_spec,
        scratch_shapes=[
            pltpu.SemaphoreType.DMA((n_grp,)),
            pltpu.SemaphoreType.DMA((n_grp,)),
            pltpu.SemaphoreType.DMA((1,)),
        ],
        compiler_params=pltpu.CompilerParams(collective_id=collective_id, has_side_effects=True),
        cost_estimate=pl.CostEstimate(flops=0, transcendentals=0, bytes_accessed=2 * x.size * 2),
    )(x)


def expert_return_kernel(n_grp, hid_ref, down_ref, y_ref, buf, stage, send_sem, recv_sem, stage_sem,
                         local_sem):
    me, at, direct, relayed = plane_plan(n_grp)
    n_rel = len(relayed)
    order = [off for off, rel in relayed] + direct + [(0, 0)]
    rel_of = [rel for off, rel in relayed]
    barrier = pltpu.get_barrier_semaphore()
    peers = plane_devices(n_grp)
    for dev in peers:
        pl.semaphore_signal(barrier, inc=1, device_id=dev, device_id_type=MESH_ID)

    def pick(k, values):
        out = values[-1]
        for i in range(len(values) - 2, -1, -1):
            out = jnp.where(k == i, values[i], out)
        return out

    def chunk_of(k):
        dy = pick(k, [o[0] for o in order])
        dz = pick(k, [o[1] for o in order])
        return at(dy, dz)

    def project(k):
        p, _ = chunk_of(k)
        buf[p] = jnp.dot(hid_ref[p], down_ref[...], preferred_element_type=jnp.float32).astype(buf.dtype)

    def first_hop(k):
        p, _ = chunk_of(k)
        ry = pick(k, [r[0] for r in rel_of])
        rz = pick(k, [r[1] for r in rel_of])
        _, dev = at(ry, rz)
        return pltpu.make_async_remote_copy(
            src_ref=buf.at[p], dst_ref=stage.at[k], send_sem=send_sem.at[k],
            recv_sem=stage_sem.at[k], device_id=dev, device_id_type=MESH_ID,
        )

    def direct_send(k):
        p, dev = chunk_of(k)
        return pltpu.make_async_remote_copy(
            src_ref=buf.at[p], dst_ref=y_ref.at[me], send_sem=send_sem.at[k],
            recv_sem=recv_sem.at[me], device_id=dev, device_id_type=MESH_ID,
        )

    def forwards():
        for j, (off, rel) in enumerate(relayed):
            src_p, _ = at(-rel[0], -rel[1])
            _, dev = at(off[0] - rel[0], off[1] - rel[1])
            pltpu.make_async_remote_copy(
                src_ref=buf.at[0], dst_ref=stage.at[j], send_sem=send_sem.at[0],
                recv_sem=stage_sem.at[j], device_id=dev, device_id_type=MESH_ID,
            ).wait_recv()
            pltpu.make_async_remote_copy(
                src_ref=stage.at[j], dst_ref=y_ref.at[src_p], send_sem=send_sem.at[n_grp - 1 + j],
                recv_sem=recv_sem.at[src_p], device_id=dev, device_id_type=MESH_ID,
            ).start()

    local = pltpu.make_async_copy(buf.at[me], y_ref.at[me], local_sem.at[0])
    project(0)
    pl.semaphore_wait(barrier, len(peers))

    def step(k, carry):
        project(k)

        @pl.when(k - 1 < n_rel)
        def _():
            first_hop(k - 1).start()

        @pl.when(k - 1 >= n_rel)
        def _():
            direct_send(k - 1).start()

        @pl.when(k == n_rel + 4)
        def _():
            forwards()

        return carry

    lax.fori_loop(1, n_grp, step, 0)
    local.start()

    local.wait()
    for k in range(n_grp - 1):
        if k < n_rel:
            first_hop(k).wait_send()
        else:
            direct_send(k).wait_send()
    for j, (off, rel) in enumerate(relayed):
        _, dev = at(off[0] - rel[0], off[1] - rel[1])
        pltpu.make_async_remote_copy(
            src_ref=stage.at[j], dst_ref=y_ref.at[0], send_sem=send_sem.at[n_grp - 1 + j],
            recv_sem=recv_sem.at[0], device_id=dev, device_id_type=MESH_ID,
        ).wait_send()
    for s in range(1, n_grp):
        q = lax.rem(me + s, n_grp)
        pltpu.make_async_remote_copy(
            src_ref=buf.at[0], dst_ref=y_ref.at[q], send_sem=send_sem.at[0],
            recv_sem=recv_sem.at[q], device_id=peers[0], device_id_type=MESH_ID,
        ).wait_recv()


def expert_return(hidden, down_full, n_grp, collective_id):
    n_src, cap, ff = hidden.shape
    width = down_full.shape[1]
    out = jax.ShapeDtypeStruct((n_src, cap, width), jnp.bfloat16)
    vmem = pl.BlockSpec(memory_space=pltpu.VMEM)
    flops = 2 * n_src * cap * ff * width
    nbytes = hidden.size * 2 + down_full.size * 2 + 2 * n_src * cap * width * 2
    return pl.pallas_call(
        functools.partial(expert_return_kernel, n_grp),
        out_shape=out,
        in_specs=[vmem] * 2,
        out_specs=pl.BlockSpec(memory_space=pl.ANY),
        scratch_shapes=[
            pltpu.VMEM((n_src, cap, width), jnp.bfloat16),
            pltpu.VMEM((7, cap, width), jnp.bfloat16),
            pltpu.SemaphoreType.DMA((n_grp + 8,)),
            pltpu.SemaphoreType.DMA((n_grp,)),
            pltpu.SemaphoreType.DMA((7,)),
            pltpu.SemaphoreType.DMA((1,)),
        ],
        compiler_params=pltpu.CompilerParams(
            collective_id=collective_id, has_side_effects=True, vmem_limit_bytes=56 * 1024 * 1024
        ),
        cost_estimate=pl.CostEstimate(flops=flops, transcendentals=0, bytes_accessed=nbytes),
    )(hidden, down_full)


def weight_kernel(n_x, n_grp, g_in, u_in, d_in, t_in, g_out, u_out, d_out, t_out, send_sem, recv_sem,
                  local_sem, t_send, t_recv, stage, stage_sem):
    ins = (g_in, u_in, d_in)
    outs = (g_out, u_out, d_out)
    x = lax.axis_index("x")
    h = lax.axis_index("zhi")
    c = lax.axis_index("core")

    def block(xx, hh, cc):
        return (xx * 2 + hh) * 2 + cc

    me = block(x, h, c)
    up_x = lax.rem(x + 1, n_x)
    down_x = lax.rem(x + n_x - 1, n_x)
    far_x = lax.rem(x + 2, n_x)
    toward = jnp.where(c == 0, up_x, down_x)
    away = jnp.where(c == 0, down_x, up_x)
    partner = {"core": 1 - c}
    z_peer = {"zhi": 1 - h}
    x_devs = [{"x": up_x}, {"x": down_x}]

    t_me, t_peers = exchange_peers(n_grp)
    barrier = pltpu.get_barrier_semaphore()
    greet = [partner, z_peer] + x_devs + plane_devices(n_grp)
    for dev in greet:
        pl.semaphore_signal(barrier, inc=1, device_id=dev, device_id_type=MESH_ID)
    pl.semaphore_wait(barrier, len(greet))

    count = [0]

    def send(src_of, blk, dev):
        k = count[0]
        count[0] += 1
        copies = []
        for m in range(3):
            cp = pltpu.make_async_remote_copy(
                src_ref=src_of(m),
                dst_ref=outs[m].at[blk],
                send_sem=send_sem.at[m, k],
                recv_sem=recv_sem.at[m, blk],
                device_id=dev,
                device_id_type=MESH_ID,
            )
            cp.start()
            copies.append(cp)
        return copies

    def wait_in(blk):
        for m in range(3):
            pltpu.make_async_remote_copy(
                src_ref=ins[m].at[0],
                dst_ref=outs[m].at[blk],
                send_sem=send_sem.at[m, 0],
                recv_sem=recv_sem.at[m, blk],
                device_id=partner,
                device_id_type=MESH_ID,
            ).wait_recv()

    sent = []
    local = []
    for m in range(3):
        cp = pltpu.make_async_copy(ins[m].at[h], outs[m].at[me], local_sem.at[m])
        cp.start()
        local.append(cp)
    sent += send(lambda m: ins[m].at[1 - h], me, z_peer)
    for dev in [partner] + x_devs:
        sent += send(lambda m: ins[m].at[h], me, dev)

    z_blk = block(x, 1 - h, c)
    wait_in(z_blk)
    for dev in [partner] + x_devs:
        sent += send(lambda m: outs[m].at[z_blk], z_blk, dev)

    for hh in (h, 1 - h):
        blk = block(away, hh, c)
        wait_in(blk)
        sent += send(lambda m: outs[m].at[blk], blk, partner)
        sent += send(lambda m: outs[m].at[blk], blk, {"x": toward})
    t_local, t_copies, t_k = start_plane(
        n_grp, t_in, t_out, stage, t_send, t_recv, stage_sem, local_sem.at[3]
    )
    t_copies += relay_plane(n_grp, t_k, t_in, t_out, stage, t_send, t_recv, stage_sem)
    for xp in (toward, far_x):
        for hh in (h, 1 - h):
            blk = block(xp, hh, c)
            wait_in(blk)
            sent += send(lambda m: outs[m].at[blk], blk, partner)

    for xx in range(n_x):
        for hh in (0, 1):
            wait_in(block(xx, hh, 1 - c))

    for cp in sent:
        cp.wait_send()
    for cp in local:
        cp.wait()
    finish_exchange(t_peers, t_local, t_copies, t_in, t_out, t_send, t_recv)


def gather_weights(gate_weight, up_weight, down_weight, outgoing, n_x, n_grp):
    blk_rows, width = gate_weight.shape[1], gate_weight.shape[2]
    n_blocks = n_x * 4
    n_send = 16
    shape = jax.ShapeDtypeStruct((n_blocks, blk_rows, width), gate_weight.dtype)
    any_spec = pl.BlockSpec(memory_space=pl.ANY)
    nbytes = 3 * n_blocks * blk_rows * width * 2
    return pl.pallas_call(
        functools.partial(weight_kernel, n_x, n_grp),
        out_shape=(shape, shape, shape, jax.ShapeDtypeStruct(outgoing.shape, outgoing.dtype)),
        in_specs=[any_spec] * 4,
        out_specs=(any_spec, any_spec, any_spec, any_spec),
        scratch_shapes=[
            pltpu.SemaphoreType.DMA((3, n_send)),
            pltpu.SemaphoreType.DMA((3, n_blocks)),
            pltpu.SemaphoreType.DMA((4,)),
            pltpu.SemaphoreType.DMA((n_grp + 8,)),
            pltpu.SemaphoreType.DMA((n_grp,)),
            pltpu.VMEM((7,) + outgoing.shape[1:], outgoing.dtype),
            pltpu.SemaphoreType.DMA((7,)),
        ],
        compiler_params=pltpu.CompilerParams(collective_id=0, has_side_effects=True),
        cost_estimate=pl.CostEstimate(flops=0, transcendentals=0, bytes_accessed=nbytes),
    )(gate_weight, up_weight, down_weight, outgoing)


def per_device(tokens, expert_ids, combine, gate_weight, up_weight, down_weight):
    n_x = lax.axis_size("x")
    assert n_x == 4
    per_group = gate_weight.shape[0]
    groups = lax.axis_size("expert")
    n_expert = per_group * groups
    n_grp = groups * 2
    assert n_grp == 16
    tok_rows, top_k = expert_ids.shape
    model_width = tokens.shape[1]
    n_slot = n_expert * CAP

    flat_ids = expert_ids.reshape(-1)
    onehot = (flat_ids[:, None] == jnp.arange(n_expert, dtype=jnp.int32)[None, :]).astype(jnp.int32)
    earlier = jnp.cumsum(onehot, axis=0) - onehot
    rank_within = jnp.sum(earlier * onehot, axis=1)
    slot_index = (flat_ids * CAP + rank_within).reshape(tok_rows, top_k)
    hit = slot_index[None, :, :] == jnp.arange(n_slot, dtype=jnp.int32)[:, None, None]
    pick = jnp.any(hit, axis=2).astype(jnp.bfloat16)
    outgoing = jnp.dot(pick, tokens, preferred_element_type=jnp.float32).astype(jnp.bfloat16)
    outgoing = outgoing.reshape(n_expert, CAP, model_width)

    g_all, u_all, d_all, arrived = gather_weights(
        gate_weight, up_weight, down_weight, outgoing, n_x, n_grp
    )
    gate_full = g_all.reshape(-1, model_width)
    up_full = u_all.reshape(-1, model_width)
    down_full = d_all.reshape(-1, model_width)
    gate_pre = jnp.einsum("scd,fd->scf", arrived, gate_full, preferred_element_type=jnp.float32)
    up_pre = jnp.einsum("scd,fd->scf", arrived, up_full, preferred_element_type=jnp.float32)
    hidden = (jax.nn.silu(gate_pre) * up_pre).astype(jnp.bfloat16)
    returned = expert_return(hidden, down_full, n_grp, 1)
    returned = returned.reshape(n_slot, model_width)

    weight_of = jnp.sum(
        jnp.where(hit, combine[None, :, :], jnp.zeros_like(combine)[None, :, :]), axis=2
    ).T
    weight_top = lax.reduce_precision(weight_of, exponent_bits=8, mantissa_bits=7)
    weight_hi = weight_top.astype(jnp.bfloat16)
    weight_lo = (weight_of - weight_top).astype(jnp.bfloat16)
    mixed = jnp.dot(weight_hi, returned, preferred_element_type=jnp.float32) + jnp.dot(
        weight_lo, returned, preferred_element_type=jnp.float32
    )
    return mixed.astype(jnp.bfloat16)


def solution(mesh):
    groups = mesh.shape["expert"]
    n_x = mesh.shape["fsdp"] // 4
    inner = Mesh(mesh.devices.reshape(groups, n_x, 2, 2), ("expert", "x", "zhi", "core"))
    rows = P(("expert", "x", "zhi", "core"), None)
    weights = P("expert", ("x", "zhi", "core"), None)
    return jax.shard_map(
        per_device,
        mesh=inner,
        in_specs=(rows, rows, rows, weights, weights, weights),
        out_specs=rows,
        check_vma=False,
    )
```

```python
import functools

import jax
import jax.numpy as jnp
from jax import lax
from jax.experimental import pallas as pl
from jax.experimental.pallas import tpu as pltpu
from jax.sharding import Mesh
from jax.sharding import PartitionSpec as P

CAP = 72
MESH_ID = pl.DeviceIdType.MESH


def exchange_peers(n_grp):
    me = lax.axis_index("expert") * 2 + lax.axis_index("zhi")
    peers = []
    for s in range(1, n_grp):
        p = lax.rem(me + s, n_grp)
        peers.append((p, {"expert": p // 2, "zhi": lax.rem(p, 2)}))
    return me, peers


def start_exchange(me, peers, x_ref, y_ref, send_sem, recv_sem, local_sem):
    copies = []
    local = pltpu.make_async_copy(x_ref.at[me], y_ref.at[me], local_sem)
    local.start()
    for k, (p, dev) in enumerate(peers):
        cp = pltpu.make_async_remote_copy(
            src_ref=x_ref.at[p],
            dst_ref=y_ref.at[me],
            send_sem=send_sem.at[k],
            recv_sem=recv_sem.at[me],
            device_id=dev,
            device_id_type=MESH_ID,
        )
        cp.start()
        copies.append(cp)
    return local, copies


def finish_exchange(peers, local, copies, x_ref, y_ref, send_sem, recv_sem):
    for k, (p, dev) in enumerate(peers):
        pltpu.make_async_remote_copy(
            src_ref=x_ref.at[0],
            dst_ref=y_ref.at[p],
            send_sem=send_sem.at[k],
            recv_sem=recv_sem.at[p],
            device_id=dev,
            device_id_type=MESH_ID,
        ).wait_recv()
    for cp in copies:
        cp.wait_send()
    local.wait()


def plane_plan(n_grp):
    e_idx = lax.axis_index("expert")
    h = lax.axis_index("zhi")
    c = lax.axis_index("core")
    y = e_idx // 2
    z = h * 2 + lax.rem(e_idx, 2)
    s = 1 - 2 * c

    def at(dy, dz):
        yy = lax.rem(y + dy + 4, 4)
        zz = lax.rem(z + dz + 4, 4)
        p = (yy * 2 + lax.rem(zz, 2)) * 2 + zz // 2
        return p, {"expert": yy * 2 + lax.rem(zz, 2), "zhi": zz // 2}

    direct = [(dy, dz) for dy in (0, 1, 3) for dz in (0, 1, 3) if (dy, dz) != (0, 0)]
    relayed = [((2, dz), (s, 0)) for dz in (0, 1, 3)]
    relayed += [((dy, 2), (0, s)) for dy in (0, 1, 3)]
    relayed += [((2, 2), (s, s))]
    me = (y * 2 + lax.rem(z, 2)) * 2 + z // 2
    return me, at, direct, relayed


def start_plane(n_grp, x_ref, y_ref, stage, send_sem, recv_sem, stage_sem, local_sem):
    me, at, direct, relayed = plane_plan(n_grp)
    copies = []
    local = pltpu.make_async_copy(x_ref.at[me], y_ref.at[me], local_sem)
    local.start()
    k = 0
    for j, (off, rel) in enumerate(relayed):
        p, _ = at(*off)
        _, dev = at(*rel)
        cp = pltpu.make_async_remote_copy(
            src_ref=x_ref.at[p], dst_ref=stage.at[j], send_sem=send_sem.at[k],
            recv_sem=stage_sem.at[j], device_id=dev, device_id_type=MESH_ID,
        )
        cp.start()
        copies.append(cp)
        k += 1
    for off in direct:
        p, dev = at(*off)
        cp = pltpu.make_async_remote_copy(
            src_ref=x_ref.at[p], dst_ref=y_ref.at[me], send_sem=send_sem.at[k],
            recv_sem=recv_sem.at[me], device_id=dev, device_id_type=MESH_ID,
        )
        cp.start()
        copies.append(cp)
        k += 1
    return local, copies, k


def relay_plane(n_grp, k, x_ref, y_ref, stage, send_sem, recv_sem, stage_sem):
    me, at, direct, relayed = plane_plan(n_grp)
    copies = []
    for j, (off, rel) in enumerate(relayed):
        src_p, _ = at(-rel[0], -rel[1])
        _, dev = at(off[0] - rel[0], off[1] - rel[1])
        pltpu.make_async_remote_copy(
            src_ref=x_ref.at[0], dst_ref=stage.at[j], send_sem=send_sem.at[0],
            recv_sem=stage_sem.at[j], device_id=dev, device_id_type=MESH_ID,
        ).wait_recv()
        cp = pltpu.make_async_remote_copy(
            src_ref=stage.at[j], dst_ref=y_ref.at[src_p], send_sem=send_sem.at[k],
            recv_sem=recv_sem.at[src_p], device_id=dev, device_id_type=MESH_ID,
        )
        cp.start()
        copies.append(cp)
        k += 1
    return copies


def plane_devices(n_grp):
    me, at, direct, relayed = plane_plan(n_grp)
    return [at(*off)[1] for off in direct]


def exchange_kernel(n_grp, x_ref, y_ref, send_sem, recv_sem, local_sem):
    me, peers = exchange_peers(n_grp)
    barrier = pltpu.get_barrier_semaphore()
    for p, dev in peers:
        pl.semaphore_signal(barrier, inc=1, device_id=dev, device_id_type=MESH_ID)
    pl.semaphore_wait(barrier, len(peers))
    local, copies = start_exchange(me, peers, x_ref, y_ref, send_sem, recv_sem, local_sem.at[0])
    finish_exchange(peers, local, copies, x_ref, y_ref, send_sem, recv_sem)


def exchange(x, n_grp, collective_id):
    any_spec = pl.BlockSpec(memory_space=pl.ANY)
    return pl.pallas_call(
        functools.partial(exchange_kernel, n_grp),
        out_shape=jax.ShapeDtypeStruct(x.shape, x.dtype),
        in_specs=[any_spec],
        out_specs=any_spec,
        scratch_shapes=[
            pltpu.SemaphoreType.DMA((n_grp,)),
            pltpu.SemaphoreType.DMA((n_grp,)),
            pltpu.SemaphoreType.DMA((1,)),
        ],
        compiler_params=pltpu.CompilerParams(collective_id=collective_id, has_side_effects=True),
        cost_estimate=pl.CostEstimate(flops=0, transcendentals=0, bytes_accessed=2 * x.size * 2),
    )(x)


def expert_return_kernel(n_grp, rows_ref, gate_ref, up_ref, down_ref, y_ref, buf, stage, hid_ref,
                         send_sem, recv_sem, stage_sem, local_sem):
    me, at, direct, relayed = plane_plan(n_grp)
    n_rel = len(relayed)
    order = [off for off, rel in relayed] + direct + [(0, 0)]
    rel_of = [rel for off, rel in relayed]
    barrier = pltpu.get_barrier_semaphore()
    peers = plane_devices(n_grp)
    for dev in peers:
        pl.semaphore_signal(barrier, inc=1, device_id=dev, device_id_type=MESH_ID)

    def pick(k, values):
        out = values[-1]
        for i in range(len(values) - 2, -1, -1):
            out = jnp.where(k == i, values[i], out)
        return out

    def chunk_of(k):
        dy = pick(k, [o[0] for o in order])
        dz = pick(k, [o[1] for o in order])
        return at(dy, dz)

    def project(k):
        p, _ = chunk_of(k)
        cap = buf.shape[1]
        hidden = hid_ref[pl.ds(pl.multiple_of(p * cap, 8), cap)].astype(jnp.bfloat16)
        buf[p] = jnp.dot(hidden, down_ref[...], preferred_element_type=jnp.float32).astype(buf.dtype)

    def first_hop(k):
        p, _ = chunk_of(k)
        ry = pick(k, [r[0] for r in rel_of])
        rz = pick(k, [r[1] for r in rel_of])
        _, dev = at(ry, rz)
        return pltpu.make_async_remote_copy(
            src_ref=buf.at[p], dst_ref=stage.at[k], send_sem=send_sem.at[k],
            recv_sem=stage_sem.at[k], device_id=dev, device_id_type=MESH_ID,
        )

    def direct_send(k):
        p, dev = chunk_of(k)
        return pltpu.make_async_remote_copy(
            src_ref=buf.at[p], dst_ref=y_ref.at[me], send_sem=send_sem.at[k],
            recv_sem=recv_sem.at[me], device_id=dev, device_id_type=MESH_ID,
        )

    def forwards():
        for j, (off, rel) in enumerate(relayed):
            src_p, _ = at(-rel[0], -rel[1])
            _, dev = at(off[0] - rel[0], off[1] - rel[1])
            pltpu.make_async_remote_copy(
                src_ref=buf.at[0], dst_ref=stage.at[j], send_sem=send_sem.at[0],
                recv_sem=stage_sem.at[j], device_id=dev, device_id_type=MESH_ID,
            ).wait_recv()
            pltpu.make_async_remote_copy(
                src_ref=stage.at[j], dst_ref=y_ref.at[src_p], send_sem=send_sem.at[n_grp - 1 + j],
                recv_sem=recv_sem.at[src_p], device_id=dev, device_id_type=MESH_ID,
            ).start()

    n_rows = rows_ref.shape[0]
    piece = n_rows // 2
    nt = (((1,), (1,)), ((), ()))
    for i in range(2):
        r = rows_ref[pl.ds(i * piece, piece)]
        gate_pre = lax.dot_general(r, gate_ref[...], nt, preferred_element_type=jnp.float32)
        up_pre = lax.dot_general(r, up_ref[...], nt, preferred_element_type=jnp.float32)
        hid_ref[pl.ds(i * piece, piece)] = jax.nn.silu(gate_pre) * up_pre

    local = pltpu.make_async_copy(buf.at[me], y_ref.at[me], local_sem.at[0])
    project(0)
    pl.semaphore_wait(barrier, len(peers))

    def step(k, carry):
        project(k)

        @pl.when(k - 1 < n_rel)
        def _():
            first_hop(k - 1).start()

        @pl.when(k - 1 >= n_rel)
        def _():
            direct_send(k - 1).start()

        @pl.when(k == n_rel + 4)
        def _():
            forwards()

        return carry

    lax.fori_loop(1, n_grp, step, 0)
    local.start()

    local.wait()
    for k in range(n_grp - 1):
        if k < n_rel:
            first_hop(k).wait_send()
        else:
            direct_send(k).wait_send()
    for j, (off, rel) in enumerate(relayed):
        _, dev = at(off[0] - rel[0], off[1] - rel[1])
        pltpu.make_async_remote_copy(
            src_ref=stage.at[j], dst_ref=y_ref.at[0], send_sem=send_sem.at[n_grp - 1 + j],
            recv_sem=recv_sem.at[0], device_id=dev, device_id_type=MESH_ID,
        ).wait_send()
    for s in range(1, n_grp):
        q = lax.rem(me + s, n_grp)
        pltpu.make_async_remote_copy(
            src_ref=buf.at[0], dst_ref=y_ref.at[q], send_sem=send_sem.at[0],
            recv_sem=recv_sem.at[q], device_id=peers[0], device_id_type=MESH_ID,
        ).wait_recv()


def expert_return(rows, gate_full, up_full, down_full, n_grp, collective_id):
    n_rows, width = rows.shape
    ff = gate_full.shape[0]
    n_src = n_grp
    cap = n_rows // n_src
    out = jax.ShapeDtypeStruct((n_src, cap, width), jnp.bfloat16)
    vmem = pl.BlockSpec(memory_space=pltpu.VMEM)
    flops = 6 * n_rows * ff * width
    nbytes = rows.size * 2 + 3 * gate_full.size * 2 + 2 * n_rows * width * 2
    return pl.pallas_call(
        functools.partial(expert_return_kernel, n_grp),
        out_shape=out,
        in_specs=[vmem] * 4,
        out_specs=pl.BlockSpec(memory_space=pl.ANY),
        scratch_shapes=[
            pltpu.VMEM((n_src, cap, width), jnp.bfloat16),
            pltpu.VMEM((7, cap, width), jnp.bfloat16),
            pltpu.VMEM((n_rows, ff), jnp.float32),
            pltpu.SemaphoreType.DMA((n_grp + 8,)),
            pltpu.SemaphoreType.DMA((n_grp,)),
            pltpu.SemaphoreType.DMA((7,)),
            pltpu.SemaphoreType.DMA((1,)),
        ],
        compiler_params=pltpu.CompilerParams(
            collective_id=collective_id, has_side_effects=True, vmem_limit_bytes=64 * 1024 * 1024 - 1024 * 1024
        ),
        cost_estimate=pl.CostEstimate(flops=flops, transcendentals=n_rows * ff, bytes_accessed=nbytes),
    )(rows, gate_full, up_full, down_full)


def weight_kernel(n_x, n_grp, g_in, u_in, d_in, t_in, g_out, u_out, d_out, t_out, send_sem, recv_sem,
                  local_sem, t_send, t_recv, stage, stage_sem):
    ins = (g_in, u_in, d_in)
    outs = (g_out, u_out, d_out)
    x = lax.axis_index("x")
    h = lax.axis_index("zhi")
    c = lax.axis_index("core")

    def block(xx, hh, cc):
        return (xx * 2 + hh) * 2 + cc

    me = block(x, h, c)
    up_x = lax.rem(x + 1, n_x)
    down_x = lax.rem(x + n_x - 1, n_x)
    far_x = lax.rem(x + 2, n_x)
    toward = jnp.where(c == 0, up_x, down_x)
    away = jnp.where(c == 0, down_x, up_x)
    partner = {"core": 1 - c}
    z_peer = {"zhi": 1 - h}
    x_devs = [{"x": up_x}, {"x": down_x}]

    t_me, t_peers = exchange_peers(n_grp)
    barrier = pltpu.get_barrier_semaphore()
    greet = [partner, z_peer] + x_devs + plane_devices(n_grp)
    for dev in greet:
        pl.semaphore_signal(barrier, inc=1, device_id=dev, device_id_type=MESH_ID)
    pl.semaphore_wait(barrier, len(greet))

    count = [0]

    def send(src_of, blk, dev):
        k = count[0]
        count[0] += 1
        copies = []
        for m in range(3):
            cp = pltpu.make_async_remote_copy(
                src_ref=src_of(m),
                dst_ref=outs[m].at[blk],
                send_sem=send_sem.at[m, k],
                recv_sem=recv_sem.at[m, blk],
                device_id=dev,
                device_id_type=MESH_ID,
            )
            cp.start()
            copies.append(cp)
        return copies

    def wait_in(blk):
        for m in range(3):
            pltpu.make_async_remote_copy(
                src_ref=ins[m].at[0],
                dst_ref=outs[m].at[blk],
                send_sem=send_sem.at[m, 0],
                recv_sem=recv_sem.at[m, blk],
                device_id=partner,
                device_id_type=MESH_ID,
            ).wait_recv()

    sent = []
    local = []
    for m in range(3):
        cp = pltpu.make_async_copy(ins[m].at[h], outs[m].at[me], local_sem.at[m])
        cp.start()
        local.append(cp)
    sent += send(lambda m: ins[m].at[1 - h], me, z_peer)
    for dev in [partner] + x_devs:
        sent += send(lambda m: ins[m].at[h], me, dev)

    z_blk = block(x, 1 - h, c)
    wait_in(z_blk)
    for dev in [partner] + x_devs:
        sent += send(lambda m: outs[m].at[z_blk], z_blk, dev)
    t_local, t_copies, t_k = start_plane(
        n_grp, t_in, t_out, stage, t_send, t_recv, stage_sem, local_sem.at[3]
    )
    t_copies += relay_plane(n_grp, t_k, t_in, t_out, stage, t_send, t_recv, stage_sem)

    for hh in (h, 1 - h):
        blk = block(away, hh, c)
        wait_in(blk)
        sent += send(lambda m: outs[m].at[blk], blk, partner)
        sent += send(lambda m: outs[m].at[blk], blk, {"x": toward})
    for xp in (toward, far_x):
        for hh in (h, 1 - h):
            blk = block(xp, hh, c)
            wait_in(blk)
            sent += send(lambda m: outs[m].at[blk], blk, partner)

    for xx in range(n_x):
        for hh in (0, 1):
            wait_in(block(xx, hh, 1 - c))

    for cp in sent:
        cp.wait_send()
    for cp in local:
        cp.wait()
    finish_exchange(t_peers, t_local, t_copies, t_in, t_out, t_send, t_recv)


def gather_weights(gate_weight, up_weight, down_weight, outgoing, n_x, n_grp):
    blk_rows, width = gate_weight.shape[1], gate_weight.shape[2]
    n_blocks = n_x * 4
    n_send = 16
    shape = jax.ShapeDtypeStruct((n_blocks, blk_rows, width), gate_weight.dtype)
    any_spec = pl.BlockSpec(memory_space=pl.ANY)
    nbytes = 3 * n_blocks * blk_rows * width * 2
    return pl.pallas_call(
        functools.partial(weight_kernel, n_x, n_grp),
        out_shape=(shape, shape, shape, jax.ShapeDtypeStruct(outgoing.shape, outgoing.dtype)),
        in_specs=[any_spec] * 4,
        out_specs=(any_spec, any_spec, any_spec, any_spec),
        scratch_shapes=[
            pltpu.SemaphoreType.DMA((3, n_send)),
            pltpu.SemaphoreType.DMA((3, n_blocks)),
            pltpu.SemaphoreType.DMA((4,)),
            pltpu.SemaphoreType.DMA((n_grp + 8,)),
            pltpu.SemaphoreType.DMA((n_grp,)),
            pltpu.VMEM((7,) + outgoing.shape[1:], outgoing.dtype),
            pltpu.SemaphoreType.DMA((7,)),
        ],
        compiler_params=pltpu.CompilerParams(collective_id=0, has_side_effects=True),
        cost_estimate=pl.CostEstimate(flops=0, transcendentals=0, bytes_accessed=nbytes),
    )(gate_weight, up_weight, down_weight, outgoing)


def per_device(tokens, expert_ids, combine, gate_weight, up_weight, down_weight):
    n_x = lax.axis_size("x")
    assert n_x == 4
    per_group = gate_weight.shape[0]
    groups = lax.axis_size("expert")
    n_expert = per_group * groups
    n_grp = groups * 2
    assert n_grp == 16
    tok_rows, top_k = expert_ids.shape
    model_width = tokens.shape[1]
    n_slot = n_expert * CAP

    flat_ids = expert_ids.reshape(-1)
    onehot = (flat_ids[:, None] == jnp.arange(n_expert, dtype=jnp.int32)[None, :]).astype(jnp.int32)
    earlier = jnp.cumsum(onehot, axis=0) - onehot
    rank_within = jnp.sum(earlier * onehot, axis=1)
    slot_index = (flat_ids * CAP + rank_within).reshape(tok_rows, top_k)
    hit = slot_index[None, :, :] == jnp.arange(n_slot, dtype=jnp.int32)[:, None, None]
    pick = jnp.any(hit, axis=2).astype(jnp.bfloat16)
    outgoing = jnp.dot(pick, tokens, preferred_element_type=jnp.float32).astype(jnp.bfloat16)
    outgoing = outgoing.reshape(n_expert, CAP, model_width)

    g_all, u_all, d_all, arrived = gather_weights(
        gate_weight, up_weight, down_weight, outgoing, n_x, n_grp
    )
    gate_full = g_all.reshape(-1, model_width)
    up_full = u_all.reshape(-1, model_width)
    down_full = d_all.reshape(-1, model_width)
    returned = expert_return(
        arrived.reshape(n_slot, model_width), gate_full, up_full, down_full, n_grp, 1
    )
    returned = returned.reshape(n_slot, model_width)

    weight_of = jnp.sum(
        jnp.where(hit, combine[None, :, :], jnp.zeros_like(combine)[None, :, :]), axis=2
    ).T
    weight_top = lax.reduce_precision(weight_of, exponent_bits=8, mantissa_bits=7)
    weight_hi = weight_top.astype(jnp.bfloat16)
    weight_lo = (weight_of - weight_top).astype(jnp.bfloat16)
    mixed = jnp.dot(weight_hi, returned, preferred_element_type=jnp.float32) + jnp.dot(
        weight_lo, returned, preferred_element_type=jnp.float32
    )
    return mixed.astype(jnp.bfloat16)


def solution(mesh):
    groups = mesh.shape["expert"]
    n_x = mesh.shape["fsdp"] // 4
    inner = Mesh(mesh.devices.reshape(groups, n_x, 2, 2), ("expert", "x", "zhi", "core"))
    rows = P(("expert", "x", "zhi", "core"), None)
    weights = P("expert", ("x", "zhi", "core"), None)
    return jax.shard_map(
        per_device,
        mesh=inner,
        in_specs=(rows, rows, rows, weights, weights, weights),
        out_specs=rows,
        check_vma=False,
    )
```

```python
import functools

import jax
import jax.numpy as jnp
from jax import lax
from jax.experimental import pallas as pl
from jax.experimental.pallas import tpu as pltpu
from jax.sharding import Mesh
from jax.sharding import PartitionSpec as P

CAP = 72
MESH_ID = pl.DeviceIdType.MESH


def exchange_peers(n_grp):
    me = lax.axis_index("expert") * 2 + lax.axis_index("zhi")
    peers = []
    for s in range(1, n_grp):
        p = lax.rem(me + s, n_grp)
        peers.append((p, {"expert": p // 2, "zhi": lax.rem(p, 2)}))
    return me, peers


def start_exchange(me, peers, x_ref, y_ref, send_sem, recv_sem, local_sem):
    copies = []
    local = pltpu.make_async_copy(x_ref.at[me], y_ref.at[me], local_sem)
    local.start()
    for k, (p, dev) in enumerate(peers):
        cp = pltpu.make_async_remote_copy(
            src_ref=x_ref.at[p],
            dst_ref=y_ref.at[me],
            send_sem=send_sem.at[k],
            recv_sem=recv_sem.at[me],
            device_id=dev,
            device_id_type=MESH_ID,
        )
        cp.start()
        copies.append(cp)
    return local, copies


def finish_exchange(peers, local, copies, x_ref, y_ref, send_sem, recv_sem):
    for k, (p, dev) in enumerate(peers):
        pltpu.make_async_remote_copy(
            src_ref=x_ref.at[0],
            dst_ref=y_ref.at[p],
            send_sem=send_sem.at[k],
            recv_sem=recv_sem.at[p],
            device_id=dev,
            device_id_type=MESH_ID,
        ).wait_recv()
    for cp in copies:
        cp.wait_send()
    local.wait()


def plane_plan(n_grp):
    e_idx = lax.axis_index("expert")
    h = lax.axis_index("zhi")
    c = lax.axis_index("core")
    y = e_idx // 2
    z = h * 2 + lax.rem(e_idx, 2)
    s = 1 - 2 * c

    def at(dy, dz):
        yy = lax.rem(y + dy + 4, 4)
        zz = lax.rem(z + dz + 4, 4)
        p = (yy * 2 + lax.rem(zz, 2)) * 2 + zz // 2
        return p, {"expert": yy * 2 + lax.rem(zz, 2), "zhi": zz // 2}

    direct = [(dy, dz) for dy in (0, 1, 3) for dz in (0, 1, 3) if (dy, dz) != (0, 0)]
    relayed = [((2, dz), (s, 0)) for dz in (0, 1, 3)]
    relayed += [((dy, 2), (0, s)) for dy in (0, 1, 3)]
    relayed += [((2, 2), (s, s))]
    me = (y * 2 + lax.rem(z, 2)) * 2 + z // 2
    return me, at, direct, relayed


def start_plane(n_grp, x_ref, y_ref, stage, send_sem, recv_sem, stage_sem, local_sem):
    me, at, direct, relayed = plane_plan(n_grp)
    copies = []
    local = pltpu.make_async_copy(x_ref.at[me], y_ref.at[me], local_sem)
    local.start()
    k = 0
    for j, (off, rel) in enumerate(relayed):
        p, _ = at(*off)
        _, dev = at(*rel)
        cp = pltpu.make_async_remote_copy(
            src_ref=x_ref.at[p], dst_ref=stage.at[j], send_sem=send_sem.at[k],
            recv_sem=stage_sem.at[j], device_id=dev, device_id_type=MESH_ID,
        )
        cp.start()
        copies.append(cp)
        k += 1
    for off in direct:
        p, dev = at(*off)
        cp = pltpu.make_async_remote_copy(
            src_ref=x_ref.at[p], dst_ref=y_ref.at[me], send_sem=send_sem.at[k],
            recv_sem=recv_sem.at[me], device_id=dev, device_id_type=MESH_ID,
        )
        cp.start()
        copies.append(cp)
        k += 1
    return local, copies, k


def relay_plane(n_grp, k, x_ref, y_ref, stage, send_sem, recv_sem, stage_sem):
    me, at, direct, relayed = plane_plan(n_grp)
    copies = []
    for j, (off, rel) in enumerate(relayed):
        src_p, _ = at(-rel[0], -rel[1])
        _, dev = at(off[0] - rel[0], off[1] - rel[1])
        pltpu.make_async_remote_copy(
            src_ref=x_ref.at[0], dst_ref=stage.at[j], send_sem=send_sem.at[0],
            recv_sem=stage_sem.at[j], device_id=dev, device_id_type=MESH_ID,
        ).wait_recv()
        cp = pltpu.make_async_remote_copy(
            src_ref=stage.at[j], dst_ref=y_ref.at[src_p], send_sem=send_sem.at[k],
            recv_sem=recv_sem.at[src_p], device_id=dev, device_id_type=MESH_ID,
        )
        cp.start()
        copies.append(cp)
        k += 1
    return copies


def plane_devices(n_grp):
    me, at, direct, relayed = plane_plan(n_grp)
    return [at(*off)[1] for off in direct]


def exchange_kernel(n_grp, x_ref, y_ref, send_sem, recv_sem, local_sem):
    me, peers = exchange_peers(n_grp)
    barrier = pltpu.get_barrier_semaphore()
    for p, dev in peers:
        pl.semaphore_signal(barrier, inc=1, device_id=dev, device_id_type=MESH_ID)
    pl.semaphore_wait(barrier, len(peers))
    local, copies = start_exchange(me, peers, x_ref, y_ref, send_sem, recv_sem, local_sem.at[0])
    finish_exchange(peers, local, copies, x_ref, y_ref, send_sem, recv_sem)


def exchange(x, n_grp, collective_id):
    any_spec = pl.BlockSpec(memory_space=pl.ANY)
    return pl.pallas_call(
        functools.partial(exchange_kernel, n_grp),
        out_shape=jax.ShapeDtypeStruct(x.shape, x.dtype),
        in_specs=[any_spec],
        out_specs=any_spec,
        scratch_shapes=[
            pltpu.SemaphoreType.DMA((n_grp,)),
            pltpu.SemaphoreType.DMA((n_grp,)),
            pltpu.SemaphoreType.DMA((1,)),
        ],
        compiler_params=pltpu.CompilerParams(collective_id=collective_id, has_side_effects=True),
        cost_estimate=pl.CostEstimate(flops=0, transcendentals=0, bytes_accessed=2 * x.size * 2),
    )(x)


def expert_return_kernel(n_grp, rows_ref, gate_ref, up_ref, down_ref, y_ref, buf, stage, hid_ref,
                         send_sem, recv_sem, stage_sem, local_sem):
    me, at, direct, relayed = plane_plan(n_grp)
    n_rel = len(relayed)
    order = [off for off, rel in relayed] + direct + [(0, 0)]
    rel_of = [rel for off, rel in relayed]
    barrier = pltpu.get_barrier_semaphore()
    peers = plane_devices(n_grp)
    for dev in peers:
        pl.semaphore_signal(barrier, inc=1, device_id=dev, device_id_type=MESH_ID)

    def pick(k, values):
        out = values[-1]
        for i in range(len(values) - 2, -1, -1):
            out = jnp.where(k == i, values[i], out)
        return out

    def chunk_of(k):
        dy = pick(k, [o[0] for o in order])
        dz = pick(k, [o[1] for o in order])
        return at(dy, dz)

    def project(k):
        p, _ = chunk_of(k)
        cap = buf.shape[1]
        hidden = hid_ref[pl.ds(pl.multiple_of(p * cap, 8), cap)].astype(jnp.bfloat16)
        buf[p] = jnp.dot(hidden, down_ref[...], preferred_element_type=jnp.float32).astype(buf.dtype)

    def first_hop(k):
        p, _ = chunk_of(k)
        ry = pick(k, [r[0] for r in rel_of])
        rz = pick(k, [r[1] for r in rel_of])
        _, dev = at(ry, rz)
        return pltpu.make_async_remote_copy(
            src_ref=buf.at[p], dst_ref=stage.at[k], send_sem=send_sem.at[k],
            recv_sem=stage_sem.at[k], device_id=dev, device_id_type=MESH_ID,
        )

    def direct_send(k):
        p, dev = chunk_of(k)
        return pltpu.make_async_remote_copy(
            src_ref=buf.at[p], dst_ref=y_ref.at[me], send_sem=send_sem.at[k],
            recv_sem=recv_sem.at[me], device_id=dev, device_id_type=MESH_ID,
        )

    def forwards():
        for j, (off, rel) in enumerate(relayed):
            src_p, _ = at(-rel[0], -rel[1])
            _, dev = at(off[0] - rel[0], off[1] - rel[1])
            pltpu.make_async_remote_copy(
                src_ref=buf.at[0], dst_ref=stage.at[j], send_sem=send_sem.at[0],
                recv_sem=stage_sem.at[j], device_id=dev, device_id_type=MESH_ID,
            ).wait_recv()
            pltpu.make_async_remote_copy(
                src_ref=stage.at[j], dst_ref=y_ref.at[src_p], send_sem=send_sem.at[n_grp - 1 + j],
                recv_sem=recv_sem.at[src_p], device_id=dev, device_id_type=MESH_ID,
            ).start()

    n_rows = rows_ref.shape[0]
    piece = n_rows // 2
    nt = (((1,), (1,)), ((), ()))
    for i in range(2):
        r = rows_ref[pl.ds(i * piece, piece)]
        gate_pre = lax.dot_general(r, gate_ref[...], nt, preferred_element_type=jnp.float32)
        up_pre = lax.dot_general(r, up_ref[...], nt, preferred_element_type=jnp.float32)
        hid_ref[pl.ds(i * piece, piece)] = jax.nn.silu(gate_pre) * up_pre

    local = pltpu.make_async_copy(buf.at[me], y_ref.at[me], local_sem.at[0])
    project(0)
    pl.semaphore_wait(barrier, len(peers))

    def step(k, carry):
        project(k)

        @pl.when(k - 1 < n_rel)
        def _():
            first_hop(k - 1).start()

        @pl.when(k - 1 >= n_rel)
        def _():
            direct_send(k - 1).start()

        @pl.when(k == n_rel + 4)
        def _():
            forwards()

        return carry

    lax.fori_loop(1, n_grp, step, 0)
    local.start()

    local.wait()
    for k in range(n_grp - 1):
        if k < n_rel:
            first_hop(k).wait_send()
        else:
            direct_send(k).wait_send()
    for j, (off, rel) in enumerate(relayed):
        _, dev = at(off[0] - rel[0], off[1] - rel[1])
        pltpu.make_async_remote_copy(
            src_ref=stage.at[j], dst_ref=y_ref.at[0], send_sem=send_sem.at[n_grp - 1 + j],
            recv_sem=recv_sem.at[0], device_id=dev, device_id_type=MESH_ID,
        ).wait_send()
    for s in range(1, n_grp):
        q = lax.rem(me + s, n_grp)
        pltpu.make_async_remote_copy(
            src_ref=buf.at[0], dst_ref=y_ref.at[q], send_sem=send_sem.at[0],
            recv_sem=recv_sem.at[q], device_id=peers[0], device_id_type=MESH_ID,
        ).wait_recv()


def expert_return(rows, gate_full, up_full, down_full, n_grp, collective_id):
    n_rows, width = rows.shape
    ff = gate_full.shape[0]
    n_src = n_grp
    cap = n_rows // n_src
    out = jax.ShapeDtypeStruct((n_src, cap, width), jnp.bfloat16)
    vmem = pl.BlockSpec(memory_space=pltpu.VMEM)
    flops = 6 * n_rows * ff * width
    nbytes = rows.size * 2 + 3 * gate_full.size * 2 + 2 * n_rows * width * 2
    return pl.pallas_call(
        functools.partial(expert_return_kernel, n_grp),
        out_shape=out,
        in_specs=[vmem] * 4,
        out_specs=pl.BlockSpec(memory_space=pl.ANY),
        scratch_shapes=[
            pltpu.VMEM((n_src, cap, width), jnp.bfloat16),
            pltpu.VMEM((7, cap, width), jnp.bfloat16),
            pltpu.VMEM((n_rows, ff), jnp.float32),
            pltpu.SemaphoreType.DMA((n_grp + 8,)),
            pltpu.SemaphoreType.DMA((n_grp,)),
            pltpu.SemaphoreType.DMA((7,)),
            pltpu.SemaphoreType.DMA((1,)),
        ],
        compiler_params=pltpu.CompilerParams(
            collective_id=collective_id, has_side_effects=True, vmem_limit_bytes=64 * 1024 * 1024 - 1024 * 1024
        ),
        cost_estimate=pl.CostEstimate(flops=flops, transcendentals=n_rows * ff, bytes_accessed=nbytes),
    )(rows, gate_full, up_full, down_full)


def weight_kernel(n_x, n_grp, g_in, u_in, d_in, t_in, g_out, u_out, d_out, t_out, send_sem, recv_sem,
                  local_sem, t_send, t_recv, stage, stage_sem):
    ins = (g_in, u_in, d_in)
    outs = (g_out, u_out, d_out)
    x = lax.axis_index("x")
    h = lax.axis_index("zhi")
    c = lax.axis_index("core")

    def block(xx, hh, cc):
        return (xx * 2 + hh) * 2 + cc

    me = block(x, h, c)
    up_x = lax.rem(x + 1, n_x)
    down_x = lax.rem(x + n_x - 1, n_x)
    far_x = lax.rem(x + 2, n_x)
    toward = jnp.where(c == 0, up_x, down_x)
    away = jnp.where(c == 0, down_x, up_x)
    partner = {"core": 1 - c}
    z_peer = {"zhi": 1 - h}
    x_devs = [{"x": up_x}, {"x": down_x}]

    t_me, t_peers = exchange_peers(n_grp)
    barrier = pltpu.get_barrier_semaphore()
    greet = [partner, z_peer] + x_devs + plane_devices(n_grp)
    for dev in greet:
        pl.semaphore_signal(barrier, inc=1, device_id=dev, device_id_type=MESH_ID)
    pl.semaphore_wait(barrier, len(greet))

    count = [0]

    def send(src_of, blk, dev):
        k = count[0]
        count[0] += 1
        copies = []
        for m in range(3):
            cp = pltpu.make_async_remote_copy(
                src_ref=src_of(m),
                dst_ref=outs[m].at[blk],
                send_sem=send_sem.at[m, k],
                recv_sem=recv_sem.at[m, blk],
                device_id=dev,
                device_id_type=MESH_ID,
            )
            cp.start()
            copies.append(cp)
        return copies

    def wait_in(blk):
        for m in range(3):
            pltpu.make_async_remote_copy(
                src_ref=ins[m].at[0],
                dst_ref=outs[m].at[blk],
                send_sem=send_sem.at[m, 0],
                recv_sem=recv_sem.at[m, blk],
                device_id=partner,
                device_id_type=MESH_ID,
            ).wait_recv()

    sent = []
    local = []
    for m in range(3):
        cp = pltpu.make_async_copy(ins[m].at[h], outs[m].at[me], local_sem.at[m])
        cp.start()
        local.append(cp)
    sent += send(lambda m: ins[m].at[1 - h], me, z_peer)
    for dev in [partner] + x_devs:
        sent += send(lambda m: ins[m].at[h], me, dev)

    z_blk = block(x, 1 - h, c)
    wait_in(z_blk)
    for dev in [partner] + x_devs:
        sent += send(lambda m: outs[m].at[z_blk], z_blk, dev)
    t_local, t_copies, t_k = start_plane(
        n_grp, t_in, t_out, stage, t_send, t_recv, stage_sem, local_sem.at[3]
    )
    t_copies += relay_plane(n_grp, t_k, t_in, t_out, stage, t_send, t_recv, stage_sem)

    for hh in (h, 1 - h):
        blk = block(away, hh, c)
        wait_in(blk)
        sent += send(lambda m: outs[m].at[blk], blk, partner)
        sent += send(lambda m: outs[m].at[blk], blk, {"x": toward})
    for xp in (toward, far_x):
        for hh in (h, 1 - h):
            blk = block(xp, hh, c)
            wait_in(blk)
            sent += send(lambda m: outs[m].at[blk], blk, partner)

    for xx in range(n_x):
        for hh in (0, 1):
            wait_in(block(xx, hh, 1 - c))

    for cp in sent:
        cp.wait_send()
    for cp in local:
        cp.wait()
    finish_exchange(t_peers, t_local, t_copies, t_in, t_out, t_send, t_recv)


def gather_weights(gate_weight, up_weight, down_weight, outgoing, n_x, n_grp):
    blk_rows, width = gate_weight.shape[1], gate_weight.shape[2]
    n_blocks = n_x * 4
    n_send = 16
    shape = jax.ShapeDtypeStruct((n_blocks, blk_rows, width), gate_weight.dtype)
    any_spec = pl.BlockSpec(memory_space=pl.ANY)
    nbytes = 3 * n_blocks * blk_rows * width * 2
    return pl.pallas_call(
        functools.partial(weight_kernel, n_x, n_grp),
        out_shape=(shape, shape, shape, jax.ShapeDtypeStruct(outgoing.shape, outgoing.dtype)),
        in_specs=[any_spec] * 4,
        out_specs=(any_spec, any_spec, any_spec, any_spec),
        scratch_shapes=[
            pltpu.SemaphoreType.DMA((3, n_send)),
            pltpu.SemaphoreType.DMA((3, n_blocks)),
            pltpu.SemaphoreType.DMA((4,)),
            pltpu.SemaphoreType.DMA((n_grp + 8,)),
            pltpu.SemaphoreType.DMA((n_grp,)),
            pltpu.VMEM((7,) + outgoing.shape[1:], outgoing.dtype),
            pltpu.SemaphoreType.DMA((7,)),
        ],
        compiler_params=pltpu.CompilerParams(collective_id=0, has_side_effects=True),
        cost_estimate=pl.CostEstimate(flops=0, transcendentals=0, bytes_accessed=nbytes),
    )(gate_weight, up_weight, down_weight, outgoing)


def per_device(tokens, expert_ids, combine, gate_weight, up_weight, down_weight):
    n_x = lax.axis_size("x")
    assert n_x == 4
    per_group = gate_weight.shape[0]
    groups = lax.axis_size("expert")
    n_expert = per_group * groups
    n_grp = groups * 2
    assert n_grp == 16
    tok_rows, top_k = expert_ids.shape
    model_width = tokens.shape[1]
    n_slot = n_expert * CAP

    flat_ids = expert_ids.reshape(-1)
    onehot = (flat_ids[:, None] == jnp.arange(n_expert, dtype=jnp.int32)[None, :]).astype(jnp.int32)
    earlier = jnp.cumsum(onehot, axis=0) - onehot
    rank_within = jnp.sum(earlier * onehot, axis=1)
    slot_index = (flat_ids * CAP + rank_within).reshape(tok_rows, top_k)
    hit = slot_index[None, :, :] == jnp.arange(n_slot, dtype=jnp.int32)[:, None, None]
    pick = jnp.any(hit, axis=2).astype(jnp.bfloat16)
    outgoing = jnp.dot(pick, tokens, preferred_element_type=jnp.float32).astype(jnp.bfloat16)
    outgoing = outgoing.reshape(n_expert, CAP, model_width)

    g_all, u_all, d_all, arrived = gather_weights(
        gate_weight, up_weight, down_weight, outgoing, n_x, n_grp
    )
    gate_full = g_all.reshape(-1, model_width)
    up_full = u_all.reshape(-1, model_width)
    down_full = d_all.reshape(-1, model_width)
    returned = expert_return(
        arrived.reshape(n_slot, model_width), gate_full, up_full, down_full, n_grp, 1
    )
    returned = returned.reshape(n_slot, model_width)

    weight_of = jnp.sum(
        jnp.where(hit, combine[None, :, :], jnp.zeros_like(combine)[None, :, :]), axis=2
    ).T
    weight_top = lax.reduce_precision(weight_of, exponent_bits=8, mantissa_bits=7)
    weight_hi = weight_top.astype(jnp.bfloat16)
    weight_lo = (weight_of - weight_top).astype(jnp.bfloat16)
    both = jnp.dot(
        jnp.concatenate([weight_hi, weight_lo], axis=0), returned, preferred_element_type=jnp.float32
    )
    mixed = both[:tok_rows] + both[tok_rows:]
    return mixed.astype(jnp.bfloat16)


def solution(mesh):
    groups = mesh.shape["expert"]
    n_x = mesh.shape["fsdp"] // 4
    inner = Mesh(mesh.devices.reshape(groups, n_x, 2, 2), ("expert", "x", "zhi", "core"))
    rows = P(("expert", "x", "zhi", "core"), None)
    weights = P("expert", ("x", "zhi", "core"), None)
    return jax.shard_map(
        per_device,
        mesh=inner,
        in_specs=(rows, rows, rows, weights, weights, weights),
        out_specs=rows,
        check_vma=False,
    )
```

```python
import functools

import jax
import jax.numpy as jnp
from jax import lax
from jax.experimental import pallas as pl
from jax.experimental.pallas import tpu as pltpu
from jax.sharding import Mesh
from jax.sharding import PartitionSpec as P

CAP = 72
MESH_ID = pl.DeviceIdType.MESH


def exchange_peers(n_grp):
    me = lax.axis_index("expert") * 2 + lax.axis_index("zhi")
    peers = []
    for s in range(1, n_grp):
        p = lax.rem(me + s, n_grp)
        peers.append((p, {"expert": p // 2, "zhi": lax.rem(p, 2)}))
    return me, peers


def start_exchange(me, peers, x_ref, y_ref, send_sem, recv_sem, local_sem):
    copies = []
    local = pltpu.make_async_copy(x_ref.at[me], y_ref.at[me], local_sem)
    local.start()
    for k, (p, dev) in enumerate(peers):
        cp = pltpu.make_async_remote_copy(
            src_ref=x_ref.at[p],
            dst_ref=y_ref.at[me],
            send_sem=send_sem.at[k],
            recv_sem=recv_sem.at[me],
            device_id=dev,
            device_id_type=MESH_ID,
        )
        cp.start()
        copies.append(cp)
    return local, copies


def finish_exchange(peers, local, copies, x_ref, y_ref, send_sem, recv_sem):
    for k, (p, dev) in enumerate(peers):
        pltpu.make_async_remote_copy(
            src_ref=x_ref.at[0],
            dst_ref=y_ref.at[p],
            send_sem=send_sem.at[k],
            recv_sem=recv_sem.at[p],
            device_id=dev,
            device_id_type=MESH_ID,
        ).wait_recv()
    for cp in copies:
        cp.wait_send()
    local.wait()


def plane_plan(n_grp):
    e_idx = lax.axis_index("expert")
    h = lax.axis_index("zhi")
    c = lax.axis_index("core")
    y = e_idx // 2
    z = h * 2 + lax.rem(e_idx, 2)
    s = 1 - 2 * c

    def at(dy, dz):
        yy = lax.rem(y + dy + 4, 4)
        zz = lax.rem(z + dz + 4, 4)
        p = (yy * 2 + lax.rem(zz, 2)) * 2 + zz // 2
        return p, {"expert": yy * 2 + lax.rem(zz, 2), "zhi": zz // 2}

    direct = [(dy, dz) for dy in (0, 1, 3) for dz in (0, 1, 3) if (dy, dz) != (0, 0)]
    relayed = [((2, dz), (s, 0)) for dz in (0, 1, 3)]
    relayed += [((dy, 2), (0, s)) for dy in (0, 1, 3)]
    relayed += [((2, 2), (s, s))]
    me = (y * 2 + lax.rem(z, 2)) * 2 + z // 2
    return me, at, direct, relayed


def start_plane(n_grp, x_ref, y_ref, stage, send_sem, recv_sem, stage_sem, local_sem):
    me, at, direct, relayed = plane_plan(n_grp)
    copies = []
    local = pltpu.make_async_copy(x_ref.at[me], y_ref.at[me], local_sem)
    local.start()
    k = 0
    for j, (off, rel) in enumerate(relayed):
        p, _ = at(*off)
        _, dev = at(*rel)
        cp = pltpu.make_async_remote_copy(
            src_ref=x_ref.at[p], dst_ref=stage.at[j], send_sem=send_sem.at[k],
            recv_sem=stage_sem.at[j], device_id=dev, device_id_type=MESH_ID,
        )
        cp.start()
        copies.append(cp)
        k += 1
    for off in direct:
        p, dev = at(*off)
        cp = pltpu.make_async_remote_copy(
            src_ref=x_ref.at[p], dst_ref=y_ref.at[me], send_sem=send_sem.at[k],
            recv_sem=recv_sem.at[me], device_id=dev, device_id_type=MESH_ID,
        )
        cp.start()
        copies.append(cp)
        k += 1
    return local, copies, k


def relay_plane(n_grp, k, x_ref, y_ref, stage, send_sem, recv_sem, stage_sem):
    me, at, direct, relayed = plane_plan(n_grp)
    copies = []
    for j, (off, rel) in enumerate(relayed):
        src_p, _ = at(-rel[0], -rel[1])
        _, dev = at(off[0] - rel[0], off[1] - rel[1])
        pltpu.make_async_remote_copy(
            src_ref=x_ref.at[0], dst_ref=stage.at[j], send_sem=send_sem.at[0],
            recv_sem=stage_sem.at[j], device_id=dev, device_id_type=MESH_ID,
        ).wait_recv()
        cp = pltpu.make_async_remote_copy(
            src_ref=stage.at[j], dst_ref=y_ref.at[src_p], send_sem=send_sem.at[k],
            recv_sem=recv_sem.at[src_p], device_id=dev, device_id_type=MESH_ID,
        )
        cp.start()
        copies.append(cp)
        k += 1
    return copies


def plane_devices(n_grp):
    me, at, direct, relayed = plane_plan(n_grp)
    return [at(*off)[1] for off in direct]


def exchange_kernel(n_grp, x_ref, y_ref, send_sem, recv_sem, local_sem):
    me, peers = exchange_peers(n_grp)
    barrier = pltpu.get_barrier_semaphore()
    for p, dev in peers:
        pl.semaphore_signal(barrier, inc=1, device_id=dev, device_id_type=MESH_ID)
    pl.semaphore_wait(barrier, len(peers))
    local, copies = start_exchange(me, peers, x_ref, y_ref, send_sem, recv_sem, local_sem.at[0])
    finish_exchange(peers, local, copies, x_ref, y_ref, send_sem, recv_sem)


def exchange(x, n_grp, collective_id):
    any_spec = pl.BlockSpec(memory_space=pl.ANY)
    return pl.pallas_call(
        functools.partial(exchange_kernel, n_grp),
        out_shape=jax.ShapeDtypeStruct(x.shape, x.dtype),
        in_specs=[any_spec],
        out_specs=any_spec,
        scratch_shapes=[
            pltpu.SemaphoreType.DMA((n_grp,)),
            pltpu.SemaphoreType.DMA((n_grp,)),
            pltpu.SemaphoreType.DMA((1,)),
        ],
        compiler_params=pltpu.CompilerParams(collective_id=collective_id, has_side_effects=True),
        cost_estimate=pl.CostEstimate(flops=0, transcendentals=0, bytes_accessed=2 * x.size * 2),
    )(x)


def expert_return_kernel(n_grp, rows_ref, gate_ref, up_ref, down_ref, y_ref, buf, stage, hid_ref,
                         send_sem, recv_sem, stage_sem, local_sem):
    me, at, direct, relayed = plane_plan(n_grp)
    n_rel = len(relayed)
    order = [off for off, rel in relayed] + direct + [(0, 0)]
    rel_of = [rel for off, rel in relayed]
    barrier = pltpu.get_barrier_semaphore()
    peers = plane_devices(n_grp)
    for dev in peers:
        pl.semaphore_signal(barrier, inc=1, device_id=dev, device_id_type=MESH_ID)

    def pick(k, values):
        out = values[-1]
        for i in range(len(values) - 2, -1, -1):
            out = jnp.where(k == i, values[i], out)
        return out

    def chunk_of(k):
        dy = pick(k, [o[0] for o in order])
        dz = pick(k, [o[1] for o in order])
        return at(dy, dz)

    def project(k):
        p, _ = chunk_of(k)
        cap = buf.shape[1]
        hidden = hid_ref[pl.ds(pl.multiple_of(p * cap, 8), cap)].astype(jnp.bfloat16)
        buf[p] = jnp.dot(hidden, down_ref[...], preferred_element_type=jnp.float32).astype(buf.dtype)

    def first_hop(k):
        p, _ = chunk_of(k)
        ry = pick(k, [r[0] for r in rel_of])
        rz = pick(k, [r[1] for r in rel_of])
        _, dev = at(ry, rz)
        return pltpu.make_async_remote_copy(
            src_ref=buf.at[p], dst_ref=stage.at[k], send_sem=send_sem.at[k],
            recv_sem=stage_sem.at[k], device_id=dev, device_id_type=MESH_ID,
        )

    def direct_send(k):
        p, dev = chunk_of(k)
        return pltpu.make_async_remote_copy(
            src_ref=buf.at[p], dst_ref=y_ref.at[me], send_sem=send_sem.at[k],
            recv_sem=recv_sem.at[me], device_id=dev, device_id_type=MESH_ID,
        )

    def forwards():
        for j, (off, rel) in enumerate(relayed):
            src_p, _ = at(-rel[0], -rel[1])
            _, dev = at(off[0] - rel[0], off[1] - rel[1])
            pltpu.make_async_remote_copy(
                src_ref=buf.at[0], dst_ref=stage.at[j], send_sem=send_sem.at[0],
                recv_sem=stage_sem.at[j], device_id=dev, device_id_type=MESH_ID,
            ).wait_recv()
            pltpu.make_async_remote_copy(
                src_ref=stage.at[j], dst_ref=y_ref.at[src_p], send_sem=send_sem.at[n_grp - 1 + j],
                recv_sem=recv_sem.at[src_p], device_id=dev, device_id_type=MESH_ID,
            ).start()

    n_rows = rows_ref.shape[0]
    piece = n_rows // 2
    nt = (((1,), (1,)), ((), ()))
    for i in range(2):
        r = rows_ref[pl.ds(i * piece, piece)]
        gate_pre = lax.dot_general(r, gate_ref[...], nt, preferred_element_type=jnp.float32)
        up_pre = lax.dot_general(r, up_ref[...], nt, preferred_element_type=jnp.float32)
        hid_ref[pl.ds(i * piece, piece)] = jax.nn.silu(gate_pre) * up_pre

    local = pltpu.make_async_copy(buf.at[me], y_ref.at[me], local_sem.at[0])
    project(0)
    pl.semaphore_wait(barrier, len(peers))

    def step(k, carry):
        project(k)

        @pl.when(k - 1 < n_rel)
        def _():
            first_hop(k - 1).start()

        @pl.when(k - 1 >= n_rel)
        def _():
            direct_send(k - 1).start()

        @pl.when(k == n_rel + 4)
        def _():
            forwards()

        return carry

    lax.fori_loop(1, n_grp, step, 0)
    local.start()

    local.wait()
    for k in range(n_grp - 1):
        if k < n_rel:
            first_hop(k).wait_send()
        else:
            direct_send(k).wait_send()
    for j, (off, rel) in enumerate(relayed):
        _, dev = at(off[0] - rel[0], off[1] - rel[1])
        pltpu.make_async_remote_copy(
            src_ref=stage.at[j], dst_ref=y_ref.at[0], send_sem=send_sem.at[n_grp - 1 + j],
            recv_sem=recv_sem.at[0], device_id=dev, device_id_type=MESH_ID,
        ).wait_send()
    for s in range(1, n_grp):
        q = lax.rem(me + s, n_grp)
        pltpu.make_async_remote_copy(
            src_ref=buf.at[0], dst_ref=y_ref.at[q], send_sem=send_sem.at[0],
            recv_sem=recv_sem.at[q], device_id=peers[0], device_id_type=MESH_ID,
        ).wait_recv()


def expert_return(rows, gate_full, up_full, down_full, n_grp, collective_id):
    n_rows, width = rows.shape
    ff = gate_full.shape[0]
    n_src = n_grp
    cap = n_rows // n_src
    out = jax.ShapeDtypeStruct((n_src, cap, width), jnp.bfloat16)
    vmem = pl.BlockSpec(memory_space=pltpu.VMEM)
    flops = 6 * n_rows * ff * width
    nbytes = rows.size * 2 + 3 * gate_full.size * 2 + 2 * n_rows * width * 2
    return pl.pallas_call(
        functools.partial(expert_return_kernel, n_grp),
        out_shape=out,
        in_specs=[vmem] * 4,
        out_specs=pl.BlockSpec(memory_space=pl.ANY),
        scratch_shapes=[
            pltpu.VMEM((n_src, cap, width), jnp.bfloat16),
            pltpu.VMEM((7, cap, width), jnp.bfloat16),
            pltpu.VMEM((n_rows, ff), jnp.float32),
            pltpu.SemaphoreType.DMA((n_grp + 8,)),
            pltpu.SemaphoreType.DMA((n_grp,)),
            pltpu.SemaphoreType.DMA((7,)),
            pltpu.SemaphoreType.DMA((1,)),
        ],
        compiler_params=pltpu.CompilerParams(
            collective_id=collective_id, has_side_effects=True, vmem_limit_bytes=64 * 1024 * 1024 - 1024 * 1024
        ),
        cost_estimate=pl.CostEstimate(flops=flops, transcendentals=n_rows * ff, bytes_accessed=nbytes),
    )(rows, gate_full, up_full, down_full)


def weight_kernel(n_x, n_grp, g_in, u_in, d_in, t_in, g_out, u_out, d_out, t_out, send_sem, recv_sem,
                  local_sem, t_send, t_recv, stage, stage_sem):
    ins = (g_in, u_in, d_in)
    outs = (g_out, u_out, d_out)
    x = lax.axis_index("x")
    h = lax.axis_index("zhi")
    c = lax.axis_index("core")

    def block(xx, hh, cc):
        return (xx * 2 + hh) * 2 + cc

    me = block(x, h, c)
    up_x = lax.rem(x + 1, n_x)
    down_x = lax.rem(x + n_x - 1, n_x)
    far_x = lax.rem(x + 2, n_x)
    toward = jnp.where(c == 0, up_x, down_x)
    away = jnp.where(c == 0, down_x, up_x)
    partner = {"core": 1 - c}
    z_peer = {"zhi": 1 - h}
    x_devs = [{"x": up_x}, {"x": down_x}]

    t_me, t_peers = exchange_peers(n_grp)
    barrier = pltpu.get_barrier_semaphore()
    greet = [partner, z_peer] + x_devs + plane_devices(n_grp)
    for dev in greet:
        pl.semaphore_signal(barrier, inc=1, device_id=dev, device_id_type=MESH_ID)
    pl.semaphore_wait(barrier, len(greet))

    count = [0]

    def send(src_of, blk, dev):
        k = count[0]
        count[0] += 1
        copies = []
        for m in range(3):
            cp = pltpu.make_async_remote_copy(
                src_ref=src_of(m),
                dst_ref=outs[m].at[blk],
                send_sem=send_sem.at[m, k],
                recv_sem=recv_sem.at[m, blk],
                device_id=dev,
                device_id_type=MESH_ID,
            )
            cp.start()
            copies.append(cp)
        return copies

    def wait_in(blk):
        for m in range(3):
            pltpu.make_async_remote_copy(
                src_ref=ins[m].at[0],
                dst_ref=outs[m].at[blk],
                send_sem=send_sem.at[m, 0],
                recv_sem=recv_sem.at[m, blk],
                device_id=partner,
                device_id_type=MESH_ID,
            ).wait_recv()

    sent = []
    local = []
    for m in range(3):
        cp = pltpu.make_async_copy(ins[m].at[h], outs[m].at[me], local_sem.at[m])
        cp.start()
        local.append(cp)
    sent += send(lambda m: ins[m].at[1 - h], me, z_peer)
    for dev in [partner] + x_devs:
        sent += send(lambda m: ins[m].at[h], me, dev)

    z_blk = block(x, 1 - h, c)
    wait_in(z_blk)
    for dev in [partner] + x_devs:
        sent += send(lambda m: outs[m].at[z_blk], z_blk, dev)
    t_local, t_copies, t_k = start_plane(
        n_grp, t_in, t_out, stage, t_send, t_recv, stage_sem, local_sem.at[3]
    )
    t_copies += relay_plane(n_grp, t_k, t_in, t_out, stage, t_send, t_recv, stage_sem)

    for hh in (h, 1 - h):
        blk = block(away, hh, c)
        wait_in(blk)
        sent += send(lambda m: outs[m].at[blk], blk, partner)
        sent += send(lambda m: outs[m].at[blk], blk, {"x": toward})
    for xp in (toward, far_x):
        for hh in (h, 1 - h):
            blk = block(xp, hh, c)
            wait_in(blk)
            sent += send(lambda m: outs[m].at[blk], blk, partner)

    for xx in range(n_x):
        for hh in (0, 1):
            wait_in(block(xx, hh, 1 - c))

    for cp in sent:
        cp.wait_send()
    for cp in local:
        cp.wait()
    finish_exchange(t_peers, t_local, t_copies, t_in, t_out, t_send, t_recv)


def gather_weights(gate_weight, up_weight, down_weight, outgoing, n_x, n_grp):
    blk_rows, width = gate_weight.shape[1], gate_weight.shape[2]
    n_blocks = n_x * 4
    n_send = 16
    shape = jax.ShapeDtypeStruct((n_blocks, blk_rows, width), gate_weight.dtype)
    any_spec = pl.BlockSpec(memory_space=pl.ANY)
    nbytes = 3 * n_blocks * blk_rows * width * 2
    return pl.pallas_call(
        functools.partial(weight_kernel, n_x, n_grp),
        out_shape=(shape, shape, shape, jax.ShapeDtypeStruct(outgoing.shape, outgoing.dtype)),
        in_specs=[any_spec] * 4,
        out_specs=(any_spec, any_spec, any_spec, any_spec),
        scratch_shapes=[
            pltpu.SemaphoreType.DMA((3, n_send)),
            pltpu.SemaphoreType.DMA((3, n_blocks)),
            pltpu.SemaphoreType.DMA((4,)),
            pltpu.SemaphoreType.DMA((n_grp + 8,)),
            pltpu.SemaphoreType.DMA((n_grp,)),
            pltpu.VMEM((7,) + outgoing.shape[1:], outgoing.dtype),
            pltpu.SemaphoreType.DMA((7,)),
        ],
        compiler_params=pltpu.CompilerParams(collective_id=0, has_side_effects=True),
        cost_estimate=pl.CostEstimate(flops=0, transcendentals=0, bytes_accessed=nbytes),
    )(gate_weight, up_weight, down_weight, outgoing)


def per_device(tokens, expert_ids, combine, gate_weight, up_weight, down_weight):
    n_x = lax.axis_size("x")
    assert n_x == 4
    per_group = gate_weight.shape[0]
    groups = lax.axis_size("expert")
    n_expert = per_group * groups
    n_grp = groups * 2
    assert n_grp == 16
    tok_rows, top_k = expert_ids.shape
    model_width = tokens.shape[1]
    n_slot = n_expert * CAP

    flat_ids = expert_ids.reshape(-1)
    onehot = (flat_ids[:, None] == jnp.arange(n_expert, dtype=jnp.int32)[None, :]).astype(jnp.int32)
    n_pair = flat_ids.shape[0]
    before = (
        lax.broadcasted_iota(jnp.int32, (n_pair, n_pair), 0)
        > lax.broadcasted_iota(jnp.int32, (n_pair, n_pair), 1)
    ).astype(jnp.bfloat16)
    earlier = jnp.dot(before, onehot.astype(jnp.bfloat16), preferred_element_type=jnp.float32)
    earlier = earlier.astype(jnp.int32)
    rank_within = jnp.sum(earlier * onehot, axis=1)
    slot_index = (flat_ids * CAP + rank_within).reshape(tok_rows, top_k)
    hit = slot_index[None, :, :] == jnp.arange(n_slot, dtype=jnp.int32)[:, None, None]
    pick = jnp.any(hit, axis=2).astype(jnp.bfloat16)
    outgoing = jnp.dot(pick, tokens, preferred_element_type=jnp.float32).astype(jnp.bfloat16)
    outgoing = outgoing.reshape(n_expert, CAP, model_width)

    g_all, u_all, d_all, arrived = gather_weights(
        gate_weight, up_weight, down_weight, outgoing, n_x, n_grp
    )
    gate_full = g_all.reshape(-1, model_width)
    up_full = u_all.reshape(-1, model_width)
    down_full = d_all.reshape(-1, model_width)
    returned = expert_return(
        arrived.reshape(n_slot, model_width), gate_full, up_full, down_full, n_grp, 1
    )
    returned = returned.reshape(n_slot, model_width)

    weight_of = jnp.sum(
        jnp.where(hit, combine[None, :, :], jnp.zeros_like(combine)[None, :, :]), axis=2
    ).T
    weight_top = lax.reduce_precision(weight_of, exponent_bits=8, mantissa_bits=7)
    weight_hi = weight_top.astype(jnp.bfloat16)
    weight_lo = (weight_of - weight_top).astype(jnp.bfloat16)
    both = jnp.dot(
        jnp.concatenate([weight_hi, weight_lo], axis=0), returned, preferred_element_type=jnp.float32
    )
    mixed = both[:tok_rows] + both[tok_rows:]
    return mixed.astype(jnp.bfloat16)


def solution(mesh):
    groups = mesh.shape["expert"]
    n_x = mesh.shape["fsdp"] // 4
    inner = Mesh(mesh.devices.reshape(groups, n_x, 2, 2), ("expert", "x", "zhi", "core"))
    rows = P(("expert", "x", "zhi", "core"), None)
    weights = P("expert", ("x", "zhi", "core"), None)
    return jax.shard_map(
        per_device,
        mesh=inner,
        in_specs=(rows, rows, rows, weights, weights, weights),
        out_specs=rows,
        check_vma=False,
    )
```

```python
import functools

import jax
import jax.numpy as jnp
from jax import lax
from jax.experimental import pallas as pl
from jax.experimental.pallas import tpu as pltpu
from jax.sharding import Mesh
from jax.sharding import PartitionSpec as P

CAP = 72
MESH_ID = pl.DeviceIdType.MESH


def exchange_peers(n_grp):
    me = lax.axis_index("expert") * 2 + lax.axis_index("zhi")
    peers = []
    for s in range(1, n_grp):
        p = lax.rem(me + s, n_grp)
        peers.append((p, {"expert": p // 2, "zhi": lax.rem(p, 2)}))
    return me, peers


def start_exchange(me, peers, x_ref, y_ref, send_sem, recv_sem, local_sem):
    copies = []
    local = pltpu.make_async_copy(x_ref.at[me], y_ref.at[me], local_sem)
    local.start()
    for k, (p, dev) in enumerate(peers):
        cp = pltpu.make_async_remote_copy(
            src_ref=x_ref.at[p],
            dst_ref=y_ref.at[me],
            send_sem=send_sem.at[k],
            recv_sem=recv_sem.at[me],
            device_id=dev,
            device_id_type=MESH_ID,
        )
        cp.start()
        copies.append(cp)
    return local, copies


def finish_exchange(peers, local, copies, x_ref, y_ref, send_sem, recv_sem):
    for k, (p, dev) in enumerate(peers):
        pltpu.make_async_remote_copy(
            src_ref=x_ref.at[0],
            dst_ref=y_ref.at[p],
            send_sem=send_sem.at[k],
            recv_sem=recv_sem.at[p],
            device_id=dev,
            device_id_type=MESH_ID,
        ).wait_recv()
    for cp in copies:
        cp.wait_send()
    local.wait()


def plane_plan(n_grp):
    e_idx = lax.axis_index("expert")
    h = lax.axis_index("zhi")
    c = lax.axis_index("core")
    y = e_idx // 2
    z = h * 2 + lax.rem(e_idx, 2)
    s = 1 - 2 * c

    def at(dy, dz):
        yy = lax.rem(y + dy + 4, 4)
        zz = lax.rem(z + dz + 4, 4)
        p = (yy * 2 + lax.rem(zz, 2)) * 2 + zz // 2
        return p, {"expert": yy * 2 + lax.rem(zz, 2), "zhi": zz // 2}

    direct = [(dy, dz) for dy in (0, 1, 3) for dz in (0, 1, 3) if (dy, dz) != (0, 0)]
    relayed = [((2, dz), (s, 0)) for dz in (0, 1, 3)]
    relayed += [((dy, 2), (0, s)) for dy in (0, 1, 3)]
    relayed += [((2, 2), (s, s))]
    me = (y * 2 + lax.rem(z, 2)) * 2 + z // 2
    return me, at, direct, relayed


def start_plane(n_grp, x_ref, y_ref, stage, send_sem, recv_sem, stage_sem, local_sem):
    me, at, direct, relayed = plane_plan(n_grp)
    copies = []
    local = pltpu.make_async_copy(x_ref.at[me], y_ref.at[me], local_sem)
    local.start()
    k = 0
    for j, (off, rel) in enumerate(relayed):
        p, _ = at(*off)
        _, dev = at(*rel)
        cp = pltpu.make_async_remote_copy(
            src_ref=x_ref.at[p], dst_ref=stage.at[j], send_sem=send_sem.at[k],
            recv_sem=stage_sem.at[j], device_id=dev, device_id_type=MESH_ID,
        )
        cp.start()
        copies.append(cp)
        k += 1
    for off in direct:
        p, dev = at(*off)
        cp = pltpu.make_async_remote_copy(
            src_ref=x_ref.at[p], dst_ref=y_ref.at[me], send_sem=send_sem.at[k],
            recv_sem=recv_sem.at[me], device_id=dev, device_id_type=MESH_ID,
        )
        cp.start()
        copies.append(cp)
        k += 1
    return local, copies, k


def relay_plane(n_grp, k, x_ref, y_ref, stage, send_sem, recv_sem, stage_sem):
    me, at, direct, relayed = plane_plan(n_grp)
    copies = []
    for j, (off, rel) in enumerate(relayed):
        src_p, _ = at(-rel[0], -rel[1])
        _, dev = at(off[0] - rel[0], off[1] - rel[1])
        pltpu.make_async_remote_copy(
            src_ref=x_ref.at[0], dst_ref=stage.at[j], send_sem=send_sem.at[0],
            recv_sem=stage_sem.at[j], device_id=dev, device_id_type=MESH_ID,
        ).wait_recv()
        cp = pltpu.make_async_remote_copy(
            src_ref=stage.at[j], dst_ref=y_ref.at[src_p], send_sem=send_sem.at[k],
            recv_sem=recv_sem.at[src_p], device_id=dev, device_id_type=MESH_ID,
        )
        cp.start()
        copies.append(cp)
        k += 1
    return copies


def plane_devices(n_grp):
    me, at, direct, relayed = plane_plan(n_grp)
    return [at(*off)[1] for off in direct]


def exchange_kernel(n_grp, x_ref, y_ref, send_sem, recv_sem, local_sem):
    me, peers = exchange_peers(n_grp)
    barrier = pltpu.get_barrier_semaphore()
    for p, dev in peers:
        pl.semaphore_signal(barrier, inc=1, device_id=dev, device_id_type=MESH_ID)
    pl.semaphore_wait(barrier, len(peers))
    local, copies = start_exchange(me, peers, x_ref, y_ref, send_sem, recv_sem, local_sem.at[0])
    finish_exchange(peers, local, copies, x_ref, y_ref, send_sem, recv_sem)


def exchange(x, n_grp, collective_id):
    any_spec = pl.BlockSpec(memory_space=pl.ANY)
    return pl.pallas_call(
        functools.partial(exchange_kernel, n_grp),
        out_shape=jax.ShapeDtypeStruct(x.shape, x.dtype),
        in_specs=[any_spec],
        out_specs=any_spec,
        scratch_shapes=[
            pltpu.SemaphoreType.DMA((n_grp,)),
            pltpu.SemaphoreType.DMA((n_grp,)),
            pltpu.SemaphoreType.DMA((1,)),
        ],
        compiler_params=pltpu.CompilerParams(collective_id=collective_id, has_side_effects=True),
        cost_estimate=pl.CostEstimate(flops=0, transcendentals=0, bytes_accessed=2 * x.size * 2),
    )(x)


def expert_return_kernel(n_grp, rows_ref, gate_ref, up_ref, down_ref, y_ref, buf, stage, hid_ref,
                         send_sem, recv_sem, stage_sem, local_sem):
    me, at, direct, relayed = plane_plan(n_grp)
    n_rel = len(relayed)
    order = [off for off, rel in relayed] + direct + [(0, 0)]
    rel_of = [rel for off, rel in relayed]
    barrier = pltpu.get_barrier_semaphore()
    peers = plane_devices(n_grp)
    for dev in peers:
        pl.semaphore_signal(barrier, inc=1, device_id=dev, device_id_type=MESH_ID)

    def pick(k, values):
        out = values[-1]
        for i in range(len(values) - 2, -1, -1):
            out = jnp.where(k == i, values[i], out)
        return out

    def chunk_of(k):
        dy = pick(k, [o[0] for o in order])
        dz = pick(k, [o[1] for o in order])
        return at(dy, dz)

    def project(k):
        p, _ = chunk_of(k)
        cap = buf.shape[1]
        hidden = hid_ref[pl.ds(pl.multiple_of(p * cap, 8), cap)].astype(jnp.bfloat16)
        buf[p] = jnp.dot(hidden, down_ref[...], preferred_element_type=jnp.float32).astype(buf.dtype)

    def first_hop(k):
        p, _ = chunk_of(k)
        ry = pick(k, [r[0] for r in rel_of])
        rz = pick(k, [r[1] for r in rel_of])
        _, dev = at(ry, rz)
        return pltpu.make_async_remote_copy(
            src_ref=buf.at[p], dst_ref=stage.at[k], send_sem=send_sem.at[k],
            recv_sem=stage_sem.at[k], device_id=dev, device_id_type=MESH_ID,
        )

    def direct_send(k):
        p, dev = chunk_of(k)
        return pltpu.make_async_remote_copy(
            src_ref=buf.at[p], dst_ref=y_ref.at[me], send_sem=send_sem.at[k],
            recv_sem=recv_sem.at[me], device_id=dev, device_id_type=MESH_ID,
        )

    def forwards():
        for j, (off, rel) in enumerate(relayed):
            src_p, _ = at(-rel[0], -rel[1])
            _, dev = at(off[0] - rel[0], off[1] - rel[1])
            pltpu.make_async_remote_copy(
                src_ref=buf.at[0], dst_ref=stage.at[j], send_sem=send_sem.at[0],
                recv_sem=stage_sem.at[j], device_id=dev, device_id_type=MESH_ID,
            ).wait_recv()
            pltpu.make_async_remote_copy(
                src_ref=stage.at[j], dst_ref=y_ref.at[src_p], send_sem=send_sem.at[n_grp - 1 + j],
                recv_sem=recv_sem.at[src_p], device_id=dev, device_id_type=MESH_ID,
            ).start()

    n_rows = rows_ref.shape[0]
    piece = n_rows // 2
    nt = (((1,), (1,)), ((), ()))
    for i in range(2):
        r = rows_ref[pl.ds(i * piece, piece)]
        gate_pre = lax.dot_general(r, gate_ref[...], nt, preferred_element_type=jnp.float32)
        up_pre = lax.dot_general(r, up_ref[...], nt, preferred_element_type=jnp.float32)
        hid_ref[pl.ds(i * piece, piece)] = jax.nn.silu(gate_pre) * up_pre

    local = pltpu.make_async_copy(buf.at[me], y_ref.at[me], local_sem.at[0])
    project(0)
    pl.semaphore_wait(barrier, len(peers))

    def step(k, carry):
        project(k)

        @pl.when(k - 1 < n_rel)
        def _():
            first_hop(k - 1).start()

        @pl.when(k - 1 >= n_rel)
        def _():
            direct_send(k - 1).start()

        @pl.when(k == n_rel + 4)
        def _():
            forwards()

        return carry

    lax.fori_loop(1, n_grp, step, 0)
    local.start()

    local.wait()
    for k in range(n_grp - 1):
        if k < n_rel:
            first_hop(k).wait_send()
        else:
            direct_send(k).wait_send()
    for j, (off, rel) in enumerate(relayed):
        _, dev = at(off[0] - rel[0], off[1] - rel[1])
        pltpu.make_async_remote_copy(
            src_ref=stage.at[j], dst_ref=y_ref.at[0], send_sem=send_sem.at[n_grp - 1 + j],
            recv_sem=recv_sem.at[0], device_id=dev, device_id_type=MESH_ID,
        ).wait_send()
    for s in range(1, n_grp):
        q = lax.rem(me + s, n_grp)
        pltpu.make_async_remote_copy(
            src_ref=buf.at[0], dst_ref=y_ref.at[q], send_sem=send_sem.at[0],
            recv_sem=recv_sem.at[q], device_id=peers[0], device_id_type=MESH_ID,
        ).wait_recv()


def expert_return(rows, gate_full, up_full, down_full, n_grp, collective_id):
    n_rows, width = rows.shape
    ff = gate_full.shape[0]
    n_src = n_grp
    cap = n_rows // n_src
    out = jax.ShapeDtypeStruct((n_src, cap, width), jnp.bfloat16)
    vmem = pl.BlockSpec(memory_space=pltpu.VMEM)
    flops = 6 * n_rows * ff * width
    nbytes = rows.size * 2 + 3 * gate_full.size * 2 + 2 * n_rows * width * 2
    return pl.pallas_call(
        functools.partial(expert_return_kernel, n_grp),
        out_shape=out,
        in_specs=[vmem] * 4,
        out_specs=pl.BlockSpec(memory_space=pl.ANY),
        scratch_shapes=[
            pltpu.VMEM((n_src, cap, width), jnp.bfloat16),
            pltpu.VMEM((7, cap, width), jnp.bfloat16),
            pltpu.VMEM((n_rows, ff), jnp.float32),
            pltpu.SemaphoreType.DMA((n_grp + 8,)),
            pltpu.SemaphoreType.DMA((n_grp,)),
            pltpu.SemaphoreType.DMA((7,)),
            pltpu.SemaphoreType.DMA((1,)),
        ],
        compiler_params=pltpu.CompilerParams(
            collective_id=collective_id, has_side_effects=True, vmem_limit_bytes=64 * 1024 * 1024 - 1024 * 1024
        ),
        cost_estimate=pl.CostEstimate(flops=flops, transcendentals=n_rows * ff, bytes_accessed=nbytes),
    )(rows, gate_full, up_full, down_full)


def weight_kernel(n_x, n_grp, g_in, u_in, d_in, t_in, g_out, u_out, d_out, t_out, send_sem, recv_sem,
                  local_sem, t_send, t_recv, stage, stage_sem):
    ins = (g_in, u_in, d_in)
    outs = (g_out, u_out, d_out)
    x = lax.axis_index("x")
    h = lax.axis_index("zhi")
    c = lax.axis_index("core")

    def block(xx, hh, cc):
        return (xx * 2 + hh) * 2 + cc

    me = block(x, h, c)
    up_x = lax.rem(x + 1, n_x)
    down_x = lax.rem(x + n_x - 1, n_x)
    far_x = lax.rem(x + 2, n_x)
    toward = jnp.where(c == 0, up_x, down_x)
    away = jnp.where(c == 0, down_x, up_x)
    partner = {"core": 1 - c}
    z_peer = {"zhi": 1 - h}
    x_devs = [{"x": up_x}, {"x": down_x}]

    t_me, t_peers = exchange_peers(n_grp)
    barrier = pltpu.get_barrier_semaphore()
    greet = [partner, z_peer] + x_devs + plane_devices(n_grp)
    for dev in greet:
        pl.semaphore_signal(barrier, inc=1, device_id=dev, device_id_type=MESH_ID)
    pl.semaphore_wait(barrier, len(greet))

    count = [0]

    def send(src_of, blk, dev):
        k = count[0]
        count[0] += 1
        copies = []
        for m in range(3):
            cp = pltpu.make_async_remote_copy(
                src_ref=src_of(m),
                dst_ref=outs[m].at[blk],
                send_sem=send_sem.at[m, k],
                recv_sem=recv_sem.at[m, blk],
                device_id=dev,
                device_id_type=MESH_ID,
            )
            cp.start()
            copies.append(cp)
        return copies

    def wait_in(blk):
        for m in range(3):
            pltpu.make_async_remote_copy(
                src_ref=ins[m].at[0],
                dst_ref=outs[m].at[blk],
                send_sem=send_sem.at[m, 0],
                recv_sem=recv_sem.at[m, blk],
                device_id=partner,
                device_id_type=MESH_ID,
            ).wait_recv()

    sent = []
    local = []
    for m in range(3):
        cp = pltpu.make_async_copy(ins[m].at[h], outs[m].at[me], local_sem.at[m])
        cp.start()
        local.append(cp)
    sent += send(lambda m: ins[m].at[1 - h], me, z_peer)
    for dev in [partner] + x_devs:
        sent += send(lambda m: ins[m].at[h], me, dev)

    z_blk = block(x, 1 - h, c)
    wait_in(z_blk)
    for dev in [partner] + x_devs:
        sent += send(lambda m: outs[m].at[z_blk], z_blk, dev)
    t_local, t_copies, t_k = start_plane(
        n_grp, t_in, t_out, stage, t_send, t_recv, stage_sem, local_sem.at[3]
    )
    t_copies += relay_plane(n_grp, t_k, t_in, t_out, stage, t_send, t_recv, stage_sem)

    for hh in (h, 1 - h):
        blk = block(away, hh, c)
        wait_in(blk)
        sent += send(lambda m: outs[m].at[blk], blk, partner)
        sent += send(lambda m: outs[m].at[blk], blk, {"x": toward})
    for xp in (toward, far_x):
        for hh in (h, 1 - h):
            blk = block(xp, hh, c)
            wait_in(blk)
            sent += send(lambda m: outs[m].at[blk], blk, partner)

    for xx in range(n_x):
        for hh in (0, 1):
            wait_in(block(xx, hh, 1 - c))

    for cp in sent:
        cp.wait_send()
    for cp in local:
        cp.wait()
    finish_exchange(t_peers, t_local, t_copies, t_in, t_out, t_send, t_recv)


def gather_weights(gate_weight, up_weight, down_weight, outgoing, n_x, n_grp):
    blk_rows, width = gate_weight.shape[1], gate_weight.shape[2]
    n_blocks = n_x * 4
    n_send = 16
    shape = jax.ShapeDtypeStruct((n_blocks, blk_rows, width), gate_weight.dtype)
    any_spec = pl.BlockSpec(memory_space=pl.ANY)
    nbytes = 3 * n_blocks * blk_rows * width * 2
    return pl.pallas_call(
        functools.partial(weight_kernel, n_x, n_grp),
        out_shape=(shape, shape, shape, jax.ShapeDtypeStruct(outgoing.shape, outgoing.dtype)),
        in_specs=[any_spec] * 4,
        out_specs=(any_spec, any_spec, any_spec, any_spec),
        scratch_shapes=[
            pltpu.SemaphoreType.DMA((3, n_send)),
            pltpu.SemaphoreType.DMA((3, n_blocks)),
            pltpu.SemaphoreType.DMA((4,)),
            pltpu.SemaphoreType.DMA((n_grp + 8,)),
            pltpu.SemaphoreType.DMA((n_grp,)),
            pltpu.VMEM((7,) + outgoing.shape[1:], outgoing.dtype),
            pltpu.SemaphoreType.DMA((7,)),
        ],
        compiler_params=pltpu.CompilerParams(collective_id=0, has_side_effects=True),
        cost_estimate=pl.CostEstimate(flops=0, transcendentals=0, bytes_accessed=nbytes),
    )(gate_weight, up_weight, down_weight, outgoing)


def per_device(tokens, expert_ids, combine, gate_weight, up_weight, down_weight):
    n_x = lax.axis_size("x")
    assert n_x == 4
    per_group = gate_weight.shape[0]
    groups = lax.axis_size("expert")
    n_expert = per_group * groups
    n_grp = groups * 2
    assert n_grp == 16
    tok_rows, top_k = expert_ids.shape
    model_width = tokens.shape[1]
    n_slot = n_expert * CAP

    flat_ids = expert_ids.reshape(-1)
    onehot = (flat_ids[:, None] == jnp.arange(n_expert, dtype=jnp.int32)[None, :]).astype(jnp.int32)
    n_pair = flat_ids.shape[0]
    before = (
        lax.broadcasted_iota(jnp.int32, (n_pair, n_pair), 0)
        > lax.broadcasted_iota(jnp.int32, (n_pair, n_pair), 1)
    ).astype(jnp.bfloat16)
    earlier = jnp.dot(before, onehot.astype(jnp.bfloat16), preferred_element_type=jnp.float32)
    earlier = earlier.astype(jnp.int32)
    rank_within = jnp.sum(earlier * onehot, axis=1)
    slot_index = (flat_ids * CAP + rank_within).reshape(tok_rows, top_k)
    slot_col = lax.broadcasted_iota(jnp.int32, (n_slot, tok_rows), 0)
    pick = sum(
        (slot_index[:, k][None, :] == slot_col).astype(jnp.bfloat16) for k in range(top_k)
    )
    outgoing = jnp.dot(pick, tokens, preferred_element_type=jnp.float32).astype(jnp.bfloat16)
    outgoing = outgoing.reshape(n_expert, CAP, model_width)

    g_all, u_all, d_all, arrived = gather_weights(
        gate_weight, up_weight, down_weight, outgoing, n_x, n_grp
    )
    gate_full = g_all.reshape(-1, model_width)
    up_full = u_all.reshape(-1, model_width)
    down_full = d_all.reshape(-1, model_width)
    returned = expert_return(
        arrived.reshape(n_slot, model_width), gate_full, up_full, down_full, n_grp, 1
    )
    returned = returned.reshape(n_slot, model_width)

    slot_row = lax.broadcasted_iota(jnp.int32, (tok_rows, n_slot), 1)
    weight_of = sum(
        jnp.where(slot_index[:, k][:, None] == slot_row, combine[:, k][:, None], 0.0)
        for k in range(top_k)
    )
    weight_top = lax.reduce_precision(weight_of, exponent_bits=8, mantissa_bits=7)
    weight_hi = weight_top.astype(jnp.bfloat16)
    weight_lo = (weight_of - weight_top).astype(jnp.bfloat16)
    both = jnp.dot(
        jnp.concatenate([weight_hi, weight_lo], axis=0), returned, preferred_element_type=jnp.float32
    )
    mixed = both[:tok_rows] + both[tok_rows:]
    return mixed.astype(jnp.bfloat16)


def solution(mesh):
    groups = mesh.shape["expert"]
    n_x = mesh.shape["fsdp"] // 4
    inner = Mesh(mesh.devices.reshape(groups, n_x, 2, 2), ("expert", "x", "zhi", "core"))
    rows = P(("expert", "x", "zhi", "core"), None)
    weights = P("expert", ("x", "zhi", "core"), None)
    return jax.shard_map(
        per_device,
        mesh=inner,
        in_specs=(rows, rows, rows, weights, weights, weights),
        out_specs=rows,
        check_vma=False,
    )
```

```python
import functools

import jax
import jax.numpy as jnp
from jax import lax
from jax.experimental import pallas as pl
from jax.experimental.pallas import tpu as pltpu
from jax.sharding import Mesh
from jax.sharding import PartitionSpec as P

CAP = 72
MESH_ID = pl.DeviceIdType.MESH


def exchange_peers(n_grp):
    me = lax.axis_index("expert") * 2 + lax.axis_index("zhi")
    peers = []
    for s in range(1, n_grp):
        p = lax.rem(me + s, n_grp)
        peers.append((p, {"expert": p // 2, "zhi": lax.rem(p, 2)}))
    return me, peers


def start_exchange(me, peers, x_ref, y_ref, send_sem, recv_sem, local_sem):
    copies = []
    local = pltpu.make_async_copy(x_ref.at[me], y_ref.at[me], local_sem)
    local.start()
    for k, (p, dev) in enumerate(peers):
        cp = pltpu.make_async_remote_copy(
            src_ref=x_ref.at[p],
            dst_ref=y_ref.at[me],
            send_sem=send_sem.at[k],
            recv_sem=recv_sem.at[me],
            device_id=dev,
            device_id_type=MESH_ID,
        )
        cp.start()
        copies.append(cp)
    return local, copies


def finish_exchange(peers, local, copies, x_ref, y_ref, send_sem, recv_sem):
    for k, (p, dev) in enumerate(peers):
        pltpu.make_async_remote_copy(
            src_ref=x_ref.at[0],
            dst_ref=y_ref.at[p],
            send_sem=send_sem.at[k],
            recv_sem=recv_sem.at[p],
            device_id=dev,
            device_id_type=MESH_ID,
        ).wait_recv()
    for cp in copies:
        cp.wait_send()
    local.wait()


def plane_plan(n_grp):
    e_idx = lax.axis_index("expert")
    h = lax.axis_index("zhi")
    c = lax.axis_index("core")
    y = e_idx // 2
    z = h * 2 + lax.rem(e_idx, 2)
    s = 1 - 2 * c

    def at(dy, dz):
        yy = lax.rem(y + dy + 4, 4)
        zz = lax.rem(z + dz + 4, 4)
        p = (yy * 2 + lax.rem(zz, 2)) * 2 + zz // 2
        return p, {"expert": yy * 2 + lax.rem(zz, 2), "zhi": zz // 2}

    direct = [(dy, dz) for dy in (0, 1, 3) for dz in (0, 1, 3) if (dy, dz) != (0, 0)]
    relayed = [((2, dz), (s, 0)) for dz in (0, 1, 3)]
    relayed += [((dy, 2), (0, s)) for dy in (0, 1, 3)]
    relayed += [((2, 2), (s, s))]
    me = (y * 2 + lax.rem(z, 2)) * 2 + z // 2
    return me, at, direct, relayed


def start_plane(n_grp, x_ref, y_ref, stage, send_sem, recv_sem, stage_sem, local_sem):
    me, at, direct, relayed = plane_plan(n_grp)
    copies = []
    local = pltpu.make_async_copy(x_ref.at[me], y_ref.at[me], local_sem)
    local.start()
    k = 0
    for j, (off, rel) in enumerate(relayed):
        p, _ = at(*off)
        _, dev = at(*rel)
        cp = pltpu.make_async_remote_copy(
            src_ref=x_ref.at[p], dst_ref=stage.at[j], send_sem=send_sem.at[k],
            recv_sem=stage_sem.at[j], device_id=dev, device_id_type=MESH_ID,
        )
        cp.start()
        copies.append(cp)
        k += 1
    for off in direct:
        p, dev = at(*off)
        cp = pltpu.make_async_remote_copy(
            src_ref=x_ref.at[p], dst_ref=y_ref.at[me], send_sem=send_sem.at[k],
            recv_sem=recv_sem.at[me], device_id=dev, device_id_type=MESH_ID,
        )
        cp.start()
        copies.append(cp)
        k += 1
    return local, copies, k


def relay_plane(n_grp, k, x_ref, y_ref, stage, send_sem, recv_sem, stage_sem):
    me, at, direct, relayed = plane_plan(n_grp)
    copies = []
    for j, (off, rel) in enumerate(relayed):
        src_p, _ = at(-rel[0], -rel[1])
        _, dev = at(off[0] - rel[0], off[1] - rel[1])
        pltpu.make_async_remote_copy(
            src_ref=x_ref.at[0], dst_ref=stage.at[j], send_sem=send_sem.at[0],
            recv_sem=stage_sem.at[j], device_id=dev, device_id_type=MESH_ID,
        ).wait_recv()
        cp = pltpu.make_async_remote_copy(
            src_ref=stage.at[j], dst_ref=y_ref.at[src_p], send_sem=send_sem.at[k],
            recv_sem=recv_sem.at[src_p], device_id=dev, device_id_type=MESH_ID,
        )
        cp.start()
        copies.append(cp)
        k += 1
    return copies


def plane_devices(n_grp):
    me, at, direct, relayed = plane_plan(n_grp)
    return [at(*off)[1] for off in direct]


def exchange_kernel(n_grp, x_ref, y_ref, send_sem, recv_sem, local_sem):
    me, peers = exchange_peers(n_grp)
    barrier = pltpu.get_barrier_semaphore()
    for p, dev in peers:
        pl.semaphore_signal(barrier, inc=1, device_id=dev, device_id_type=MESH_ID)
    pl.semaphore_wait(barrier, len(peers))
    local, copies = start_exchange(me, peers, x_ref, y_ref, send_sem, recv_sem, local_sem.at[0])
    finish_exchange(peers, local, copies, x_ref, y_ref, send_sem, recv_sem)


def exchange(x, n_grp, collective_id):
    any_spec = pl.BlockSpec(memory_space=pl.ANY)
    return pl.pallas_call(
        functools.partial(exchange_kernel, n_grp),
        out_shape=jax.ShapeDtypeStruct(x.shape, x.dtype),
        in_specs=[any_spec],
        out_specs=any_spec,
        scratch_shapes=[
            pltpu.SemaphoreType.DMA((n_grp,)),
            pltpu.SemaphoreType.DMA((n_grp,)),
            pltpu.SemaphoreType.DMA((1,)),
        ],
        compiler_params=pltpu.CompilerParams(collective_id=collective_id, has_side_effects=True),
        cost_estimate=pl.CostEstimate(flops=0, transcendentals=0, bytes_accessed=2 * x.size * 2),
    )(x)


def expert_return_kernel(n_grp, rows_ref, gate_ref, up_ref, down_ref, y_ref, buf, stage, hid_ref,
                         send_sem, recv_sem, stage_sem, local_sem):
    me, at, direct, relayed = plane_plan(n_grp)
    n_rel = len(relayed)
    order = [off for off, rel in relayed] + direct + [(0, 0)]
    rel_of = [rel for off, rel in relayed]
    barrier = pltpu.get_barrier_semaphore()
    peers = plane_devices(n_grp)
    for dev in peers:
        pl.semaphore_signal(barrier, inc=1, device_id=dev, device_id_type=MESH_ID)

    def pick(k, values):
        out = values[-1]
        for i in range(len(values) - 2, -1, -1):
            out = jnp.where(k == i, values[i], out)
        return out

    def chunk_of(k):
        dy = pick(k, [o[0] for o in order])
        dz = pick(k, [o[1] for o in order])
        return at(dy, dz)

    def project(k):
        p, _ = chunk_of(k)
        cap = buf.shape[1]
        hidden = hid_ref[pl.ds(pl.multiple_of(p * cap, 8), cap)].astype(jnp.bfloat16)
        buf[p] = jnp.dot(hidden, down_ref[...], preferred_element_type=jnp.float32).astype(buf.dtype)

    def first_hop(k):
        p, _ = chunk_of(k)
        ry = pick(k, [r[0] for r in rel_of])
        rz = pick(k, [r[1] for r in rel_of])
        _, dev = at(ry, rz)
        return pltpu.make_async_remote_copy(
            src_ref=buf.at[p], dst_ref=stage.at[k], send_sem=send_sem.at[k],
            recv_sem=stage_sem.at[k], device_id=dev, device_id_type=MESH_ID,
        )

    def direct_send(k):
        p, dev = chunk_of(k)
        return pltpu.make_async_remote_copy(
            src_ref=buf.at[p], dst_ref=y_ref.at[me], send_sem=send_sem.at[k],
            recv_sem=recv_sem.at[me], device_id=dev, device_id_type=MESH_ID,
        )

    def forwards():
        for j, (off, rel) in enumerate(relayed):
            src_p, _ = at(-rel[0], -rel[1])
            _, dev = at(off[0] - rel[0], off[1] - rel[1])
            pltpu.make_async_remote_copy(
                src_ref=buf.at[0], dst_ref=stage.at[j], send_sem=send_sem.at[0],
                recv_sem=stage_sem.at[j], device_id=dev, device_id_type=MESH_ID,
            ).wait_recv()
            pltpu.make_async_remote_copy(
                src_ref=stage.at[j], dst_ref=y_ref.at[src_p], send_sem=send_sem.at[n_grp - 1 + j],
                recv_sem=recv_sem.at[src_p], device_id=dev, device_id_type=MESH_ID,
            ).start()

    n_rows = rows_ref.shape[0]
    piece = n_rows
    nt = (((1,), (1,)), ((), ()))
    for i in range(1):
        r = rows_ref[pl.ds(i * piece, piece)]
        gate_pre = lax.dot_general(r, gate_ref[...], nt, preferred_element_type=jnp.float32)
        up_pre = lax.dot_general(r, up_ref[...], nt, preferred_element_type=jnp.float32)
        hid_ref[pl.ds(i * piece, piece)] = jax.nn.silu(gate_pre) * up_pre

    local = pltpu.make_async_copy(buf.at[me], y_ref.at[me], local_sem.at[0])
    project(0)
    pl.semaphore_wait(barrier, len(peers))

    def step(k, carry):
        project(k)

        @pl.when(k - 1 < n_rel)
        def _():
            first_hop(k - 1).start()

        @pl.when(k - 1 >= n_rel)
        def _():
            direct_send(k - 1).start()

        @pl.when(k == n_rel + 4)
        def _():
            forwards()

        return carry

    lax.fori_loop(1, n_grp, step, 0)
    local.start()

    local.wait()
    for k in range(n_grp - 1):
        if k < n_rel:
            first_hop(k).wait_send()
        else:
            direct_send(k).wait_send()
    for j, (off, rel) in enumerate(relayed):
        _, dev = at(off[0] - rel[0], off[1] - rel[1])
        pltpu.make_async_remote_copy(
            src_ref=stage.at[j], dst_ref=y_ref.at[0], send_sem=send_sem.at[n_grp - 1 + j],
            recv_sem=recv_sem.at[0], device_id=dev, device_id_type=MESH_ID,
        ).wait_send()
    for s in range(1, n_grp):
        q = lax.rem(me + s, n_grp)
        pltpu.make_async_remote_copy(
            src_ref=buf.at[0], dst_ref=y_ref.at[q], send_sem=send_sem.at[0],
            recv_sem=recv_sem.at[q], device_id=peers[0], device_id_type=MESH_ID,
        ).wait_recv()


def expert_return(rows, gate_full, up_full, down_full, n_grp, collective_id):
    n_rows, width = rows.shape
    ff = gate_full.shape[0]
    n_src = n_grp
    cap = n_rows // n_src
    out = jax.ShapeDtypeStruct((n_src, cap, width), jnp.bfloat16)
    vmem = pl.BlockSpec(memory_space=pltpu.VMEM)
    flops = 6 * n_rows * ff * width
    nbytes = rows.size * 2 + 3 * gate_full.size * 2 + 2 * n_rows * width * 2
    return pl.pallas_call(
        functools.partial(expert_return_kernel, n_grp),
        out_shape=out,
        in_specs=[vmem] * 4,
        out_specs=pl.BlockSpec(memory_space=pl.ANY),
        scratch_shapes=[
            pltpu.VMEM((n_src, cap, width), jnp.bfloat16),
            pltpu.VMEM((7, cap, width), jnp.bfloat16),
            pltpu.VMEM((n_rows, ff), jnp.float32),
            pltpu.SemaphoreType.DMA((n_grp + 8,)),
            pltpu.SemaphoreType.DMA((n_grp,)),
            pltpu.SemaphoreType.DMA((7,)),
            pltpu.SemaphoreType.DMA((1,)),
        ],
        compiler_params=pltpu.CompilerParams(
            collective_id=collective_id, has_side_effects=True, vmem_limit_bytes=64 * 1024 * 1024 - 1024 * 1024
        ),
        cost_estimate=pl.CostEstimate(flops=flops, transcendentals=n_rows * ff, bytes_accessed=nbytes),
    )(rows, gate_full, up_full, down_full)


def weight_kernel(n_x, n_grp, g_in, u_in, d_in, t_in, g_out, u_out, d_out, t_out, send_sem, recv_sem,
                  local_sem, t_send, t_recv, stage, stage_sem):
    ins = (g_in, u_in, d_in)
    outs = (g_out, u_out, d_out)
    x = lax.axis_index("x")
    h = lax.axis_index("zhi")
    c = lax.axis_index("core")

    def block(xx, hh, cc):
        return (xx * 2 + hh) * 2 + cc

    me = block(x, h, c)
    up_x = lax.rem(x + 1, n_x)
    down_x = lax.rem(x + n_x - 1, n_x)
    far_x = lax.rem(x + 2, n_x)
    toward = jnp.where(c == 0, up_x, down_x)
    away = jnp.where(c == 0, down_x, up_x)
    partner = {"core": 1 - c}
    z_peer = {"zhi": 1 - h}
    x_devs = [{"x": up_x}, {"x": down_x}]

    t_me, t_peers = exchange_peers(n_grp)
    barrier = pltpu.get_barrier_semaphore()
    greet = [partner, z_peer] + x_devs + plane_devices(n_grp)
    for dev in greet:
        pl.semaphore_signal(barrier, inc=1, device_id=dev, device_id_type=MESH_ID)
    pl.semaphore_wait(barrier, len(greet))

    count = [0]

    def send(src_of, blk, dev):
        k = count[0]
        count[0] += 1
        copies = []
        for m in range(3):
            cp = pltpu.make_async_remote_copy(
                src_ref=src_of(m),
                dst_ref=outs[m].at[blk],
                send_sem=send_sem.at[m, k],
                recv_sem=recv_sem.at[m, blk],
                device_id=dev,
                device_id_type=MESH_ID,
            )
            cp.start()
            copies.append(cp)
        return copies

    def wait_in(blk):
        for m in range(3):
            pltpu.make_async_remote_copy(
                src_ref=ins[m].at[0],
                dst_ref=outs[m].at[blk],
                send_sem=send_sem.at[m, 0],
                recv_sem=recv_sem.at[m, blk],
                device_id=partner,
                device_id_type=MESH_ID,
            ).wait_recv()

    sent = []
    local = []
    for m in range(3):
        cp = pltpu.make_async_copy(ins[m].at[h], outs[m].at[me], local_sem.at[m])
        cp.start()
        local.append(cp)
    sent += send(lambda m: ins[m].at[1 - h], me, z_peer)
    for dev in [partner] + x_devs:
        sent += send(lambda m: ins[m].at[h], me, dev)

    z_blk = block(x, 1 - h, c)
    wait_in(z_blk)
    for dev in [partner] + x_devs:
        sent += send(lambda m: outs[m].at[z_blk], z_blk, dev)
    t_local, t_copies, t_k = start_plane(
        n_grp, t_in, t_out, stage, t_send, t_recv, stage_sem, local_sem.at[3]
    )
    t_copies += relay_plane(n_grp, t_k, t_in, t_out, stage, t_send, t_recv, stage_sem)

    for hh in (h, 1 - h):
        blk = block(away, hh, c)
        wait_in(blk)
        sent += send(lambda m: outs[m].at[blk], blk, partner)
        sent += send(lambda m: outs[m].at[blk], blk, {"x": toward})
    for xp in (toward, far_x):
        for hh in (h, 1 - h):
            blk = block(xp, hh, c)
            wait_in(blk)
            sent += send(lambda m: outs[m].at[blk], blk, partner)

    for xx in range(n_x):
        for hh in (0, 1):
            wait_in(block(xx, hh, 1 - c))

    for cp in sent:
        cp.wait_send()
    for cp in local:
        cp.wait()
    finish_exchange(t_peers, t_local, t_copies, t_in, t_out, t_send, t_recv)


def gather_weights(gate_weight, up_weight, down_weight, outgoing, n_x, n_grp):
    blk_rows, width = gate_weight.shape[1], gate_weight.shape[2]
    n_blocks = n_x * 4
    n_send = 16
    shape = jax.ShapeDtypeStruct((n_blocks, blk_rows, width), gate_weight.dtype)
    any_spec = pl.BlockSpec(memory_space=pl.ANY)
    nbytes = 3 * n_blocks * blk_rows * width * 2
    return pl.pallas_call(
        functools.partial(weight_kernel, n_x, n_grp),
        out_shape=(shape, shape, shape, jax.ShapeDtypeStruct(outgoing.shape, outgoing.dtype)),
        in_specs=[any_spec] * 4,
        out_specs=(any_spec, any_spec, any_spec, any_spec),
        scratch_shapes=[
            pltpu.SemaphoreType.DMA((3, n_send)),
            pltpu.SemaphoreType.DMA((3, n_blocks)),
            pltpu.SemaphoreType.DMA((4,)),
            pltpu.SemaphoreType.DMA((n_grp + 8,)),
            pltpu.SemaphoreType.DMA((n_grp,)),
            pltpu.VMEM((7,) + outgoing.shape[1:], outgoing.dtype),
            pltpu.SemaphoreType.DMA((7,)),
        ],
        compiler_params=pltpu.CompilerParams(collective_id=0, has_side_effects=True),
        cost_estimate=pl.CostEstimate(flops=0, transcendentals=0, bytes_accessed=nbytes),
    )(gate_weight, up_weight, down_weight, outgoing)


def per_device(tokens, expert_ids, combine, gate_weight, up_weight, down_weight):
    n_x = lax.axis_size("x")
    assert n_x == 4
    per_group = gate_weight.shape[0]
    groups = lax.axis_size("expert")
    n_expert = per_group * groups
    n_grp = groups * 2
    assert n_grp == 16
    tok_rows, top_k = expert_ids.shape
    model_width = tokens.shape[1]
    n_slot = n_expert * CAP

    flat_ids = expert_ids.reshape(-1)
    onehot = (flat_ids[:, None] == jnp.arange(n_expert, dtype=jnp.int32)[None, :]).astype(jnp.int32)
    n_pair = flat_ids.shape[0]
    before = (
        lax.broadcasted_iota(jnp.int32, (n_pair, n_pair), 0)
        > lax.broadcasted_iota(jnp.int32, (n_pair, n_pair), 1)
    ).astype(jnp.bfloat16)
    earlier = jnp.dot(before, onehot.astype(jnp.bfloat16), preferred_element_type=jnp.float32)
    earlier = earlier.astype(jnp.int32)
    rank_within = jnp.sum(earlier * onehot, axis=1)
    slot_index = (flat_ids * CAP + rank_within).reshape(tok_rows, top_k)
    slot_col = lax.broadcasted_iota(jnp.int32, (n_slot, tok_rows), 0)
    pick = sum(
        (slot_index[:, k][None, :] == slot_col).astype(jnp.bfloat16) for k in range(top_k)
    )
    outgoing = jnp.dot(pick, tokens, preferred_element_type=jnp.float32).astype(jnp.bfloat16)
    outgoing = outgoing.reshape(n_expert, CAP, model_width)

    g_all, u_all, d_all, arrived = gather_weights(
        gate_weight, up_weight, down_weight, outgoing, n_x, n_grp
    )
    gate_full = g_all.reshape(-1, model_width)
    up_full = u_all.reshape(-1, model_width)
    down_full = d_all.reshape(-1, model_width)
    returned = expert_return(
        arrived.reshape(n_slot, model_width), gate_full, up_full, down_full, n_grp, 1
    )
    returned = returned.reshape(n_slot, model_width)

    slot_row = lax.broadcasted_iota(jnp.int32, (tok_rows, n_slot), 1)
    weight_of = sum(
        jnp.where(slot_index[:, k][:, None] == slot_row, combine[:, k][:, None], 0.0)
        for k in range(top_k)
    )
    weight_top = lax.reduce_precision(weight_of, exponent_bits=8, mantissa_bits=7)
    weight_hi = weight_top.astype(jnp.bfloat16)
    weight_lo = (weight_of - weight_top).astype(jnp.bfloat16)
    both = jnp.dot(
        jnp.concatenate([weight_hi, weight_lo], axis=0), returned, preferred_element_type=jnp.float32
    )
    mixed = both[:tok_rows] + both[tok_rows:]
    return mixed.astype(jnp.bfloat16)


def solution(mesh):
    groups = mesh.shape["expert"]
    n_x = mesh.shape["fsdp"] // 4
    inner = Mesh(mesh.devices.reshape(groups, n_x, 2, 2), ("expert", "x", "zhi", "core"))
    rows = P(("expert", "x", "zhi", "core"), None)
    weights = P("expert", ("x", "zhi", "core"), None)
    return jax.shard_map(
        per_device,
        mesh=inner,
        in_specs=(rows, rows, rows, weights, weights, weights),
        out_specs=rows,
        check_vma=False,
    )
```

```python
import functools

import jax
import jax.numpy as jnp
from jax import lax
from jax.experimental import pallas as pl
from jax.experimental.pallas import tpu as pltpu
from jax.sharding import Mesh
from jax.sharding import PartitionSpec as P

CAP = 72
MESH_ID = pl.DeviceIdType.MESH


def exchange_peers(n_grp):
    me = lax.axis_index("expert") * 2 + lax.axis_index("zhi")
    peers = []
    for s in range(1, n_grp):
        p = lax.rem(me + s, n_grp)
        peers.append((p, {"expert": p // 2, "zhi": lax.rem(p, 2)}))
    return me, peers


def start_exchange(me, peers, x_ref, y_ref, send_sem, recv_sem, local_sem):
    copies = []
    local = pltpu.make_async_copy(x_ref.at[me], y_ref.at[me], local_sem)
    local.start()
    for k, (p, dev) in enumerate(peers):
        cp = pltpu.make_async_remote_copy(
            src_ref=x_ref.at[p],
            dst_ref=y_ref.at[me],
            send_sem=send_sem.at[k],
            recv_sem=recv_sem.at[me],
            device_id=dev,
            device_id_type=MESH_ID,
        )
        cp.start()
        copies.append(cp)
    return local, copies


def finish_exchange(peers, local, copies, x_ref, y_ref, send_sem, recv_sem):
    for k, (p, dev) in enumerate(peers):
        pltpu.make_async_remote_copy(
            src_ref=x_ref.at[0],
            dst_ref=y_ref.at[p],
            send_sem=send_sem.at[k],
            recv_sem=recv_sem.at[p],
            device_id=dev,
            device_id_type=MESH_ID,
        ).wait_recv()
    for cp in copies:
        cp.wait_send()
    local.wait()


def plane_plan(n_grp):
    e_idx = lax.axis_index("expert")
    h = lax.axis_index("zhi")
    c = lax.axis_index("core")
    y = e_idx // 2
    z = h * 2 + lax.rem(e_idx, 2)
    s = 1 - 2 * c

    def at(dy, dz):
        yy = lax.rem(y + dy + 4, 4)
        zz = lax.rem(z + dz + 4, 4)
        p = (yy * 2 + lax.rem(zz, 2)) * 2 + zz // 2
        return p, {"expert": yy * 2 + lax.rem(zz, 2), "zhi": zz // 2}

    direct = [(dy, dz) for dy in (0, 1, 3) for dz in (0, 1, 3) if (dy, dz) != (0, 0)]
    relayed = [((2, dz), (s, 0)) for dz in (0, 1, 3)]
    relayed += [((dy, 2), (0, s)) for dy in (0, 1, 3)]
    relayed += [((2, 2), (s, s))]
    me = (y * 2 + lax.rem(z, 2)) * 2 + z // 2
    return me, at, direct, relayed


def start_plane(n_grp, x_ref, y_ref, stage, send_sem, recv_sem, stage_sem, local_sem):
    me, at, direct, relayed = plane_plan(n_grp)
    copies = []
    local = pltpu.make_async_copy(x_ref.at[me], y_ref.at[me], local_sem)
    local.start()
    k = 0
    for off in direct:
        p, dev = at(*off)
        cp = pltpu.make_async_remote_copy(
            src_ref=x_ref.at[p], dst_ref=y_ref.at[me], send_sem=send_sem.at[k],
            recv_sem=recv_sem.at[me], device_id=dev, device_id_type=MESH_ID,
        )
        cp.start()
        copies.append(cp)
        k += 1
    for j, (off, rel) in enumerate(relayed):
        p, _ = at(*off)
        _, dev = at(*rel)
        cp = pltpu.make_async_remote_copy(
            src_ref=x_ref.at[p], dst_ref=stage.at[j], send_sem=send_sem.at[k],
            recv_sem=stage_sem.at[j], device_id=dev, device_id_type=MESH_ID,
        )
        cp.start()
        copies.append(cp)
        k += 1
    return local, copies, k


def relay_plane(n_grp, k, x_ref, y_ref, stage, send_sem, recv_sem, stage_sem):
    me, at, direct, relayed = plane_plan(n_grp)
    copies = []
    for j, (off, rel) in enumerate(relayed):
        src_p, _ = at(-rel[0], -rel[1])
        _, dev = at(off[0] - rel[0], off[1] - rel[1])
        pltpu.make_async_remote_copy(
            src_ref=x_ref.at[0], dst_ref=stage.at[j], send_sem=send_sem.at[0],
            recv_sem=stage_sem.at[j], device_id=dev, device_id_type=MESH_ID,
        ).wait_recv()
        cp = pltpu.make_async_remote_copy(
            src_ref=stage.at[j], dst_ref=y_ref.at[src_p], send_sem=send_sem.at[k],
            recv_sem=recv_sem.at[src_p], device_id=dev, device_id_type=MESH_ID,
        )
        cp.start()
        copies.append(cp)
        k += 1
    return copies


def plane_devices(n_grp):
    me, at, direct, relayed = plane_plan(n_grp)
    return [at(*off)[1] for off in direct]


def exchange_kernel(n_grp, x_ref, y_ref, send_sem, recv_sem, local_sem):
    me, peers = exchange_peers(n_grp)
    barrier = pltpu.get_barrier_semaphore()
    for p, dev in peers:
        pl.semaphore_signal(barrier, inc=1, device_id=dev, device_id_type=MESH_ID)
    pl.semaphore_wait(barrier, len(peers))
    local, copies = start_exchange(me, peers, x_ref, y_ref, send_sem, recv_sem, local_sem.at[0])
    finish_exchange(peers, local, copies, x_ref, y_ref, send_sem, recv_sem)


def exchange(x, n_grp, collective_id):
    any_spec = pl.BlockSpec(memory_space=pl.ANY)
    return pl.pallas_call(
        functools.partial(exchange_kernel, n_grp),
        out_shape=jax.ShapeDtypeStruct(x.shape, x.dtype),
        in_specs=[any_spec],
        out_specs=any_spec,
        scratch_shapes=[
            pltpu.SemaphoreType.DMA((n_grp,)),
            pltpu.SemaphoreType.DMA((n_grp,)),
            pltpu.SemaphoreType.DMA((1,)),
        ],
        compiler_params=pltpu.CompilerParams(collective_id=collective_id, has_side_effects=True),
        cost_estimate=pl.CostEstimate(flops=0, transcendentals=0, bytes_accessed=2 * x.size * 2),
    )(x)


def expert_return_kernel(n_grp, rows_ref, gate_ref, up_ref, down_ref, y_ref, buf, stage, hid_ref,
                         send_sem, recv_sem, stage_sem, local_sem):
    me, at, direct, relayed = plane_plan(n_grp)
    n_rel = len(relayed)
    order = [off for off, rel in relayed] + direct + [(0, 0)]
    rel_of = [rel for off, rel in relayed]
    barrier = pltpu.get_barrier_semaphore()
    peers = plane_devices(n_grp)
    for dev in peers:
        pl.semaphore_signal(barrier, inc=1, device_id=dev, device_id_type=MESH_ID)

    def pick(k, values):
        out = values[-1]
        for i in range(len(values) - 2, -1, -1):
            out = jnp.where(k == i, values[i], out)
        return out

    def chunk_of(k):
        dy = pick(k, [o[0] for o in order])
        dz = pick(k, [o[1] for o in order])
        return at(dy, dz)

    def project(k):
        p, _ = chunk_of(k)
        cap = buf.shape[1]
        hidden = hid_ref[pl.ds(pl.multiple_of(p * cap, 8), cap)].astype(jnp.bfloat16)
        buf[p] = jnp.dot(hidden, down_ref[...], preferred_element_type=jnp.float32).astype(buf.dtype)

    def first_hop(k):
        p, _ = chunk_of(k)
        ry = pick(k, [r[0] for r in rel_of])
        rz = pick(k, [r[1] for r in rel_of])
        _, dev = at(ry, rz)
        return pltpu.make_async_remote_copy(
            src_ref=buf.at[p], dst_ref=stage.at[k], send_sem=send_sem.at[k],
            recv_sem=stage_sem.at[k], device_id=dev, device_id_type=MESH_ID,
        )

    def direct_send(k):
        p, dev = chunk_of(k)
        return pltpu.make_async_remote_copy(
            src_ref=buf.at[p], dst_ref=y_ref.at[me], send_sem=send_sem.at[k],
            recv_sem=recv_sem.at[me], device_id=dev, device_id_type=MESH_ID,
        )

    def forwards():
        for j, (off, rel) in enumerate(relayed):
            src_p, _ = at(-rel[0], -rel[1])
            _, dev = at(off[0] - rel[0], off[1] - rel[1])
            pltpu.make_async_remote_copy(
                src_ref=buf.at[0], dst_ref=stage.at[j], send_sem=send_sem.at[0],
                recv_sem=stage_sem.at[j], device_id=dev, device_id_type=MESH_ID,
            ).wait_recv()
            pltpu.make_async_remote_copy(
                src_ref=stage.at[j], dst_ref=y_ref.at[src_p], send_sem=send_sem.at[n_grp - 1 + j],
                recv_sem=recv_sem.at[src_p], device_id=dev, device_id_type=MESH_ID,
            ).start()

    n_rows = rows_ref.shape[0]
    piece = n_rows // 2
    nt = (((1,), (1,)), ((), ()))
    for i in range(2):
        r = rows_ref[pl.ds(i * piece, piece)]
        gate_pre = lax.dot_general(r, gate_ref[...], nt, preferred_element_type=jnp.float32)
        up_pre = lax.dot_general(r, up_ref[...], nt, preferred_element_type=jnp.float32)
        hid_ref[pl.ds(i * piece, piece)] = jax.nn.silu(gate_pre) * up_pre

    local = pltpu.make_async_copy(buf.at[me], y_ref.at[me], local_sem.at[0])
    project(0)
    pl.semaphore_wait(barrier, len(peers))

    def step(k, carry):
        project(k)

        @pl.when(k - 1 < n_rel)
        def _():
            first_hop(k - 1).start()

        @pl.when(k - 1 >= n_rel)
        def _():
            direct_send(k - 1).start()

        @pl.when(k == n_rel + 4)
        def _():
            forwards()

        return carry

    lax.fori_loop(1, n_grp, step, 0)
    local.start()

    local.wait()
    for k in range(n_grp - 1):
        if k < n_rel:
            first_hop(k).wait_send()
        else:
            direct_send(k).wait_send()
    for j, (off, rel) in enumerate(relayed):
        _, dev = at(off[0] - rel[0], off[1] - rel[1])
        pltpu.make_async_remote_copy(
            src_ref=stage.at[j], dst_ref=y_ref.at[0], send_sem=send_sem.at[n_grp - 1 + j],
            recv_sem=recv_sem.at[0], device_id=dev, device_id_type=MESH_ID,
        ).wait_send()
    for s in range(1, n_grp):
        q = lax.rem(me + s, n_grp)
        pltpu.make_async_remote_copy(
            src_ref=buf.at[0], dst_ref=y_ref.at[q], send_sem=send_sem.at[0],
            recv_sem=recv_sem.at[q], device_id=peers[0], device_id_type=MESH_ID,
        ).wait_recv()


def expert_return(rows, gate_full, up_full, down_full, n_grp, collective_id):
    n_rows, width = rows.shape
    ff = gate_full.shape[0]
    n_src = n_grp
    cap = n_rows // n_src
    out = jax.ShapeDtypeStruct((n_src, cap, width), jnp.bfloat16)
    vmem = pl.BlockSpec(memory_space=pltpu.VMEM)
    flops = 6 * n_rows * ff * width
    nbytes = rows.size * 2 + 3 * gate_full.size * 2 + 2 * n_rows * width * 2
    return pl.pallas_call(
        functools.partial(expert_return_kernel, n_grp),
        out_shape=out,
        in_specs=[vmem] * 4,
        out_specs=pl.BlockSpec(memory_space=pl.ANY),
        scratch_shapes=[
            pltpu.VMEM((n_src, cap, width), jnp.bfloat16),
            pltpu.VMEM((7, cap, width), jnp.bfloat16),
            pltpu.VMEM((n_rows, ff), jnp.float32),
            pltpu.SemaphoreType.DMA((n_grp + 8,)),
            pltpu.SemaphoreType.DMA((n_grp,)),
            pltpu.SemaphoreType.DMA((7,)),
            pltpu.SemaphoreType.DMA((1,)),
        ],
        compiler_params=pltpu.CompilerParams(
            collective_id=collective_id, has_side_effects=True, vmem_limit_bytes=64 * 1024 * 1024 - 1024 * 1024
        ),
        cost_estimate=pl.CostEstimate(flops=flops, transcendentals=n_rows * ff, bytes_accessed=nbytes),
    )(rows, gate_full, up_full, down_full)


def weight_kernel(n_x, n_grp, g_in, u_in, d_in, t_in, g_out, u_out, d_out, t_out, send_sem, recv_sem,
                  local_sem, t_send, t_recv, stage, stage_sem):
    ins = (g_in, u_in, d_in)
    outs = (g_out, u_out, d_out)
    x = lax.axis_index("x")
    h = lax.axis_index("zhi")
    c = lax.axis_index("core")

    def block(xx, hh, cc):
        return (xx * 2 + hh) * 2 + cc

    me = block(x, h, c)
    up_x = lax.rem(x + 1, n_x)
    down_x = lax.rem(x + n_x - 1, n_x)
    far_x = lax.rem(x + 2, n_x)
    toward = jnp.where(c == 0, up_x, down_x)
    away = jnp.where(c == 0, down_x, up_x)
    partner = {"core": 1 - c}
    z_peer = {"zhi": 1 - h}
    x_devs = [{"x": up_x}, {"x": down_x}]

    t_me, t_peers = exchange_peers(n_grp)
    barrier = pltpu.get_barrier_semaphore()
    greet = [partner, z_peer] + x_devs + plane_devices(n_grp)
    for dev in greet:
        pl.semaphore_signal(barrier, inc=1, device_id=dev, device_id_type=MESH_ID)
    pl.semaphore_wait(barrier, len(greet))

    count = [0]

    def send(src_of, blk, dev):
        k = count[0]
        count[0] += 1
        copies = []
        for m in range(3):
            cp = pltpu.make_async_remote_copy(
                src_ref=src_of(m),
                dst_ref=outs[m].at[blk],
                send_sem=send_sem.at[m, k],
                recv_sem=recv_sem.at[m, blk],
                device_id=dev,
                device_id_type=MESH_ID,
            )
            cp.start()
            copies.append(cp)
        return copies

    def wait_in(blk):
        for m in range(3):
            pltpu.make_async_remote_copy(
                src_ref=ins[m].at[0],
                dst_ref=outs[m].at[blk],
                send_sem=send_sem.at[m, 0],
                recv_sem=recv_sem.at[m, blk],
                device_id=partner,
                device_id_type=MESH_ID,
            ).wait_recv()

    sent = []
    local = []
    for m in range(3):
        cp = pltpu.make_async_copy(ins[m].at[h], outs[m].at[me], local_sem.at[m])
        cp.start()
        local.append(cp)
    sent += send(lambda m: ins[m].at[1 - h], me, z_peer)
    for dev in [partner] + x_devs:
        sent += send(lambda m: ins[m].at[h], me, dev)

    z_blk = block(x, 1 - h, c)
    wait_in(z_blk)
    for dev in [partner] + x_devs:
        sent += send(lambda m: outs[m].at[z_blk], z_blk, dev)
    t_local, t_copies, t_k = start_plane(
        n_grp, t_in, t_out, stage, t_send, t_recv, stage_sem, local_sem.at[3]
    )
    t_copies += relay_plane(n_grp, t_k, t_in, t_out, stage, t_send, t_recv, stage_sem)

    for hh in (h, 1 - h):
        blk = block(away, hh, c)
        wait_in(blk)
        sent += send(lambda m: outs[m].at[blk], blk, partner)
        sent += send(lambda m: outs[m].at[blk], blk, {"x": toward})
    for xp in (toward, far_x):
        for hh in (h, 1 - h):
            blk = block(xp, hh, c)
            wait_in(blk)
            sent += send(lambda m: outs[m].at[blk], blk, partner)

    for xx in range(n_x):
        for hh in (0, 1):
            wait_in(block(xx, hh, 1 - c))

    for cp in sent:
        cp.wait_send()
    for cp in local:
        cp.wait()
    finish_exchange(t_peers, t_local, t_copies, t_in, t_out, t_send, t_recv)


def gather_weights(gate_weight, up_weight, down_weight, outgoing, n_x, n_grp):
    blk_rows, width = gate_weight.shape[1], gate_weight.shape[2]
    n_blocks = n_x * 4
    n_send = 16
    shape = jax.ShapeDtypeStruct((n_blocks, blk_rows, width), gate_weight.dtype)
    any_spec = pl.BlockSpec(memory_space=pl.ANY)
    nbytes = 3 * n_blocks * blk_rows * width * 2
    return pl.pallas_call(
        functools.partial(weight_kernel, n_x, n_grp),
        out_shape=(shape, shape, shape, jax.ShapeDtypeStruct(outgoing.shape, outgoing.dtype)),
        in_specs=[any_spec] * 4,
        out_specs=(any_spec, any_spec, any_spec, any_spec),
        scratch_shapes=[
            pltpu.SemaphoreType.DMA((3, n_send)),
            pltpu.SemaphoreType.DMA((3, n_blocks)),
            pltpu.SemaphoreType.DMA((4,)),
            pltpu.SemaphoreType.DMA((n_grp + 8,)),
            pltpu.SemaphoreType.DMA((n_grp,)),
            pltpu.VMEM((7,) + outgoing.shape[1:], outgoing.dtype),
            pltpu.SemaphoreType.DMA((7,)),
        ],
        compiler_params=pltpu.CompilerParams(collective_id=0, has_side_effects=True),
        cost_estimate=pl.CostEstimate(flops=0, transcendentals=0, bytes_accessed=nbytes),
    )(gate_weight, up_weight, down_weight, outgoing)


def per_device(tokens, expert_ids, combine, gate_weight, up_weight, down_weight):
    n_x = lax.axis_size("x")
    assert n_x == 4
    per_group = gate_weight.shape[0]
    groups = lax.axis_size("expert")
    n_expert = per_group * groups
    n_grp = groups * 2
    assert n_grp == 16
    tok_rows, top_k = expert_ids.shape
    model_width = tokens.shape[1]
    n_slot = n_expert * CAP

    flat_ids = expert_ids.reshape(-1)
    onehot = (flat_ids[:, None] == jnp.arange(n_expert, dtype=jnp.int32)[None, :]).astype(jnp.int32)
    n_pair = flat_ids.shape[0]
    before = (
        lax.broadcasted_iota(jnp.int32, (n_pair, n_pair), 0)
        > lax.broadcasted_iota(jnp.int32, (n_pair, n_pair), 1)
    ).astype(jnp.bfloat16)
    earlier = jnp.dot(before, onehot.astype(jnp.bfloat16), preferred_element_type=jnp.float32)
    earlier = earlier.astype(jnp.int32)
    rank_within = jnp.sum(earlier * onehot, axis=1)
    slot_index = (flat_ids * CAP + rank_within).reshape(tok_rows, top_k)
    slot_col = lax.broadcasted_iota(jnp.int32, (n_slot, tok_rows), 0)
    pick = sum(
        (slot_index[:, k][None, :] == slot_col).astype(jnp.bfloat16) for k in range(top_k)
    )
    outgoing = jnp.dot(pick, tokens, preferred_element_type=jnp.float32).astype(jnp.bfloat16)
    outgoing = outgoing.reshape(n_expert, CAP, model_width)

    g_all, u_all, d_all, arrived = gather_weights(
        gate_weight, up_weight, down_weight, outgoing, n_x, n_grp
    )
    gate_full = g_all.reshape(-1, model_width)
    up_full = u_all.reshape(-1, model_width)
    down_full = d_all.reshape(-1, model_width)
    returned = expert_return(
        arrived.reshape(n_slot, model_width), gate_full, up_full, down_full, n_grp, 1
    )
    returned = returned.reshape(n_slot, model_width)

    slot_row = lax.broadcasted_iota(jnp.int32, (tok_rows, n_slot), 1)
    weight_of = sum(
        jnp.where(slot_index[:, k][:, None] == slot_row, combine[:, k][:, None], 0.0)
        for k in range(top_k)
    )
    weight_top = lax.reduce_precision(weight_of, exponent_bits=8, mantissa_bits=7)
    weight_hi = weight_top.astype(jnp.bfloat16)
    weight_lo = (weight_of - weight_top).astype(jnp.bfloat16)
    both = jnp.dot(
        jnp.concatenate([weight_hi, weight_lo], axis=0), returned, preferred_element_type=jnp.float32
    )
    mixed = both[:tok_rows] + both[tok_rows:]
    return mixed.astype(jnp.bfloat16)


def solution(mesh):
    groups = mesh.shape["expert"]
    n_x = mesh.shape["fsdp"] // 4
    inner = Mesh(mesh.devices.reshape(groups, n_x, 2, 2), ("expert", "x", "zhi", "core"))
    rows = P(("expert", "x", "zhi", "core"), None)
    weights = P("expert", ("x", "zhi", "core"), None)
    return jax.shard_map(
        per_device,
        mesh=inner,
        in_specs=(rows, rows, rows, weights, weights, weights),
        out_specs=rows,
        check_vma=False,
    )
```
